128 devices in a mesh: tile: 16 (over x_hi, y, core), layer: 8 (over x_lo, z).
Axes of the slice: x: 4 (x_hi: 2, x_lo: 2; x = x_hi * 2 + x_lo), y: 4, z: 4, core: 2. Of those that a mesh axis runs over, the one named last changes fastest.
Arguments:
- classes: int32 [256, 64, 512], P('tile', 'layer'), may hold values from 0 to 15
- well_mask: int32 [256, 64, 512], P('tile', 'layer'), may hold values 0 or 1
- source: float32 [256, 64, 512], P('tile', 'layer'), may hold values from -96 to 96
Outputs:
- pressure: float32 [256, 64, 512], P('tile', 'layer')
The draws below stay inside these ranges and needn't reach their ends.
Inputs may be any that keep to these rules, and one draw needn't show every extreme that they name: `classes`: an index into the table of 16 permeabilities. `well_mask`: 1 marks a well cell.
All inputs are finite; a program needn't handle non-finite values. No bound on the sum of `well_mask` on one device may be relied on, other than what follows from the above.
Results may differ from the reference program's by a relative error of at most 0.0003.
Values sent between devices are 32-bit elements; how exact they have to be, the bound alone decides.
No kernel may reach another device: no remote copies, remote signals or barrier semaphores. Data moves between devices by JAX's collectives and lax.ppermute only.
A program may use at most 64 MiB of HBM per device.

```python
import jax
import jax.numpy as jnp
import numpy as np
from jax import lax

NY = 512
EDGE = 16
CLASSES = 16
SWEEPS = 4
NX = 256
NZ = 64
NCX = 16
NCZ = 4
NCY = 32


def place_ends(values, stream_key, low, largest):
    spot = [jax.random.randint(jax.random.fold_in(stream_key, axis), (), 0, length) for axis, length in enumerate(values.shape)]
    main_axis = values.shape.index(max(values.shape))
    beside = spot[:main_axis] + [(spot[main_axis] + 1) % values.shape[main_axis]] + spot[main_axis + 1:]
    return values.at[tuple(spot)].set(low).at[tuple(beside)].set(largest)


def shard_levels(key, extent, split, smallest, top_value):
    level, own = 1.0, jax.random.fold_in(key, 6)
    for axis_at, parts in split:
        steps = jnp.exp(jax.random.uniform(jax.random.fold_in(own, axis_at), (parts,), jnp.float32, smallest / len(split), top_value / len(split)))
        level = level * jnp.repeat(steps, extent[axis_at] // parts).reshape([-1 if axis == axis_at else 1 for axis in range(len(extent))])
    return level


def bell_draw(stream_key, extent, deviation, most, pieces=(), kind=jnp.bfloat16):
    loudness = shard_levels(stream_key, extent, pieces, -0.22, 0.18) if pieces else 1.0
    values = jax.random.normal(stream_key, extent, jnp.float32) * deviation * loudness
    return jnp.minimum(jnp.maximum(values, -most), most).astype(kind)


def setup_inputs(seed: int = 0) -> dict:
    seeds = jax.random.split(jax.random.key(seed), 4)
    return {
        "classes": place_ends(jax.random.randint(seeds[0], (NX, NZ, NY), 0, CLASSES), jax.random.fold_in(seeds[0], 1), 0, CLASSES - 1).astype(jnp.int32),
        "well_mask": place_ends((jax.random.randint(seeds[1], (NX, NZ, NY), 0, 8) < 1).astype(jnp.int32), jax.random.fold_in(seeds[1], 1), 0, 1),
        "source": bell_draw(seeds[2], (NX, NZ, NY), 16.0, 96.0, ((0, 16), (1, 8)), jnp.float32),
    }


FINE_DAMPING = 0.67
COARSE_DAMPING = 0.5
SINK_RATE = 0.5
VERTICAL_RATIO = 0.25


def oriented(vector, dimension):
    shape_list = [1, 1, 1]
    shape_list[dimension] = vector.shape[0]
    return vector.reshape(shape_list)


def permeability_of(classes):
    table_values = np.exp(np.linspace(-2.5, 2.5, CLASSES))
    result = jnp.zeros(classes.shape, jnp.float32)
    for entry_index in range(CLASSES):
        result = result + jnp.where(classes == entry_index, jnp.float32(table_values[entry_index]), jnp.float32(0.0))
    return result


def harmonic(left_value, right_value):
    summed = left_value + right_value
    safe_sum = jnp.where(summed > 0, summed, 1.0)
    return 2.0 * left_value * right_value / safe_sum


def neighbour(values, dimension, offset):
    starts = [1, 1, 1]
    limits = [values.shape[0] - 1, values.shape[1] - 1, values.shape[2] - 1]
    starts[dimension] += offset
    limits[dimension] += offset
    return lax.slice(values, starts, limits)


def inner_part(values):
    return values[1:-1, 1:-1, 1:-1]


def face_trans(permeability):
    center = inner_part(permeability)
    face_pairs = []
    for dimension in range(3):
        factor = VERTICAL_RATIO if dimension == 1 else 1.0
        lower_trans = factor * harmonic(center, neighbour(permeability, dimension, -1))
        upper_trans = factor * harmonic(center, neighbour(permeability, dimension, 1))
        face_pairs.append((lower_trans, upper_trans))
    return face_pairs


def face_masks(coords, dimension):
    local_index = coords[dimension] % EDGE
    lower_mask = oriented((local_index == 0).astype(jnp.float32), dimension)
    upper_mask = oriented((local_index == EDGE - 1).astype(jnp.float32), dimension)
    return lower_mask, upper_mask


def smoothed_basis(permeability, sink_padded, coords):
    face_pairs = face_trans(permeability)
    inside = inner_part(permeability) > 0
    sink_term = inner_part(sink_padded)
    diagonal = sink_term
    for face_pair in face_pairs:
        diagonal = diagonal + face_pair[0] + face_pair[1]
    diagonal = jnp.where(inside, diagonal, 1.0)
    leaving = sink_term
    outer_basis = []
    for dimension in range(3):
        lower_mask, upper_mask = face_masks(coords, dimension)
        across = lower_mask * face_pairs[dimension][0] + upper_mask * face_pairs[dimension][1]
        leaving = leaving + across
        outer_basis.append(jnp.where(inside, FINE_DAMPING * across / diagonal, 0.0))
    own_basis = jnp.where(inside, 1.0 - FINE_DAMPING * leaving / diagonal, 0.0)
    return own_basis, outer_basis, face_pairs, sink_term


def colour_probe(own_basis, outer_basis, coords, colour):
    parity = [oriented((coords[dimension] // EDGE) % 2, dimension) for dimension in range(3)]
    matches = [(parity[dimension] == colour[dimension]).astype(jnp.float32) for dimension in range(3)]
    values = own_basis * matches[0] * matches[1] * matches[2]
    for dimension in range(3):
        weight_mask = 1.0 - matches[dimension]
        for other_dim in range(3):
            if other_dim != dimension:
                weight_mask = weight_mask * matches[other_dim]
        values = values + outer_basis[dimension] * weight_mask
    return values


def apply_operator(values, face_pairs, sink_term):
    center = inner_part(values)
    applied = sink_term * center
    for dimension in range(3):
        applied = applied + face_pairs[dimension][0] * (center - neighbour(values, dimension, -1))
        applied = applied + face_pairs[dimension][1] * (center - neighbour(values, dimension, 1))
    return applied


def half_sum(values):
    size_x, size_z, size_y = values.shape
    half_edge = EDGE // 2
    return values.reshape(size_x // half_edge, half_edge, size_z // half_edge, half_edge, size_y // half_edge, half_edge).sum(axis=(1, 3, 5))


def routing(halves, row_index, colour_bit, outer_term):
    parent = halves // 2
    sign_value = 2 * (halves % 2) - 1
    if outer_term:
        target = parent + sign_value
        toward = -sign_value
    else:
        target = parent
        toward = sign_value
    offset = jnp.where(target % 2 == colour_bit, 0, toward)
    hit_row = row_index[:, None] == target[None, :]
    return jnp.stack([(hit_row & (offset[None, :] == shift_value)).astype(jnp.float32) for shift_value in (-1, 0, 1)])


def assemble(own_wide, outer_wide, coords_wide, face_pairs, sink_term, own_basis, outer_basis, source, halves, row_index):
    row_shape = (row_index[0].shape[0], row_index[1].shape[0], row_index[2].shape[0])
    stiffness = jnp.zeros((3, 3, 3) + row_shape, jnp.float32)
    rhs_sum = jnp.zeros(row_shape, jnp.float32)
    weights = [own_basis] + list(outer_basis)
    for term_index in range(4):
        outer_flags = [term_index == dimension + 1 for dimension in range(3)]
        row_maps = [routing(halves[dimension], row_index[dimension], 0, outer_flags[dimension]).sum(axis=0) for dimension in range(3)]
        half_sums = half_sum(weights[term_index] * source)
        rhs_sum = rhs_sum + jnp.einsum("ih,jg,kf,hgf->ijk", row_maps[0], row_maps[1], row_maps[2], half_sums, precision=lax.Precision.HIGHEST)
    for bit_x in (0, 1):
        for bit_z in (0, 1):
            for bit_y in (0, 1):
                colour = (bit_x, bit_z, bit_y)
                applied = apply_operator(colour_probe(own_wide, outer_wide, coords_wide, colour), face_pairs, sink_term)
                for term_index in range(4):
                    outer_flags = [term_index == dimension + 1 for dimension in range(3)]
                    route_mats = [routing(halves[dimension], row_index[dimension], colour[dimension], outer_flags[dimension]) for dimension in range(3)]
                    half_sums = half_sum(weights[term_index] * applied)
                    stiffness = stiffness + jnp.einsum("aih,bjg,ckf,hgf->abcijk", route_mats[0], route_mats[1], route_mats[2], half_sums, precision=lax.Precision.HIGHEST)
    return jnp.concatenate([stiffness.reshape((27,) + row_shape), rhs_sum[None]], axis=0)


def coarse_apply(stiffness, padded):
    size_x = padded.shape[0] - 2
    size_z = padded.shape[1] - 2
    size_y = padded.shape[2] - 2
    result = jnp.zeros((size_x, size_z, size_y), jnp.float32)
    for offset_index in range(27):
        step_x = offset_index // 9
        step_z = (offset_index // 3) % 3
        step_y = offset_index % 3
        result = result + stiffness[offset_index] * padded[step_x:step_x + size_x, step_z:step_z + size_z, step_y:step_y + size_y]
    return result


def jacobi_step(coarse_rows, padded, pressure):
    residual = coarse_rows[27] - coarse_apply(coarse_rows[:27], padded)
    return pressure + COARSE_DAMPING * residual / coarse_rows[13]


def expand_coarse(coarse_block, shifts, fine_shape, fine_offsets):
    values = coarse_block
    for dimension in range(3):
        first_row = EDGE * (1 + shifts[dimension]) + fine_offsets[dimension]
        values = lax.dynamic_slice_in_dim(jnp.repeat(values, EDGE, axis=dimension), first_row, fine_shape[dimension], dimension)
    return values


def prolong(coarse_block, own_basis, outer_basis, coords, fine_shape, fine_offsets):
    result = own_basis * expand_coarse(coarse_block, (0, 0, 0), fine_shape, fine_offsets)
    for dimension in range(3):
        lower_mask, upper_mask = face_masks(coords, dimension)
        minus_shift = [0, 0, 0]
        minus_shift[dimension] = -1
        plus_shift = [0, 0, 0]
        plus_shift[dimension] = 1
        beside = lower_mask * expand_coarse(coarse_block, minus_shift, fine_shape, fine_offsets)
        beside = beside + upper_mask * expand_coarse(coarse_block, plus_shift, fine_shape, fine_offsets)
        result = result + outer_basis[dimension] * beside
    return result


def reference(classes, well_mask, source):
    permeability = permeability_of(classes)
    sink_field = SINK_RATE * well_mask.astype(jnp.float32) * permeability
    perm_padded = jnp.pad(permeability, 2)
    sink_padded = jnp.pad(sink_field, 2)
    coords_wide = [jnp.arange(-1, NX + 1, dtype=jnp.int32), jnp.arange(-1, NZ + 1, dtype=jnp.int32), jnp.arange(-1, NY + 1, dtype=jnp.int32)]
    coords_inner = [jnp.arange(NX, dtype=jnp.int32), jnp.arange(NZ, dtype=jnp.int32), jnp.arange(NY, dtype=jnp.int32)]
    own_wide, outer_wide, pairs_wide, sink_wide = smoothed_basis(perm_padded, sink_padded, coords_wide)
    face_pairs = [(inner_part(face_pair[0]), inner_part(face_pair[1])) for face_pair in pairs_wide]
    sink_term = inner_part(sink_wide)
    own_basis = inner_part(own_wide)
    outer_basis = [inner_part(values) for values in outer_wide]
    half_edge = EDGE // 2
    halves = [jnp.arange(NX // half_edge, dtype=jnp.int32), jnp.arange(NZ // half_edge, dtype=jnp.int32), jnp.arange(NY // half_edge, dtype=jnp.int32)]
    row_index = [jnp.arange(NCX, dtype=jnp.int32), jnp.arange(NCZ, dtype=jnp.int32), jnp.arange(NCY, dtype=jnp.int32)]
    coarse_rows = assemble(own_wide, outer_wide, coords_wide, face_pairs, sink_term, own_basis, outer_basis, source, halves, row_index)
    pressure = jnp.zeros((NCX, NCZ, NCY), jnp.float32)
    for sweep_index in range(SWEEPS):
        pressure = jacobi_step(coarse_rows, jnp.pad(pressure, 1), pressure)
    return prolong(jnp.pad(pressure, 1), own_basis, outer_basis, coords_inner, (NX, NZ, NY), (0, 0, 0))
```

```python
import functools

import jax
import jax.numpy as jnp
import numpy as np
from jax import lax
from jax.experimental import pallas as pl
from jax.experimental.pallas import tpu as pltpu
from jax.sharding import PartitionSpec as P

EDGE = 16
SWEEPS = 4
FINE_DAMPING = 0.67
COARSE_DAMPING = 0.5
NXL, NZL, NY = 16, 8, 512
TILES, LAYERS = 16, 8
NCY = NY // EDGE
NCZ = LAYERS * NZL // EDGE
ROWS = 40
F32 = jnp.float32
VMEM = pl.BlockSpec(memory_space=pltpu.VMEM)

NODES = ("N", "Z", "M", "Q", "MZ", "QZ")


def order(key):
    return NODES.index(key[0]) * 2 + (key[1] == "v")


def pair(a, b):
    return (a, b) if order(a) <= order(b) else (b, a)


ROW = {}
for x in (-1, 0, 1):
    for dy in (0, 1):
        ROW["s", x, x, dy] = len(ROW)
for lo, hi in ((-1, 0), (0, 1)):
    for dy in (-1, 0, 1):
        ROW["s", lo, hi, dy] = len(ROW)
for lo, hi in ((0, 0), (-1, -1), (1, 1), (-1, 0), (0, -1), (1, 0), (0, 1)):
    for dy in (-1, 0, 1):
        ROW["z", lo, hi, dy] = len(ROW)
for x in (-1, 0, 1):
    ROW["r", x] = len(ROW)
HERE = {-1: "M", 0: "N", 1: "Q"}
BESIDE = {-1: "MZ", 0: "Z", 1: "QZ"}


def swap_pairs(count, first):
    if first:
        return [(i, i ^ 1) for i in range(count)]
    return [(i, (((i + 1) ^ 1) - 1) % count) for i in range(count)]


def pack_z(cls, well, out_a, out_b):
    odd = lax.axis_index("layer") % 2 == 1
    first = cls[:, 0, :].astype(F32)
    last = cls[:, NZL - 1, :].astype(F32)
    out_a[0] = jnp.where(odd, first, last)
    out_b[0] = jnp.where(odd, last, first)
    second = cls[:, 1, :].astype(F32)
    wells = well[:, 0, :].astype(F32)
    for out in (out_a, out_b):
        out[1] = second
        out[2] = wells


def pack_x(cls, well, z_a, z_b, out_a, out_b):
    odd_z = lax.axis_index("layer") % 2 == 1
    odd = lax.axis_index("tile") % 2 == 1
    up = jnp.where(odd_z, z_b[0], z_a[0])
    down = jnp.where(odd_z, z_a[0], z_b[0])
    first, last = cls[0].astype(F32), cls[NXL - 1].astype(F32)
    out_a[0] = jnp.where(odd, first, last)
    out_b[0] = jnp.where(odd, last, first)
    above_first, above_last = up[0:1], up[NXL - 1 : NXL]
    for out in (out_a, out_b):
        out[1] = cls[1].astype(F32)
        out[2] = well[0].astype(F32)
        out[3] = jnp.broadcast_to(down[0:1], (8, NY))
    out_a[3, 1:2] = jnp.where(odd, above_first, above_last)
    out_b[3, 1:2] = jnp.where(odd, above_last, above_first)


def lane_roll(value, by):
    return pltpu.roll(value, by % value.shape[-1], value.ndim - 1)


def row_roll(value, by):
    return pltpu.roll(value, by % value.shape[0], 0)


def assemble(cls, well, src, z_a, z_b, x_a, x_b, part, own, beside_y, beside_z, beside_x, lanes_ref, g_ref, out_ref):
    tile, layer = lax.axis_index("tile"), lax.axis_index("layer")
    odd_z, odd_x = layer % 2 == 1, tile % 2 == 1
    has_up, has_down = (layer < LAYERS - 1).astype(F32), (layer > 0).astype(F32)
    has_right, has_left = (tile < TILES - 1).astype(F32), (tile > 0).astype(F32)

    def resist(c):
        return jnp.exp(2.5 - c * F32(1.0 / 3.0))

    def sink(c, w):
        return 0.5 * w * jnp.exp(c * F32(1.0 / 3.0) - 2.5)

    plane = (NZL, NY)
    zrow = lax.broadcasted_iota(jnp.int32, plane, 0)
    lane = lax.broadcasted_iota(jnp.int32, plane, 1)
    m_l = lane % EDGE == 0
    m_r = lane % EDGE == EDGE - 1
    no_last = (lane < NY - 1).astype(F32)

    def y_faces(r):
        ty = 2.0 / (r + lane_roll(r, -1))
        ty = jnp.where(lax.broadcasted_iota(jnp.int32, r.shape, 1) < NY - 1, ty, 0.0)
        return ty, lane_roll(ty, 1)

    up = [jnp.where(odd_z, z_b[i], z_a[i]) for i in range(3)]
    down = jnp.where(odd_z, z_a[0], z_b[0])
    right = [jnp.where(odd_x, x_b[i], x_a[i]) for i in range(4)]
    left = [jnp.where(odd_x, x_a[i], x_b[i]) for i in (0, 3)]

    tall = (NXL, NY)
    xrow = lax.broadcasted_iota(jnp.int32, tall, 0)
    lane16 = lax.broadcasted_iota(jnp.int32, tall, 1)
    r8, r9 = resist(up[0]), resist(up[1])
    s8 = sink(up[0], up[2])
    r7 = resist(cls[:, NZL - 1, :].astype(F32))
    line_left, line_right = resist(left[1][1:2]), resist(right[3][1:2])
    r8_left = jnp.where(xrow == 0, jnp.broadcast_to(line_left, tall), row_roll(r8, 1))
    r8_right = jnp.where(xrow == NXL - 1, jnp.broadcast_to(line_right, tall), row_roll(r8, -1))
    tx8_lo = 2.0 / (r8 + r8_left) * jnp.where(xrow == 0, has_left, 1.0)
    tx8_hi = 2.0 / (r8 + r8_right) * jnp.where(xrow == NXL - 1, has_right, 1.0)
    t78 = 0.5 / (r7 + r8) * has_up
    t89 = 0.5 / (r8 + r9)
    ty8, ty8_lo = y_faces(r8)
    diag8 = s8 + tx8_lo + tx8_hi + t78 + t89 + ty8 + ty8_lo
    d8 = FINE_DAMPING / diag8
    ey8 = d8 * jnp.where(lane16 % EDGE == 0, ty8_lo, jnp.where(lane16 % EDGE == EDGE - 1, ty8, 0.0))
    ex8 = d8 * jnp.where(xrow == 0, tx8_lo, jnp.where(xrow == NXL - 1, tx8_hi, 0.0))
    ez8 = jnp.where(odd_z, d8 * t78, 0.0)
    o8 = 1.0 - d8 * s8 - ey8 - ex8 - ez8
    zero16 = jnp.zeros(tall, F32)
    above = {
        ("N", "u"): jnp.where(odd_z, ez8, o8),
        ("N", "v"): jnp.where(odd_z, zero16, ey8),
        ("Z", "u"): jnp.where(odd_z, o8, zero16),
        ("Z", "v"): jnp.where(odd_z, ey8, zero16),
        ("X", "u"): jnp.where(odd_z, zero16, ex8),
        ("XZ", "u"): jnp.where(odd_z, ex8, zero16),
    }

    cs = [cls[x].astype(F32) for x in range(NXL)] + [right[0]]
    rs = [resist(c) for c in cs]
    ss = [sink(cs[x], well[x].astype(F32)) for x in range(NXL)] + [sink(right[0], right[2])]
    txs = [2.0 / (resist(left[0]) + rs[0]) * has_left]
    txs += [2.0 / (rs[x] + rs[x + 1]) for x in range(NXL - 1)]
    txs += [2.0 / (rs[NXL - 1] + rs[NXL]) * has_right, 2.0 / (rs[NXL] + resist(right[1]))]
    zb = jnp.where(odd_z, NZL - 1, 0)
    at_zb = zrow == zb
    basis, tzs, tys = [], [], []
    for x in range(NXL + 1):
        r = rs[x]
        if x < NXL:
            below, over = resist(down[x : x + 1]), r8[x : x + 1]
        else:
            below, over = resist(right[3][0:1]), line_right
        r_up = jnp.where(zrow == NZL - 1, jnp.broadcast_to(over, plane), row_roll(r, -1))
        r_dn = jnp.where(zrow == 0, jnp.broadcast_to(below, plane), row_roll(r, 1))
        tz_hi = 0.5 / (r + r_up) * jnp.where(zrow == NZL - 1, has_up, 1.0)
        tz_lo = 0.5 / (r + r_dn) * jnp.where(zrow == 0, has_down, 1.0)
        ty, ty_lo = y_faces(r)
        diag = ss[x] + txs[x] + txs[x + 1] + tz_hi + tz_lo + ty + ty_lo
        d = FINE_DAMPING / diag
        ey = d * jnp.where(m_l, ty_lo, jnp.where(m_r, ty, 0.0))
        ez = jnp.where(at_zb, d * jnp.where(odd_z, tz_hi, tz_lo), 0.0)
        o = 1.0 - d * ss[x] - ey - ez
        here = {("Z", "u"): ez, ("N", "v"): ey}
        if x == 0:
            here["M", "u"] = d * txs[0]
            o = o - here["M", "u"]
            beside_x[0] = here["M", "u"]
        if x == NXL - 1:
            here["Q", "u"] = d * txs[NXL]
            o = o - here["Q", "u"]
            beside_x[1] = here["Q", "u"]
        if x == NXL:
            here["Q", "u"] = d * txs[NXL]
            o = o - here["Q", "u"]
        else:
            own[x] = o
            beside_y[x] = ey
            beside_z[x] = ez
        here["N", "u"] = o
        basis.append(here)
        tzs.append(tz_hi)
        tys.append(ty)

    sums = {}

    def add(key, value):
        sums[key] = sums[key] + value if key in sums else value

    def add_pairs(weight, values):
        keys = sorted(values, key=order)
        for i, a in enumerate(keys):
            scaled = weight * values[a]
            for b in keys[i:]:
                add((a, b), scaled * values[b])

    def minus(a, b):
        out = {}
        for key in {**a, **b}:
            if key in a and key in b:
                out[key] = a[key] - b[key]
            else:
                out[key] = a[key] if key in a else -b[key]
        return out

    for x in range(NXL):
        here = basis[x]
        add_pairs(ss[x], here)
        source = src[x]
        for key, value in here.items():
            add(("rhs", key), value * source)
        if x < NXL - 1:
            there = basis[x + 1]
        else:
            b = basis[NXL]
            there = {("N", "u"): b["Q", "u"], ("Q", "u"): b["N", "u"], ("Q", "v"): b["N", "v"], ("QZ", "u"): b["Z", "u"]}
        add_pairs(txs[x + 1], minus(here, there))
        there = {}
        for key, value in here.items():
            name = key if key[0] in "NZ" else ("X", "u")
            row = jnp.broadcast_to(above[name][x : x + 1], plane)
            there[key] = jnp.where(zrow == NZL - 1, row, row_roll(value, -1))
        there["Z", "v"] = jnp.where(zrow == NZL - 1, jnp.broadcast_to(above["Z", "v"][x : x + 1], plane), 0.0)
        for node in "MQ":
            if (node, "u") in here:
                row = jnp.broadcast_to(above["XZ", "u"][x : x + 1], plane)
                there[node + "Z", "u"] = jnp.where(zrow == NZL - 1, row, 0.0)
        add_pairs(tzs[x], minus(here, there))
        rolled = {key: lane_roll(value, -1) for key, value in here.items()}
        there = {
            ("N", "u"): jnp.where(m_r, rolled["N", "v"], rolled["N", "u"]),
            ("N", "v"): jnp.where(m_r, rolled["N", "u"], rolled["N", "v"]),
        }
        for node in "ZMQ":
            if (node, "u") in here:
                there[node, "u"] = jnp.where(m_r, 0.0, rolled[node, "u"])
                there[node, "v"] = jnp.where(m_r, rolled[node, "u"], 0.0)
        add_pairs(tys[x], minus(here, there))

    index = {key: i for i, key in enumerate(sums)}
    for key, i in index.items():
        lanes_ref[i : i + 1, :] = jnp.sum(sums[key], axis=0, keepdims=True)
    count = -(-len(index) // 8) * 8
    if count > len(index):
        lanes_ref[len(index) : count, :] = jnp.zeros((count - len(index), NY), F32)

    j = lax.broadcasted_iota(jnp.int32, (NY, 128), 0)
    n = lax.broadcasted_iota(jnp.int32, (NY, 128), 1)
    group, pos = n // NCY, j % EDGE
    taken = (group == 0) | ((group == 1) & (pos == 0)) | ((group == 2) & (pos >= EDGE - 2))
    select = ((j // EDGE == n % NCY) & taken).astype(F32)
    grouped = jnp.dot(lanes_ref[0:count, :], select, precision=lax.Precision.HIGHEST, preferred_element_type=F32)
    gl = lax.broadcasted_iota(jnp.int32, (count, 128), 1)
    g_l_next = jnp.where(gl < NCY - 1, lane_roll(grouped, -(NCY + 1)), 0.0)
    g_r_next = jnp.where((gl > 0) & (gl < NCY), lane_roll(grouped, -(2 * NCY - 1)), 0.0)
    forms = {
        "all": jnp.where(gl < NCY, grouped, 0.0),
        "L": jnp.where(gl < NCY, lane_roll(grouped, -NCY), 0.0),
        "R": jnp.where(gl < NCY, lane_roll(grouped, -2 * NCY), 0.0),
        "Ls": g_l_next,
        "Rs": g_r_next,
        "vv": g_l_next + g_r_next,
    }
    at = {}
    for i, (name, value) in enumerate(forms.items()):
        at[name] = i
        g_ref[i, 0:count, :] = value

    def taken_rows(terms):
        total = None
        for name, key in terms:
            if key in index:
                q = index[key]
                row = g_ref[at[name], q : q + 1, :]
                total = row if total is None else total + row
        return total

    def terms_of(a, b, dy):
        au, av, bu, bv = (a, "u"), (a, "v"), (b, "u"), (b, "v")
        if a == b:
            if dy == 0:
                return [("all", pair(au, au)), ("vv", pair(av, av))]
            return [("Ls", pair(au, av)), ("R", pair(au, av))]
        if dy == 0:
            return [("all", pair(au, bu)), ("vv", pair(av, bv))]
        if dy < 0:
            return [("L", pair(au, bv)), ("Rs", pair(av, bu))]
        return [("R", pair(au, bv)), ("Ls", pair(av, bu))]

    nothing = jnp.zeros((1, 128), F32)
    out_ref[...] = jnp.zeros(out_ref.shape, F32)
    for key, r in ROW.items():
        rows = {}
        if key[0] == "s":
            rows[0] = taken_rows(terms_of(HERE[key[1]], HERE[key[2]], key[3]))
            rows[1] = taken_rows(terms_of(BESIDE[key[1]], BESIDE[key[2]], key[3]))
        elif key[0] == "z":
            when_odd = taken_rows(terms_of(HERE[key[1]], BESIDE[key[2]], key[3]))
            when_even = taken_rows(terms_of(BESIDE[key[1]], HERE[key[2]], key[3]))
            when_odd = nothing if when_odd is None else when_odd
            when_even = nothing if when_even is None else when_even
            rows[2] = jnp.where(odd_z, when_odd, when_even)
        else:
            node, near = HERE[key[1]], BESIDE[key[1]]
            rows[0] = taken_rows([("all", ("rhs", (node, "u"))), ("vv", ("rhs", (node, "v")))])
            rows[1] = taken_rows([("all", ("rhs", (near, "u"))), ("vv", ("rhs", (near, "v")))])
        for where, row in rows.items():
            if row is not None:
                out_ref[where, r : r + 1, :] = row
    cell = layer // 2
    near_cell = jnp.where(odd_z, cell + 1, cell - 1)
    zl = lax.broadcasted_iota(jnp.int32, (ROWS, 128), 1) // NCY
    total = jnp.zeros((ROWS, 128), F32)
    for where, z in ((0, cell), (1, near_cell), (2, jnp.minimum(cell, near_cell))):
        rows = out_ref[where]
        spread = rows
        for k in range(1, NCZ):
            spread = spread + lane_roll(rows, k * NCY)
        total = total + jnp.where(zl == z, spread, 0.0)
    for k in range(LAYERS):
        part[k] = total


def add_layers(received, out):
    total = received[0]
    for k in range(1, LAYERS):
        total = total + received[k]
    for k in range(TILES):
        out[k] = total


def solve(rows, own, beside_y, beside_z, beside_x, pressure):
    tile, layer = lax.axis_index("tile"), lax.axis_index("layer")
    odd_z = layer % 2 == 1
    cell = layer // 2
    near_cell = jnp.where(odd_z, cell + 1, cell - 1)
    shape = (TILES, 128)
    strip = lax.broadcasted_iota(jnp.int32, shape, 0)
    lane_cell = lax.broadcasted_iota(jnp.int32, (1, 128), 1) // NCY

    def load(key):
        return rows[pl.ds(ROW[key], TILES, stride=ROWS), :]

    def from_next(value):
        return jnp.where(strip < TILES - 1, row_roll(value, -1), 0.0)

    def from_last(value):
        return jnp.where(strip > 0, row_roll(value, 1), 0.0)

    half = {}
    for dy in (0, 1):
        half[0, 0, dy] = load(("s", 0, 0, dy)) + from_next(load(("s", -1, -1, dy))) + from_last(load(("s", 1, 1, dy)))
    for dy in (-1, 0, 1):
        half[1, 0, dy] = load(("s", 0, 1, dy)) + from_next(load(("s", -1, 0, dy)))
        half[0, 1, dy] = load(("z", 0, 0, dy)) + from_next(load(("z", -1, -1, dy))) + from_last(load(("z", 1, 1, dy)))
        half[1, 1, dy] = load(("z", 0, 1, dy)) + from_next(load(("z", -1, 0, dy)))
        half[-1, 1, dy] = load(("z", 0, -1, dy)) + from_last(load(("z", 1, 0, dy)))
    rhs = load(("r", 0)) + from_next(load(("r", -1))) + from_last(load(("r", 1)))
    centre = half.pop((0, 0, 0))
    scale = COARSE_DAMPING / centre

    def shifted(value, dx, dz, dy):
        by = -(dz * NCY + dy)
        if by:
            value = lane_roll(value, by)
        return row_roll(value, -dx) if dx else value

    full = dict(half)
    for (dx, dz, dy), value in half.items():
        full[-dx, -dz, -dy] = shifted(value, -dx, -dz, -dy)
    coarse = scale * rhs
    for _ in range(SWEEPS - 1):
        applied = centre * coarse
        for dz in (-1, 0, 1):
            for dy in (-1, 0, 1):
                moved = shifted(coarse, 0, dz, dy)
                for dx in (-1, 0, 1):
                    if (dx, dz, dy) in full:
                        applied = applied + full[dx, dz, dy] * shifted(moved, dx, 0, 0)
        coarse = coarse + scale * (rhs - applied)

    def strip_row(at):
        return jnp.sum(jnp.where(strip == at, coarse, 0.0), axis=0, keepdims=True)

    here = strip_row(tile)
    own_row = jnp.where(lane_cell == cell, here, 0.0)
    picked = [
        own_row,
        jnp.where(lane_cell == cell, strip_row(tile - 1), 0.0),
        jnp.where(lane_cell == cell, strip_row(tile + 1), 0.0),
        jnp.where(lane_cell == near_cell, here, 0.0),
        lane_roll(own_row, 1),
        lane_roll(own_row, -1),
        jnp.zeros((2, 128), F32),
    ]
    picked = jnp.concatenate(picked, axis=0)
    i = lax.broadcasted_iota(jnp.int32, (128, NY), 0)
    j = lax.broadcasted_iota(jnp.int32, (128, NY), 1)
    spread = (i % NCY == j // EDGE).astype(F32)
    fine = jnp.dot(picked, spread, precision=lax.Precision.HIGHEST, preferred_element_type=F32)
    lane = lax.broadcasted_iota(jnp.int32, (1, NY), 1) % EDGE
    near_y = jnp.where(lane == 0, fine[4:5], jnp.where(lane == EDGE - 1, fine[5:6], 0.0))
    for x in range(NXL):
        value = own[x] * fine[0:1] + beside_y[x] * near_y + beside_z[x] * fine[3:4]
        if x == 0:
            value = value + beside_x[0] * fine[1:2]
        if x == NXL - 1:
            value = value + beside_x[1] * fine[2:3]
        pressure[x] = value


def struct(*shape):
    return jax.ShapeDtypeStruct(shape, F32)


def call(kernel, outs, scratch=(), **kw):
    many = isinstance(outs, (list, tuple))
    return pl.pallas_call(
        kernel,
        out_shape=outs,
        out_specs=[VMEM] * len(outs) if many else VMEM,
        scratch_shapes=list(scratch),
        compiler_params=pltpu.CompilerParams(vmem_limit_bytes=48 * 1024 * 1024),
        **kw,
    )


def body(classes, well_mask, source):
    def swap(values, axis, count):
        return [lax.ppermute(v, axis, swap_pairs(count, i == 0)) for i, v in enumerate(values)]

    z_out = call(pack_z, [struct(3, NXL, NY)] * 2, in_specs=[VMEM] * 2)(classes, well_mask)
    z_a, z_b = swap(z_out, "layer", LAYERS)
    x_out = call(pack_x, [struct(4, NZL, NY)] * 2, in_specs=[VMEM] * 4)(classes, well_mask, z_a, z_b)
    x_a, x_b = swap(x_out, "tile", TILES)
    block = struct(NXL, NZL, NY)
    part, own, beside_y, beside_z, beside_x = call(
        assemble,
        [struct(LAYERS, ROWS, 128), block, block, block, struct(2, NZL, NY)],
        [pltpu.VMEM((64, NY), F32), pltpu.VMEM((6, 64, 128), F32), pltpu.VMEM((3, ROWS, 128), F32)],
        in_specs=[VMEM] * 7,
    )(classes, well_mask, source, z_a, z_b, x_a, x_b)
    received = lax.all_to_all(part, "layer", 0, 0, tiled=True)
    column = call(add_layers, struct(TILES, ROWS, 128), in_specs=[VMEM])(received)
    rows = lax.all_to_all(column, "tile", 0, 0, tiled=True).reshape(TILES * ROWS, 128)
    return call(solve, block, in_specs=[VMEM] * 5)(rows, own, beside_y, beside_z, beside_x)


def solution(mesh):
    spec = P("tile", "layer", None)
    return jax.shard_map(body, mesh=mesh, in_specs=(spec, spec, spec), out_specs=spec, check_vma=False)
```

```python
import functools

import jax
import jax.numpy as jnp
import numpy as np
from jax import lax
from jax.experimental import pallas as pl
from jax.experimental.pallas import tpu as pltpu
from jax.sharding import PartitionSpec as P

EDGE = 16
SWEEPS = 4
FINE_DAMPING = 0.67
COARSE_DAMPING = 0.5
NXL, NZL, NY = 16, 8, 512
TILES, LAYERS = 16, 8
NCY = NY // EDGE
NCZ = LAYERS * NZL // EDGE
ROWS = 8
F32 = jnp.float32
VMEM = pl.BlockSpec(memory_space=pltpu.VMEM)

NODES = ("N", "Q", "Z", "QZ")


def order(key):
    return NODES.index(key[0]) * 2 + (key[1] == "v")


def pair(a, b):
    return (a, b) if order(a) <= order(b) else (b, a)


SLOT = {}
for where, row in (("own", 0), ("near", 2)):
    for i, key in enumerate(
        [("s", 0, 0, 0), ("s", 0, 0, 1), ("s", 1, 1, 0), ("s", 1, 1, 1)]
        + [("s", 0, 1, -1), ("s", 0, 1, 0), ("s", 0, 1, 1), ("r", 0)]
    ):
        SLOT[where, key] = (row + i // 4, i % 4)
SLOT["own", ("r", 1)] = (7, 0)
SLOT["near", ("r", 1)] = (7, 2)
for i, (lo, hi, dy) in enumerate((lo, hi, dy) for lo in (0, 1) for hi in (0, 1) for dy in (-1, 0, 1)):
    SLOT["low", ("z", lo, hi, dy)] = (4 + i // 4, i % 4)
HERE = ("N", "Q")
BESIDE = ("Z", "QZ")


def cells_of(layer):
    own = layer // 2
    near = own + 1 if layer % 2 else own - 1
    return {"own": own, "near": near, "low": min(own, near)}


def swap_pairs(count, first):
    if first:
        return [(i, i ^ 1) for i in range(count)]
    return [(i, (((i + 1) ^ 1) - 1) % count) for i in range(count)]


def pack(cls_hbm, well_hbm, src_hbm, z_b, z_a, x_b, x_a, cls, well, src, sems):
    copies = [
        pltpu.make_async_copy(cls_hbm, cls, sems.at[0]),
        pltpu.make_async_copy(well_hbm, well, sems.at[1]),
        pltpu.make_async_copy(src_hbm.at[0], src, sems.at[2]),
    ]
    for copy in copies:
        copy.start()
    for copy in copies:
        copy.wait()

    def both(first, last, odd, b, a):
        a[0] = jnp.where(odd, first, last)
        b[0] = jnp.where(odd, last, first)

    odd_z = lax.axis_index("layer") % 2 == 1
    odd_x = lax.axis_index("tile") % 2 == 1
    both(cls[:, 0, :].astype(F32), cls[:, NZL - 1, :].astype(F32), odd_z, z_b, z_a)
    both(cls[0].astype(F32), cls[NXL - 1].astype(F32), odd_x, x_b, x_a)
    second = cls[:, 1, :].astype(F32)
    wells = well[:, 0, :].astype(F32)
    for out in (z_b, z_a):
        out[1] = second
        out[2] = wells
    for out in (x_b, x_a):
        out[1] = cls[1].astype(F32)
        out[2] = cls[2].astype(F32)
        out[3] = well[0].astype(F32)
        out[4] = well[1].astype(F32)
        out[5] = src[...]


def pack_lines(old_b, old_a, z_b, z_a, x_b, x_a):
    odd_z = lax.axis_index("layer") % 2 == 1

    def head(ref, plane):
        return ref[plane, 0:8, :]

    up = [jnp.where(odd_z, head(z_b, i), head(z_a, i)) for i in range(3)]
    down = jnp.where(odd_z, head(z_a, 0), head(z_b, 0))
    lines = [down[0:1], down[1:2], up[0][0:1], up[0][1:2], up[1][0:1], up[2][0:1], jnp.zeros((2, NY), F32)]
    lines = jnp.concatenate(lines, axis=0)
    for old, out in ((old_b, x_b), (old_a, x_a)):
        for i in range(6):
            out[i] = old[i]
        out[6] = lines


def lane_roll(value, by):
    return pltpu.roll(value, by % value.shape[-1], value.ndim - 1)


def row_roll(value, by):
    return pltpu.roll(value, by % value.shape[0], 0)


def assemble(cls, well, src, z_b, z_a, x_b, x_a, part, own, beside_y, beside_z, beside_x, lanes_ref, g_ref, out_ref):
    tile, layer = lax.axis_index("tile"), lax.axis_index("layer")
    odd_z, odd_x = layer % 2 == 1, tile % 2 == 1
    has_up, has_down = (layer < LAYERS - 1).astype(F32), (layer > 0).astype(F32)
    has_right, has_left = (tile < TILES - 1).astype(F32), (tile > 0).astype(F32)
    is_first = 1.0 - has_left

    def resist(c):
        return jnp.exp(2.5 - c * F32(1.0 / 3.0))

    def sink(c, w):
        return 0.5 * w * jnp.exp(c * F32(1.0 / 3.0) - 2.5)

    plane = (NZL, NY)
    zrow = lax.broadcasted_iota(jnp.int32, plane, 0)
    lane = lax.broadcasted_iota(jnp.int32, plane, 1)
    m_l = lane % EDGE == 0
    m_r = lane % EDGE == EDGE - 1

    def y_faces(r):
        ty = 2.0 / (r + lane_roll(r, -1))
        ty = jnp.where(lax.broadcasted_iota(jnp.int32, r.shape, 1) < NY - 1, ty, 0.0)
        return ty, lane_roll(ty, 1)

    def y_part(d, ty, ty_lo):
        at = lax.broadcasted_iota(jnp.int32, d.shape, 1) % EDGE
        return d * jnp.where(at == 0, ty_lo, jnp.where(at == EDGE - 1, ty, 0.0))

    up = [jnp.where(odd_z, z_b[i], z_a[i]) for i in range(3)]
    down = jnp.where(odd_z, z_a[0], z_b[0])
    right = [jnp.where(odd_x, x_b[i], x_a[i]) for i in range(7)]
    left = jnp.where(odd_x, x_a[0], x_b[0])
    lines = right[6]

    def top(r7, r8, r9, s8, r8_left, r8_right, keep_left, keep_right):
        tx_lo, tx_hi = 2.0 / (r8 + r8_left) * keep_left, 2.0 / (r8 + r8_right) * keep_right
        t78, t89 = 0.5 / (r7 + r8) * has_up, 0.5 / (r8 + r9)
        ty, ty_lo = y_faces(r8)
        d = FINE_DAMPING / (s8 + tx_lo + tx_hi + t78 + t89 + ty + ty_lo)
        return d, tx_lo, tx_hi, y_part(d, ty, ty_lo), jnp.where(odd_z, d * t78, 0.0), 1.0 - d * s8

    tall = (NXL, NY)
    xrow = lax.broadcasted_iota(jnp.int32, tall, 0)
    r8, r9, s8 = resist(up[0]), resist(up[1]), sink(up[0], up[2])
    lines_r = resist(lines)
    r8_16, r8_17, r9_16 = lines_r[2:3], lines_r[3:4], lines_r[4:5]
    r7 = resist(cls[:, NZL - 1, :].astype(F32))
    d8, _, tx8_hi, ey8, ez8, o8 = top(
        r7,
        r8,
        r9,
        s8,
        row_roll(r8, 1),
        jnp.where(xrow == NXL - 1, jnp.broadcast_to(r8_16, tall), row_roll(r8, -1)),
        jnp.where(xrow == 0, 0.0, 1.0),
        jnp.where(xrow == NXL - 1, has_right, 1.0),
    )
    ex8 = jnp.where(xrow == NXL - 1, d8 * tx8_hi, 0.0)
    o8 = o8 - ex8 - ey8 - ez8
    d16, tx16_lo, _, ey16, ez16, o16 = top(
        resist(right[0][NZL - 1 : NZL]), r8_16, r9_16, sink(lines[2:3], lines[5:6]), r8[NXL - 1 : NXL], r8_17, has_right, 1.0
    )
    ex16 = d16 * tx16_lo
    o16 = o16 - ex16 - ey16 - ez16

    def above(own_u, own_v, own_z, other, names):
        (a, az), (b, bz) = names
        out = {
            (a, "u"): jnp.where(odd_z, own_z, own_u),
            (a, "v"): jnp.where(odd_z, 0.0, own_v),
            (az, "u"): jnp.where(odd_z, own_u, 0.0),
            (az, "v"): jnp.where(odd_z, own_v, 0.0),
        }
        if other is not None:
            out[b, "u"] = jnp.where(odd_z, 0.0, other)
            out[bz, "u"] = jnp.where(odd_z, other, 0.0)
        return out

    columns = (("N", "Z"), ("Q", "QZ"))
    inside = above(o8, ey8, ez8, ex8, columns)
    tops = []
    for x in range(NXL):
        tops.append({k: v[x : x + 1] for k, v in inside.items() if x == NXL - 1 or k[0] in "NZ"})
    tops.append(above(o16, ey16, ez16, ex16, columns[::-1]))

    cs = [cls[x].astype(F32) for x in range(NXL)] + right[0:2]
    rs = [resist(c) for c in cs]
    ss = [sink(cs[x], well[x].astype(F32)) for x in range(NXL)] + [sink(right[i], right[3 + i]) for i in range(2)]
    txs = [2.0 / (resist(left) + rs[0]) * has_left]
    txs += [2.0 / (rs[x] + rs[x + 1]) for x in range(NXL - 1)]
    txs += [2.0 / (rs[NXL - 1] + rs[NXL]) * has_right, 2.0 / (rs[NXL] + rs[NXL + 1]), 2.0 / (rs[NXL + 1] + resist(right[2]))]
    at_zb = zrow == jnp.where(odd_z, NZL - 1, 0)
    basis, tzs, tys = [], [], []
    for x in range(NXL + 2):
        r = rs[x]
        if x < NXL:
            below, over = resist(down[x : x + 1]), r8[x : x + 1]
        else:
            below, over = lines_r[x - NXL : x - NXL + 1], (r8_16, r8_17)[x - NXL]
        r_up = jnp.where(zrow == NZL - 1, jnp.broadcast_to(over, plane), row_roll(r, -1))
        r_dn = jnp.where(zrow == 0, jnp.broadcast_to(below, plane), row_roll(r, 1))
        tz_hi = 0.5 / (r + r_up) * jnp.where(zrow == NZL - 1, has_up, 1.0)
        tz_lo = 0.5 / (r + r_dn) * jnp.where(zrow == 0, has_down, 1.0)
        ty, ty_lo = y_faces(r)
        d = FINE_DAMPING / (ss[x] + txs[x] + txs[x + 1] + tz_hi + tz_lo + ty + ty_lo)
        ey = d * jnp.where(m_l, ty_lo, jnp.where(m_r, ty, 0.0))
        ez = jnp.where(at_zb, d * jnp.where(odd_z, tz_hi, tz_lo), 0.0)
        o = 1.0 - d * ss[x] - ey - ez
        (a, az), (b, _) = columns if x < NXL else columns[::-1]
        here = {(az, "u"): ez, (a, "v"): ey}
        if x == 0:
            beside_x[0] = d * txs[0]
            o = o - d * txs[0]
        if x in (NXL - 1, NXL):
            here[b, "u"] = d * txs[NXL]
            o = o - here[b, "u"]
        if x < NXL:
            own[x] = o
            beside_y[x] = ey
            beside_z[x] = ez
        if x == NXL - 1:
            beside_x[1] = here[b, "u"]
        here[a, "u"] = o
        basis.append(here)
        tzs.append(tz_hi)
        tys.append(ty)

    sums = {}

    def add(key, value):
        sums[key] = sums[key] + value if key in sums else value

    def add_pairs(weight, values):
        keys = sorted(values, key=order)
        for i, a in enumerate(keys):
            scaled = weight * values[a]
            for b in keys[i:]:
                add((a, b), scaled * values[b])

    def minus(a, b):
        out = {}
        for key in {**a, **b}:
            if key in a and key in b:
                out[key] = a[key] - b[key]
            else:
                out[key] = a[key] if key in a else -b[key]
        return out

    for x in range(NXL + 1):
        here = basis[x]
        counted = is_first if x == 0 else has_right if x == NXL else None

        def weigh(value):
            return value if counted is None else value * counted

        add_pairs(weigh(ss[x]), here)
        source = weigh(src[x] if x < NXL else right[5])
        for key, value in here.items():
            add(("rhs", key), value * source)
        add_pairs(weigh(txs[x + 1]), minus(here, basis[x + 1]))
        there = {}
        for key in {**here, **tops[x]}:
            row = jnp.broadcast_to(tops[x][key], plane)
            there[key] = jnp.where(zrow == NZL - 1, row, row_roll(here[key], -1) if key in here else 0.0)
        add_pairs(weigh(tzs[x]), minus(here, there))
        rolled = {key: lane_roll(value, -1) for key, value in here.items()}
        there = {}
        for node in {key[0]: None for key in here}:
            u, v = rolled.get((node, "u"), 0.0), rolled.get((node, "v"), 0.0)
            there[node, "u"] = jnp.where(m_r, v, u)
            there[node, "v"] = jnp.where(m_r, u, v)
        add_pairs(weigh(tys[x]), minus(here, there))

    index = {key: i for i, key in enumerate(sums)}
    for key, i in index.items():
        lanes_ref[i : i + 1, :] = jnp.sum(sums[key], axis=0, keepdims=True)
    count = -(-len(index) // 8) * 8
    if count > len(index):
        lanes_ref[len(index) : count, :] = jnp.zeros((count - len(index), NY), F32)

    j = lax.broadcasted_iota(jnp.int32, (NY, 128), 0)
    n = lax.broadcasted_iota(jnp.int32, (NY, 128), 1)
    group, pos = n // NCY, j % EDGE
    taken = (group == 0) | ((group == 1) & (pos == 0)) | ((group == 2) & (pos >= EDGE - 2))
    select = ((j // EDGE == n % NCY) & taken).astype(F32)
    grouped = jnp.dot(lanes_ref[0:count, :], select, precision=lax.Precision.HIGHEST, preferred_element_type=F32)
    gl = lax.broadcasted_iota(jnp.int32, (count, 128), 1)
    g_l_next = jnp.where(gl < NCY - 1, lane_roll(grouped, -(NCY + 1)), 0.0)
    g_r_next = jnp.where((gl > 0) & (gl < NCY), lane_roll(grouped, -(2 * NCY - 1)), 0.0)
    forms = {
        "all": jnp.where(gl < NCY, grouped, 0.0),
        "L": jnp.where(gl < NCY, lane_roll(grouped, -NCY), 0.0),
        "R": jnp.where(gl < NCY, lane_roll(grouped, -2 * NCY), 0.0),
        "Ls": g_l_next,
        "Rs": g_r_next,
        "vv": g_l_next + g_r_next,
    }
    at = {}
    for i, (name, value) in enumerate(forms.items()):
        at[name] = i
        g_ref[i, 0:count, :] = value

    def taken_rows(terms):
        total = None
        for name, key in terms:
            if key in index:
                q = index[key]
                row = g_ref[at[name], q : q + 1, :]
                total = row if total is None else total + row
        return total

    def terms_of(a, b, dy):
        au, av, bu, bv = (a, "u"), (a, "v"), (b, "u"), (b, "v")
        if a == b:
            if dy == 0:
                return [("all", pair(au, au)), ("vv", pair(av, av))]
            return [("Ls", pair(au, av)), ("R", pair(au, av))]
        if dy == 0:
            return [("all", pair(au, bu)), ("vv", pair(av, bv))]
        if dy < 0:
            return [("L", pair(au, bv)), ("Rs", pair(av, bu))]
        return [("R", pair(au, bv)), ("Ls", pair(av, bu))]

    nothing = jnp.zeros((1, 128), F32)
    out_ref[...] = jnp.zeros(out_ref.shape, F32)
    spots = [(where, k) for where in ("own", "near", "low") for k in range(NCZ)]
    for (where, key), (r, k) in SLOT.items():
        names = {"own": HERE, "near": BESIDE}.get(where)
        if key[0] == "s":
            row = taken_rows(terms_of(names[key[1]], names[key[2]], key[3]))
        elif key[0] == "r":
            row = taken_rows([("all", ("rhs", (names[key[1]], "u"))), ("vv", ("rhs", (names[key[1]], "v")))])
        else:
            when_odd = taken_rows(terms_of(HERE[key[1]], BESIDE[key[2]], key[3]))
            when_even = taken_rows(terms_of(BESIDE[key[1]], HERE[key[2]], key[3]))
            when_odd = nothing if when_odd is None else when_odd
            when_even = nothing if when_even is None else when_even
            row = jnp.where(odd_z, when_odd, when_even)
        if row is not None:
            out_ref[spots.index((where, k)), r : r + 1, :] = row
    cell = layer // 2
    near_cell = jnp.where(odd_z, cell + 1, cell - 1)
    coarse_layer = {"own": cell, "near": near_cell, "low": jnp.minimum(cell, near_cell)}
    group = lax.broadcasted_iota(jnp.int32, (ROWS, 128), 1) // NCY
    total = jnp.zeros((ROWS, 128), F32)
    for i, (where, k) in enumerate(spots):
        if (where, k) not in {(w, kk) for (w, _), (_, kk) in SLOT.items()}:
            continue
        rows = out_ref[i]
        spread = rows
        for n in range(1, NCZ):
            spread = spread + lane_roll(rows, n * NCY)
        total = total + jnp.where(group == (coarse_layer[where] + k + NCZ) % NCZ, spread, 0.0)
    for k in range(TILES * LAYERS):
        part[k] = total


def solve(rows, own, beside_y, beside_z, beside_x, pressure):
    tile, layer = lax.axis_index("tile"), lax.axis_index("layer")
    odd_z = layer % 2 == 1
    cell = layer // 2
    near_cell = jnp.where(odd_z, cell + 1, cell - 1)
    shape = (TILES, 128)
    strip = lax.broadcasted_iota(jnp.int32, shape, 0)
    group = lax.broadcasted_iota(jnp.int32, shape, 1) // NCY
    lane_cell = group[0:1]

    loaded = {}

    def load(layer_from, row):
        if (layer_from, row) not in loaded:
            loaded[layer_from, row] = rows[pl.ds(layer_from * ROWS + row, TILES, stride=LAYERS * ROWS), :]
        return loaded[layer_from, row]

    by_shift = {}
    for (where, key), (row, k) in SLOT.items():
        total = None
        for l in range(LAYERS):
            z = cells_of(l)[where]
            if 0 <= z and max(cells_of(l)["own"], cells_of(l)["near"] if where != "own" else 0) < NCZ:
                term = jnp.where(group == (z + k) % NCZ, load(l, row), 0.0)
                total = term if total is None else total + term
        by_shift[key, k] = by_shift[key, k] + total if (key, k) in by_shift else total
    terms = {}
    for (key, k), value in by_shift.items():
        value = lane_roll(value, -k * NCY) if k else value
        terms[key] = terms[key] + value if key in terms else value

    def from_last(value):
        return jnp.where(strip > 0, row_roll(value, 1), 0.0)

    half = {}
    for dy in (0, 1):
        half[0, 0, dy] = terms["s", 0, 0, dy] + from_last(terms["s", 1, 1, dy])
    for dy in (-1, 0, 1):
        half[1, 0, dy] = terms["s", 0, 1, dy]
        half[0, 1, dy] = terms["z", 0, 0, dy] + from_last(terms["z", 1, 1, dy])
        half[1, 1, dy] = terms["z", 0, 1, dy]
        half[-1, 1, dy] = from_last(terms["z", 1, 0, dy])
    rhs = terms["r", 0] + from_last(terms["r", 1])
    centre = half.pop((0, 0, 0))
    scale = COARSE_DAMPING / centre

    def shifted(value, dx, dz, dy):
        by = -(dz * NCY + dy)
        if by:
            value = lane_roll(value, by)
        return row_roll(value, -dx) if dx else value

    full = dict(half)
    for (dx, dz, dy), value in half.items():
        full[-dx, -dz, -dy] = shifted(value, -dx, -dz, -dy)
    coarse = scale * rhs
    for _ in range(SWEEPS - 1):
        applied = centre * coarse
        for dz in (-1, 0, 1):
            for dy in (-1, 0, 1):
                moved = shifted(coarse, 0, dz, dy)
                for dx in (-1, 0, 1):
                    if (dx, dz, dy) in full:
                        applied = applied + full[dx, dz, dy] * shifted(moved, dx, 0, 0)
        coarse = coarse + scale * (rhs - applied)

    def strip_row(at):
        return jnp.sum(jnp.where(strip == at, coarse, 0.0), axis=0, keepdims=True)

    here = strip_row(tile)
    own_row = jnp.where(lane_cell == cell, here, 0.0)
    picked = [
        own_row,
        jnp.where(lane_cell == cell, strip_row(tile - 1), 0.0),
        jnp.where(lane_cell == cell, strip_row(tile + 1), 0.0),
        jnp.where(lane_cell == near_cell, here, 0.0),
        lane_roll(own_row, 1),
        lane_roll(own_row, -1),
        jnp.zeros((2, 128), F32),
    ]
    picked = jnp.concatenate(picked, axis=0)
    i = lax.broadcasted_iota(jnp.int32, (128, NY), 0)
    j = lax.broadcasted_iota(jnp.int32, (128, NY), 1)
    spread = (i % NCY == j // EDGE).astype(F32)
    fine = jnp.dot(picked, spread, precision=lax.Precision.HIGHEST, preferred_element_type=F32)
    lane = lax.broadcasted_iota(jnp.int32, (1, NY), 1) % EDGE
    near_y = jnp.where(lane == 0, fine[4:5], jnp.where(lane == EDGE - 1, fine[5:6], 0.0))
    for x in range(NXL):
        value = own[x] * fine[0:1] + beside_y[x] * near_y + beside_z[x] * fine[3:4]
        if x == 0:
            value = value + beside_x[0] * fine[1:2]
        if x == NXL - 1:
            value = value + beside_x[1] * fine[2:3]
        pressure[x] = value


def struct(*shape):
    return jax.ShapeDtypeStruct(shape, F32)


def call(kernel, outs, scratch=(), **kw):
    many = isinstance(outs, (list, tuple))
    return pl.pallas_call(
        kernel,
        out_shape=outs,
        out_specs=[VMEM] * len(outs) if many else VMEM,
        scratch_shapes=list(scratch),
        compiler_params=pltpu.CompilerParams(vmem_limit_bytes=48 * 1024 * 1024),
        **kw,
    )


def body(classes, well_mask, source):
    def swap(values, axis, count):
        far = lax.ppermute(values[0], axis, swap_pairs(count, False))
        return far, lax.ppermute(values[1], axis, swap_pairs(count, True))

    block = struct(NXL, NZL, NY)
    ints = pltpu.VMEM((NXL, NZL, NY), jnp.int32)
    z_message, x_message = struct(3, NXL, NY), struct(7, NZL, NY)
    z_b, z_a, x_b, x_a = call(
        pack,
        [z_message, z_message, x_message, x_message],
        [ints, ints, pltpu.VMEM((NZL, NY), F32), pltpu.SemaphoreType.DMA((3,))],
        in_specs=[pl.BlockSpec(memory_space=pltpu.HBM)] * 3,
    )(*(pltpu.with_memory_space_constraint(v, pltpu.HBM) for v in (classes, well_mask, source)))
    z_b, z_a = swap((z_b, z_a), "layer", LAYERS)
    x_out = call(pack_lines, [x_message] * 2, in_specs=[VMEM] * 4)(x_b, x_a, z_b, z_a)
    x_b, x_a = swap(x_out, "tile", TILES)
    part, own, beside_y, beside_z, beside_x = call(
        assemble,
        [struct(TILES * LAYERS, ROWS, 128), block, block, block, struct(2, NZL, NY)],
        [pltpu.VMEM((64, NY), F32), pltpu.VMEM((6, 64, 128), F32), pltpu.VMEM((3 * NCZ, ROWS, 128), F32)],
        in_specs=[VMEM] * 7,
    )(classes, well_mask, source, z_b, z_a, x_b, x_a)
    received = lax.all_to_all(part, ("tile", "layer"), 0, 0, tiled=True)
    rows = received.reshape(TILES * LAYERS * ROWS, 128)
    return call(solve, block, in_specs=[VMEM] * 5)(rows, own, beside_y, beside_z, beside_x)


def solution(mesh):
    spec = P("tile", "layer", None)
    return jax.shard_map(body, mesh=mesh, in_specs=(spec, spec, spec), out_specs=spec, check_vma=False)
```

```python
import functools

import jax
import jax.numpy as jnp
import numpy as np
from jax import lax
from jax.experimental import pallas as pl
from jax.experimental.pallas import tpu as pltpu
from jax.sharding import PartitionSpec as P

EDGE = 16
SWEEPS = 4
FINE_DAMPING = 0.67
COARSE_DAMPING = 0.5
NXL, NZL, NY = 16, 8, 512
TILES, LAYERS = 16, 8
NCY = NY // EDGE
NCZ = LAYERS * NZL // EDGE
ROWS = 8
F32 = jnp.float32
VMEM = pl.BlockSpec(memory_space=pltpu.VMEM)

NODES = ("N", "Q", "Z", "QZ")


def order(key):
    return NODES.index(key[0]) * 2 + (key[1] == "v")


def pair(a, b):
    return (a, b) if order(a) <= order(b) else (b, a)


SLOT = {}
for where, row in (("own", 0), ("near", 2)):
    for i, key in enumerate(
        [("s", 0, 0, 0), ("s", 0, 0, 1), ("s", 1, 1, 0), ("s", 1, 1, 1)]
        + [("s", 0, 1, -1), ("s", 0, 1, 0), ("s", 0, 1, 1), ("r", 0)]
    ):
        SLOT[where, key] = (row + i // 4, i % 4)
SLOT["own", ("r", 1)] = (7, 0)
SLOT["near", ("r", 1)] = (7, 2)
for i, (lo, hi, dy) in enumerate((lo, hi, dy) for lo in (0, 1) for hi in (0, 1) for dy in (-1, 0, 1)):
    SLOT["low", ("z", lo, hi, dy)] = (4 + i // 4, i % 4)
HERE = ("N", "Q")
BESIDE = ("Z", "QZ")


def cells_of(layer):
    own = layer // 2
    near = own + 1 if layer % 2 else own - 1
    return {"own": own, "near": near, "low": min(own, near)}


def swap_pairs(count, first):
    if first:
        return [(i, i ^ 1) for i in range(count)]
    return [(i, (((i + 1) ^ 1) - 1) % count) for i in range(count)]


def pack(cls_hbm, well_hbm, src_hbm, z_b, z_a, x_b, x_a, cls, well, src, sems):
    copies = [
        pltpu.make_async_copy(cls_hbm, cls, sems.at[0]),
        pltpu.make_async_copy(well_hbm, well, sems.at[1]),
        pltpu.make_async_copy(src_hbm.at[0], src, sems.at[2]),
    ]
    for copy in copies:
        copy.start()
    for copy in copies:
        copy.wait()

    def both(first, last, odd, b, a):
        a[0] = jnp.where(odd, first, last)
        b[0] = jnp.where(odd, last, first)

    odd_z = lax.axis_index("layer") % 2 == 1
    odd_x = lax.axis_index("tile") % 2 == 1
    both(cls[:, 0, :].astype(F32), cls[:, NZL - 1, :].astype(F32), odd_z, z_b, z_a)
    both(cls[0].astype(F32), cls[NXL - 1].astype(F32), odd_x, x_b, x_a)
    second = cls[:, 1, :].astype(F32)
    wells = well[:, 0, :].astype(F32)
    for out in (z_b, z_a):
        out[1] = second
        out[2] = wells
    for out in (x_b, x_a):
        out[1] = cls[1].astype(F32)
        out[2] = cls[2].astype(F32)
        out[3] = well[0].astype(F32)
        out[4] = well[1].astype(F32)
        out[5] = src[...]


def pack_lines(old_b, old_a, z_b, z_a, x_b, x_a):
    odd_z = lax.axis_index("layer") % 2 == 1

    def head(ref, plane):
        return ref[plane, 0:8, :]

    up = [jnp.where(odd_z, head(z_b, i), head(z_a, i)) for i in range(3)]
    down = jnp.where(odd_z, head(z_a, 0), head(z_b, 0))
    lines = [down[0:1], down[1:2], up[0][0:1], up[0][1:2], up[1][0:1], up[2][0:1], jnp.zeros((2, NY), F32)]
    lines = jnp.concatenate(lines, axis=0)
    for old, out in ((old_b, x_b), (old_a, x_a)):
        for i in range(6):
            out[i] = old[i]
        out[6] = lines


def lane_roll(value, by):
    return pltpu.roll(value, by % value.shape[-1], value.ndim - 1)


def row_roll(value, by):
    return pltpu.roll(value, by % value.shape[0], 0)


def resist(c):
    return jnp.exp(2.5 - c * F32(1.0 / 3.0))


def sink(c, w):
    return 0.5 * w * jnp.exp(c * F32(1.0 / 3.0) - 2.5)


def y_faces(r):
    ty = 2.0 / (r + lane_roll(r, -1))
    ty = jnp.where(lax.broadcasted_iota(jnp.int32, r.shape, 1) < NY - 1, ty, 0.0)
    return ty, lane_roll(ty, 1)


def y_part(d, ty, ty_lo):
    at = lax.broadcasted_iota(jnp.int32, d.shape, 1) % EDGE
    return d * jnp.where(at == 0, ty_lo, jnp.where(at == EDGE - 1, ty, 0.0))


def minus(a, b):
    out = {}
    for key in {**a, **b}:
        if key in a and key in b:
            out[key] = a[key] - b[key]
        else:
            out[key] = a[key] if key in a else -b[key]
    return out


COLUMNS = (("N", "Z"), ("Q", "QZ"))


class Block:
    def __init__(self, z_b, z_a):
        self.tile, self.layer = lax.axis_index("tile"), lax.axis_index("layer")
        self.odd_z, self.odd_x = self.layer % 2 == 1, self.tile % 2 == 1
        self.has_up, self.has_down = (self.layer < LAYERS - 1).astype(F32), (self.layer > 0).astype(F32)
        self.has_right, self.has_left = (self.tile < TILES - 1).astype(F32), (self.tile > 0).astype(F32)
        self.plane = (NZL, NY)
        self.zrow = lax.broadcasted_iota(jnp.int32, self.plane, 0)
        self.m_r = lax.broadcasted_iota(jnp.int32, self.plane, 1) % EDGE == EDGE - 1
        self.at_zb = self.zrow == jnp.where(self.odd_z, NZL - 1, 0)
        self.up_mask = jnp.where(self.zrow == NZL - 1, self.has_up, 1.0)
        self.down_mask = jnp.where(self.zrow == 0, self.has_down, 1.0)
        self.sums = {}
        self.z_b, self.z_a = z_b, z_a

    def up(self, i, rows=slice(None)):
        return jnp.where(self.odd_z, self.z_b[i, rows, :], self.z_a[i, rows, :])

    def down(self, rows=slice(None)):
        return jnp.where(self.odd_z, self.z_a[0, rows, :], self.z_b[0, rows, :])

    def last_row(self, row, value):
        return jnp.where(self.zrow == NZL - 1, jnp.broadcast_to(row, self.plane), value)

    def basis(self, r, s, tx_lo, tx_hi, below, over):
        r_up = self.last_row(over, row_roll(r, -1))
        r_dn = jnp.where(self.zrow == 0, jnp.broadcast_to(below, self.plane), row_roll(r, 1))
        tz_hi, tz_lo = 0.5 / (r + r_up) * self.up_mask, 0.5 / (r + r_dn) * self.down_mask
        ty, ty_lo = y_faces(r)
        d = FINE_DAMPING / (s + tx_lo + tx_hi + tz_hi + tz_lo + ty + ty_lo)
        ey = y_part(d, ty, ty_lo)
        ez = jnp.where(self.at_zb, d * jnp.where(self.odd_z, tz_hi, tz_lo), 0.0)
        return 1.0 - d * s - ey - ez, ey, ez, d, tz_hi, ty

    def top(self, r7, r8, r9, s8, r8_left, r8_right, keep_left, keep_right):
        tx_lo, tx_hi = 2.0 / (r8 + r8_left) * keep_left, 2.0 / (r8 + r8_right) * keep_right
        t78, t89 = 0.5 / (r7 + r8) * self.has_up, 0.5 / (r8 + r9)
        ty, ty_lo = y_faces(r8)
        d = FINE_DAMPING / (s8 + tx_lo + tx_hi + t78 + t89 + ty + ty_lo)
        ey, ez = y_part(d, ty, ty_lo), jnp.where(self.odd_z, d * t78, 0.0)
        return 1.0 - d * s8 - ey - ez, ey, ez, d * tx_lo, d * tx_hi

    def above(self, o, ey, ez, other=None, columns=COLUMNS):
        (a, az), (b, bz) = columns
        out = {
            (a, "u"): jnp.where(self.odd_z, ez, o),
            (a, "v"): jnp.where(self.odd_z, 0.0, ey),
            (az, "u"): jnp.where(self.odd_z, o, 0.0),
            (az, "v"): jnp.where(self.odd_z, ey, 0.0),
        }
        if other is not None:
            out[b, "u"] = jnp.where(self.odd_z, 0.0, other)
            out[bz, "u"] = jnp.where(self.odd_z, other, 0.0)
        return out

    def add(self, key, value):
        self.sums[key] = self.sums[key] + value if key in self.sums else value

    def add_pairs(self, weight, values):
        keys = sorted(values, key=order)
        for i, a in enumerate(keys):
            scaled = weight * values[a]
            for b in keys[i:]:
                self.add((a, b), scaled * values[b])

    def add_plane(self, here, top, s, tz, ty, source, counted=None):
        if counted is not None:
            s, tz, ty, source = s * counted, tz * counted, ty * counted, source * counted
        self.add_pairs(s, here)
        for key, value in here.items():
            self.add(("rhs", key), value * source)
        there = {}
        for key in {**here, **top}:
            there[key] = self.last_row(top[key], row_roll(here[key], -1) if key in here else 0.0)
        self.add_pairs(tz, minus(here, there))
        rolled = {key: lane_roll(value, -1) for key, value in here.items()}
        there = {}
        for node in {key[0]: None for key in here}:
            u, v = rolled.get((node, "u"), 0.0), rolled.get((node, "v"), 0.0)
            there[node, "u"] = jnp.where(self.m_r, v, u)
            there[node, "v"] = jnp.where(self.m_r, u, v)
        self.add_pairs(ty, minus(here, there))


def inner_keys():
    held = [("N", "u"), ("N", "v"), ("Z", "u"), ("Z", "v")]
    keys = [(a, b) for i, a in enumerate(held) for b in held[i:]]
    return keys + [("rhs", key) for key in held[:3]]


def assemble_inner(cls, well, src, z_b, z_a, rows, own, beside_y, beside_z):
    block = Block(z_b, z_a)
    tall = (NXL, NY)
    xrow = lax.broadcasted_iota(jnp.int32, tall, 0)
    r8, r9, s8 = resist(block.up(0)), resist(block.up(1)), sink(block.up(0), block.up(2))
    r7 = resist(cls[:, NZL - 1, :].astype(F32))
    left_mask = jnp.where(xrow == 0, 0.0, 1.0)
    o8, ey8, ez8, _, _ = block.top(r7, r8, r9, s8, row_roll(r8, 1), row_roll(r8, -1), left_mask, 1.0)
    tops = block.above(o8, ey8, ez8)
    last = NXL - 1
    rs = [resist(cls[x].astype(F32)) for x in range(NXL)]
    txs = [jnp.zeros(block.plane, F32)] + [2.0 / (rs[x] + rs[x + 1]) for x in range(last)]
    first = 1.0 - block.has_left
    before = None
    for x in range(last):
        s = sink(cls[x].astype(F32), well[x].astype(F32))
        below = resist(block.down(slice(x, x + 1)))
        o, ey, ez, _, tz, ty = block.basis(rs[x], s, txs[x], txs[x + 1], below, r8[x : x + 1])
        own[x] = o
        beside_y[x] = ey
        beside_z[x] = ez
        here = {("N", "u"): o, ("N", "v"): ey, ("Z", "u"): ez}
        top = {key: value[x : x + 1] for key, value in tops.items()}
        block.add_plane(here, top, s, tz, ty, src[x], first if x == 0 else None)
        if x:
            block.add_pairs(txs[x] * first if x == 1 else txs[x], minus(before, here))
        before = here
    for i, key in enumerate(inner_keys()):
        rows[i : i + 1, :] = jnp.sum(block.sums[key], axis=0, keepdims=True)


def assemble(cls, well, src, z_b, z_a, x_b, x_a, rows, own, beside_y, beside_z, part, edge, lanes_ref, g_ref, out_ref):
    block = Block(z_b, z_a)
    layer, odd_z, has_right, last_row = block.layer, block.odd_z, block.has_right, slice(NZL - 1, NZL)
    right = [jnp.where(block.odd_x, x_b[i], x_a[i]) for i in range(7)]
    left = jnp.where(block.odd_x, x_a[0], x_b[0])
    lines, lines_r = right[6], resist(right[6])

    tail = slice(8, NXL)
    up_c, up_c9, up_w = (block.up(i, tail) for i in range(3))
    up_r, up_r9 = resist(up_c), resist(up_c9)
    r8_14, r8_15, r8_16, r8_17, r9_16 = up_r[6:7], up_r[7:8], lines_r[2:3], lines_r[3:4], lines_r[4:5]
    c_last = cls[NXL - 1].astype(F32)
    r_last, s_last = resist(c_last), sink(c_last, well[NXL - 1].astype(F32))
    o, ey, ez, _, ex = block.top(
        r_last[last_row], r8_15, up_r9[7:8], sink(up_c[7:8], up_w[7:8]), r8_14, r8_16, 1.0, has_right
    )
    top_15 = block.above(o - ex, ey, ez, ex)
    rs = [r_last] + [resist(right[i]) for i in range(3)]
    o, ey, ez, ex, _ = block.top(
        rs[1][last_row], r8_16, r9_16, sink(lines[2:3], lines[5:6]), r8_15, r8_17, has_right, 1.0
    )
    top_16 = block.above(o - ex, ey, ez, ex, COLUMNS[::-1])

    r0 = resist(cls[0].astype(F32))
    t_left, t_right = 2.0 / (resist(left) + r0) * block.has_left, 2.0 / (r0 + resist(cls[1].astype(F32)))
    below = resist(block.down(slice(0, 8)))[0:1]
    over = resist(block.up(0, slice(0, 8)))[0:1]
    o, ey, ez, d, _, _ = block.basis(r0, sink(cls[0].astype(F32), well[0].astype(F32)), t_left, t_right, below, over)
    for i, value in enumerate((o - d * t_left, ey, ez, d * t_left)):
        edge[i] = value

    t_14 = 2.0 / (resist(cls[NXL - 2].astype(F32)) + r_last)
    txs = [t_14, 2.0 / (rs[0] + rs[1]) * has_right, 2.0 / (rs[1] + rs[2]), 2.0 / (rs[2] + rs[3])]
    ss = [s_last] + [sink(right[i], right[3 + i]) for i in range(2)]
    belows = [resist(block.down(tail))[7:8], lines_r[0:1], lines_r[1:2]]
    overs = [r8_15, r8_16, r8_17]
    planes, faces = [], []
    for i in range(3):
        o, ey, ez, d, tz, ty = block.basis(rs[i], ss[i], txs[i], txs[i + 1], belows[i], overs[i])
        (a, az), (b, _) = COLUMNS if i == 0 else COLUMNS[::-1]
        here = {(a, "v"): ey, (az, "u"): ez}
        if i < 2:
            here[b, "u"] = d * txs[1]
            o = o - here[b, "u"]
        if i == 0:
            for k, value in enumerate((o, ey, ez, here[b, "u"])):
                edge[4 + k] = value
        here[a, "u"] = o
        planes.append(here)
        faces.append((tz, ty))
    before = {("N", "u"): own[NXL - 2], ("N", "v"): beside_y[NXL - 2], ("Z", "u"): beside_z[NXL - 2]}
    block.add_pairs(t_14, minus(before, planes[0]))
    block.add_plane(planes[0], top_15, ss[0], *faces[0], src[NXL - 1])
    block.add_pairs(txs[1], minus(planes[0], planes[1]))
    block.add_plane(planes[1], top_16, ss[1], *faces[1], right[5], has_right)
    block.add_pairs(txs[2] * has_right, minus(planes[1], planes[2]))
    sums = block.sums

    index = {key: i for i, key in enumerate(sums)}
    for key, i in index.items():
        row = jnp.sum(sums[key], axis=0, keepdims=True)
        if key in inner_keys():
            inner = inner_keys().index(key)
            row = row + rows[inner : inner + 1, :]
        lanes_ref[i : i + 1, :] = row
    count = -(-len(index) // 8) * 8
    if count > len(index):
        lanes_ref[len(index) : count, :] = jnp.zeros((count - len(index), NY), F32)

    j = lax.broadcasted_iota(jnp.int32, (NY, 128), 0)
    n = lax.broadcasted_iota(jnp.int32, (NY, 128), 1)
    group, pos = n // NCY, j % EDGE
    taken = (group == 0) | ((group == 1) & (pos == 0)) | ((group == 2) & (pos >= EDGE - 2))
    select = ((j // EDGE == n % NCY) & taken).astype(F32)
    grouped = jnp.dot(lanes_ref[0:count, :], select, precision=lax.Precision.HIGHEST, preferred_element_type=F32)
    gl = lax.broadcasted_iota(jnp.int32, (count, 128), 1)
    g_l_next = jnp.where(gl < NCY - 1, lane_roll(grouped, -(NCY + 1)), 0.0)
    g_r_next = jnp.where((gl > 0) & (gl < NCY), lane_roll(grouped, -(2 * NCY - 1)), 0.0)
    forms = {
        "all": jnp.where(gl < NCY, grouped, 0.0),
        "L": jnp.where(gl < NCY, lane_roll(grouped, -NCY), 0.0),
        "R": jnp.where(gl < NCY, lane_roll(grouped, -2 * NCY), 0.0),
        "Ls": g_l_next,
        "Rs": g_r_next,
        "vv": g_l_next + g_r_next,
    }
    at = {}
    for i, (name, value) in enumerate(forms.items()):
        at[name] = i
        g_ref[i, 0:count, :] = value

    def taken_rows(terms):
        total = None
        for name, key in terms:
            if key in index:
                q = index[key]
                row = g_ref[at[name], q : q + 1, :]
                total = row if total is None else total + row
        return total

    def terms_of(a, b, dy):
        au, av, bu, bv = (a, "u"), (a, "v"), (b, "u"), (b, "v")
        if a == b:
            if dy == 0:
                return [("all", pair(au, au)), ("vv", pair(av, av))]
            return [("Ls", pair(au, av)), ("R", pair(au, av))]
        if dy == 0:
            return [("all", pair(au, bu)), ("vv", pair(av, bv))]
        if dy < 0:
            return [("L", pair(au, bv)), ("Rs", pair(av, bu))]
        return [("R", pair(au, bv)), ("Ls", pair(av, bu))]

    nothing = jnp.zeros((1, 128), F32)
    out_ref[...] = jnp.zeros(out_ref.shape, F32)
    spots = [(where, k) for where in ("own", "near", "low") for k in range(NCZ)]
    for (where, key), (r, k) in SLOT.items():
        names = {"own": HERE, "near": BESIDE}.get(where)
        if key[0] == "s":
            row = taken_rows(terms_of(names[key[1]], names[key[2]], key[3]))
        elif key[0] == "r":
            row = taken_rows([("all", ("rhs", (names[key[1]], "u"))), ("vv", ("rhs", (names[key[1]], "v")))])
        else:
            when_odd = taken_rows(terms_of(HERE[key[1]], BESIDE[key[2]], key[3]))
            when_even = taken_rows(terms_of(BESIDE[key[1]], HERE[key[2]], key[3]))
            when_odd = nothing if when_odd is None else when_odd
            when_even = nothing if when_even is None else when_even
            row = jnp.where(odd_z, when_odd, when_even)
        if row is not None:
            out_ref[spots.index((where, k)), r : r + 1, :] = row
    cell = layer // 2
    near_cell = jnp.where(odd_z, cell + 1, cell - 1)
    coarse_layer = {"own": cell, "near": near_cell, "low": jnp.minimum(cell, near_cell)}
    group = lax.broadcasted_iota(jnp.int32, (ROWS, 128), 1) // NCY
    total = jnp.zeros((ROWS, 128), F32)
    for i, (where, k) in enumerate(spots):
        if (where, k) not in {(w, kk) for (w, _), (_, kk) in SLOT.items()}:
            continue
        rows = out_ref[i]
        spread = rows
        for n in range(1, NCZ):
            spread = spread + lane_roll(rows, n * NCY)
        total = total + jnp.where(group == (coarse_layer[where] + k + NCZ) % NCZ, spread, 0.0)
    for k in range(TILES * LAYERS):
        part[k] = total


def solve(rows, own, beside_y, beside_z, edge, pressure):
    tile, layer = lax.axis_index("tile"), lax.axis_index("layer")
    odd_z = layer % 2 == 1
    cell = layer // 2
    near_cell = jnp.where(odd_z, cell + 1, cell - 1)
    shape = (TILES, 128)
    strip = lax.broadcasted_iota(jnp.int32, shape, 0)
    group = lax.broadcasted_iota(jnp.int32, shape, 1) // NCY
    lane_cell = group[0:1]

    loaded = {}

    def load(layer_from, row):
        if (layer_from, row) not in loaded:
            loaded[layer_from, row] = rows[pl.ds(layer_from * ROWS + row, TILES, stride=LAYERS * ROWS), :]
        return loaded[layer_from, row]

    by_shift = {}
    for (where, key), (row, k) in SLOT.items():
        total = None
        for l in range(LAYERS):
            z = cells_of(l)[where]
            if 0 <= z and max(cells_of(l)["own"], cells_of(l)["near"] if where != "own" else 0) < NCZ:
                term = jnp.where(group == (z + k) % NCZ, load(l, row), 0.0)
                total = term if total is None else total + term
        by_shift[key, k] = by_shift[key, k] + total if (key, k) in by_shift else total
    terms = {}
    for (key, k), value in by_shift.items():
        value = lane_roll(value, -k * NCY) if k else value
        terms[key] = terms[key] + value if key in terms else value

    def from_last(value):
        return jnp.where(strip > 0, row_roll(value, 1), 0.0)

    half = {}
    for dy in (0, 1):
        half[0, 0, dy] = terms["s", 0, 0, dy] + from_last(terms["s", 1, 1, dy])
    for dy in (-1, 0, 1):
        half[1, 0, dy] = terms["s", 0, 1, dy]
        half[0, 1, dy] = terms["z", 0, 0, dy] + from_last(terms["z", 1, 1, dy])
        half[1, 1, dy] = terms["z", 0, 1, dy]
        half[-1, 1, dy] = from_last(terms["z", 1, 0, dy])
    rhs = terms["r", 0] + from_last(terms["r", 1])
    centre = half.pop((0, 0, 0))
    scale = COARSE_DAMPING / centre

    def shifted(value, dx, dz, dy):
        by = -(dz * NCY + dy)
        if by:
            value = lane_roll(value, by)
        return row_roll(value, -dx) if dx else value

    full = dict(half)
    for (dx, dz, dy), value in half.items():
        full[-dx, -dz, -dy] = shifted(value, -dx, -dz, -dy)
    coarse = scale * rhs
    for _ in range(SWEEPS - 1):
        applied = centre * coarse
        for dz in (-1, 0, 1):
            for dy in (-1, 0, 1):
                moved = shifted(coarse, 0, dz, dy)
                for dx in (-1, 0, 1):
                    if (dx, dz, dy) in full:
                        applied = applied + full[dx, dz, dy] * shifted(moved, dx, 0, 0)
        coarse = coarse + scale * (rhs - applied)

    def strip_row(at):
        return jnp.sum(jnp.where(strip == at, coarse, 0.0), axis=0, keepdims=True)

    here = strip_row(tile)
    own_row = jnp.where(lane_cell == cell, here, 0.0)
    picked = [
        own_row,
        jnp.where(lane_cell == cell, strip_row(tile - 1), 0.0),
        jnp.where(lane_cell == cell, strip_row(tile + 1), 0.0),
        jnp.where(lane_cell == near_cell, here, 0.0),
        lane_roll(own_row, 1),
        lane_roll(own_row, -1),
        jnp.zeros((2, 128), F32),
    ]
    picked = jnp.concatenate(picked, axis=0)
    i = lax.broadcasted_iota(jnp.int32, (128, NY), 0)
    j = lax.broadcasted_iota(jnp.int32, (128, NY), 1)
    spread = (i % NCY == j // EDGE).astype(F32)
    fine = jnp.dot(picked, spread, precision=lax.Precision.HIGHEST, preferred_element_type=F32)
    lane = lax.broadcasted_iota(jnp.int32, (1, NY), 1) % EDGE
    near_y = jnp.where(lane == 0, fine[4:5], jnp.where(lane == EDGE - 1, fine[5:6], 0.0))
    for x in range(NXL):
        if x in (0, NXL - 1):
            first, row = (0, fine[1:2]) if x == 0 else (4, fine[2:3])
            value = edge[first] * fine[0:1] + edge[first + 1] * near_y + edge[first + 2] * fine[3:4] + edge[first + 3] * row
        else:
            value = own[x] * fine[0:1] + beside_y[x] * near_y + beside_z[x] * fine[3:4]
        pressure[x] = value


def struct(*shape):
    return jax.ShapeDtypeStruct(shape, F32)


def call(kernel, outs, scratch=(), **kw):
    many = isinstance(outs, (list, tuple))
    return pl.pallas_call(
        kernel,
        out_shape=outs,
        out_specs=[VMEM] * len(outs) if many else VMEM,
        scratch_shapes=list(scratch),
        compiler_params=pltpu.CompilerParams(vmem_limit_bytes=48 * 1024 * 1024),
        **kw,
    )


def body(classes, well_mask, source):
    def swap(values, axis, count):
        far = lax.ppermute(values[0], axis, swap_pairs(count, False))
        return far, lax.ppermute(values[1], axis, swap_pairs(count, True))

    block = struct(NXL, NZL, NY)
    ints = pltpu.VMEM((NXL, NZL, NY), jnp.int32)
    z_message, x_message = struct(3, NXL, NY), struct(7, NZL, NY)
    z_b, z_a, x_b, x_a = call(
        pack,
        [z_message, z_message, x_message, x_message],
        [ints, ints, pltpu.VMEM((NZL, NY), F32), pltpu.SemaphoreType.DMA((3,))],
        in_specs=[pl.BlockSpec(memory_space=pltpu.HBM)] * 3,
    )(*(pltpu.with_memory_space_constraint(v, pltpu.HBM) for v in (classes, well_mask, source)))
    z_b, z_a = swap((z_b, z_a), "layer", LAYERS)
    x_out = call(pack_lines, [x_message] * 2, in_specs=[VMEM] * 4)(x_b, x_a, z_b, z_a)
    x_b, x_a = swap(x_out, "tile", TILES)
    inner, own, beside_y, beside_z = call(
        assemble_inner,
        [struct(16, NY), block, block, block],
        in_specs=[VMEM] * 5,
        cost_estimate=pl.CostEstimate(flops=10**7, bytes_accessed=2 * 10**6, transcendentals=10**5),
    )(classes, well_mask, source, z_b, z_a)
    part, edge = call(
        assemble,
        [struct(TILES * LAYERS, ROWS, 128), struct(8, NZL, NY)],
        [pltpu.VMEM((64, NY), F32), pltpu.VMEM((6, 64, 128), F32), pltpu.VMEM((3 * NCZ, ROWS, 128), F32)],
        in_specs=[VMEM] * 11,
    )(classes, well_mask, source, z_b, z_a, x_b, x_a, inner, own, beside_y, beside_z)
    received = lax.all_to_all(part, ("tile", "layer"), 0, 0, tiled=True)
    rows = received.reshape(TILES * LAYERS * ROWS, 128)
    return call(solve, block, in_specs=[VMEM] * 5)(rows, own, beside_y, beside_z, edge)


def solution(mesh):
    spec = P("tile", "layer", None)
    return jax.shard_map(body, mesh=mesh, in_specs=(spec, spec, spec), out_specs=spec, check_vma=False)
```

```python
import functools

import jax
import jax.numpy as jnp
import numpy as np
from jax import lax
from jax.experimental import pallas as pl
from jax.experimental.pallas import tpu as pltpu
from jax.sharding import PartitionSpec as P

EDGE = 16
SWEEPS = 4
FINE_DAMPING = 0.67
COARSE_DAMPING = 0.5
NXL, NZL, NY = 16, 8, 512
TILES, LAYERS = 16, 8
NCY = NY // EDGE
NCZ = LAYERS * NZL // EDGE
ROWS = 8
F32 = jnp.float32
VMEM = pl.BlockSpec(memory_space=pltpu.VMEM)

NODES = ("N", "Q", "Z", "QZ")


def order(key):
    return NODES.index(key[0]) * 2 + (key[1] == "v")


def pair(a, b):
    return (a, b) if order(a) <= order(b) else (b, a)


SLOT = {}
for where, row in (("own", 0), ("near", 2)):
    for i, key in enumerate(
        [("s", 0, 0, 0), ("s", 0, 0, 1), ("s", 1, 1, 0), ("s", 1, 1, 1)]
        + [("s", 0, 1, -1), ("s", 0, 1, 0), ("s", 0, 1, 1), ("r", 0)]
    ):
        SLOT[where, key] = (row + i // 4, i % 4)
SLOT["own", ("r", 1)] = (7, 0)
SLOT["near", ("r", 1)] = (7, 2)
for i, (lo, hi, dy) in enumerate((lo, hi, dy) for lo in (0, 1) for hi in (0, 1) for dy in (-1, 0, 1)):
    SLOT["low", ("z", lo, hi, dy)] = (4 + i // 4, i % 4)
HERE = ("N", "Q")
BESIDE = ("Z", "QZ")


def cells_of(layer):
    own = layer // 2
    near = own + 1 if layer % 2 else own - 1
    return {"own": own, "near": near, "low": min(own, near)}


def swap_pairs(axis, first):
    pairs = []
    for tile in range(TILES):
        for layer in range(LAYERS):
            at, count = (tile, TILES) if axis == "tile" else (layer, LAYERS)
            if first:
                to = at ^ 1
            else:
                to = at if at in (0, count - 1) else ((at + 1) ^ 1) - 1
            partner = (to, layer) if axis == "tile" else (tile, to)
            if to == at:
                partner = (tile, layer ^ 1) if axis == "tile" else (tile ^ 1, layer)
            pairs.append((tile * LAYERS + layer, partner[0] * LAYERS + partner[1]))
    return pairs


def pack(cls_hbm, well_hbm, src_hbm, z_b, z_a, x_b, x_a, cls, well, src, sems):
    copies = [
        pltpu.make_async_copy(cls_hbm, cls, sems.at[0]),
        pltpu.make_async_copy(well_hbm, well, sems.at[1]),
        pltpu.make_async_copy(src_hbm.at[0], src, sems.at[2]),
    ]
    for copy in copies:
        copy.start()
    for copy in copies:
        copy.wait()

    def both(first, last, odd, b, a):
        a[0] = jnp.where(odd, first, last)
        b[0] = jnp.where(odd, last, first)

    odd_z = lax.axis_index("layer") % 2 == 1
    odd_x = lax.axis_index("tile") % 2 == 1
    both(cls[:, 0, :].astype(F32), cls[:, NZL - 1, :].astype(F32), odd_z, z_b, z_a)
    both(cls[0].astype(F32), cls[NXL - 1].astype(F32), odd_x, x_b, x_a)
    second = cls[:, 1, :].astype(F32)
    wells = well[:, 0, :].astype(F32)
    for out in (z_b, z_a):
        out[1] = second
        out[2] = wells
    for out in (x_b, x_a):
        out[1] = cls[1].astype(F32)
        out[2] = cls[2].astype(F32)
        out[3] = well[0].astype(F32)
        out[4] = well[1].astype(F32)
        out[5] = src[...]


def pack_lines(old_b, old_a, z_b, z_a, x_b, x_a):
    odd_z = lax.axis_index("layer") % 2 == 1

    def head(ref, plane):
        return ref[plane, 0:8, :]

    up = [jnp.where(odd_z, head(z_b, i), head(z_a, i)) for i in range(3)]
    down = jnp.where(odd_z, head(z_a, 0), head(z_b, 0))
    lines = [down[0:1], down[1:2], up[0][0:1], up[0][1:2], up[1][0:1], up[2][0:1], jnp.zeros((2, NY), F32)]
    lines = jnp.concatenate(lines, axis=0)
    for old, out in ((old_b, x_b), (old_a, x_a)):
        for i in range(6):
            out[i] = old[i]
        out[6] = lines


def lane_roll(value, by):
    return pltpu.roll(value, by % value.shape[-1], value.ndim - 1)


def row_roll(value, by):
    return pltpu.roll(value, by % value.shape[0], 0)


def resist(c):
    return jnp.exp(2.5 - c * F32(1.0 / 3.0))


def sink(c, w):
    return 0.5 * w * jnp.exp(c * F32(1.0 / 3.0) - 2.5)


def y_faces(r):
    ty = 2.0 / (r + lane_roll(r, -1))
    ty = jnp.where(lax.broadcasted_iota(jnp.int32, r.shape, 1) < NY - 1, ty, 0.0)
    return ty, lane_roll(ty, 1)


def y_part(d, ty, ty_lo):
    at = lax.broadcasted_iota(jnp.int32, d.shape, 1) % EDGE
    return d * jnp.where(at == 0, ty_lo, jnp.where(at == EDGE - 1, ty, 0.0))


def minus(a, b):
    out = {}
    for key in {**a, **b}:
        if key in a and key in b:
            out[key] = a[key] - b[key]
        else:
            out[key] = a[key] if key in a else -b[key]
    return out


COLUMNS = (("N", "Z"), ("Q", "QZ"))


class Block:
    def __init__(self, z_b, z_a):
        self.tile, self.layer = lax.axis_index("tile"), lax.axis_index("layer")
        self.odd_z, self.odd_x = self.layer % 2 == 1, self.tile % 2 == 1
        self.has_up, self.has_down = (self.layer < LAYERS - 1).astype(F32), (self.layer > 0).astype(F32)
        self.has_right, self.has_left = (self.tile < TILES - 1).astype(F32), (self.tile > 0).astype(F32)
        self.plane = (NZL, NY)
        self.zrow = lax.broadcasted_iota(jnp.int32, self.plane, 0)
        self.m_r = lax.broadcasted_iota(jnp.int32, self.plane, 1) % EDGE == EDGE - 1
        self.at_zb = self.zrow == jnp.where(self.odd_z, NZL - 1, 0)
        self.up_mask = jnp.where(self.zrow == NZL - 1, self.has_up, 1.0)
        self.down_mask = jnp.where(self.zrow == 0, self.has_down, 1.0)
        self.sums = {}
        self.z_b, self.z_a = z_b, z_a

    def up(self, i, rows=slice(None)):
        return jnp.where(self.odd_z, self.z_b[i, rows, :], self.z_a[i, rows, :])

    def down(self, rows=slice(None)):
        return jnp.where(self.odd_z, self.z_a[0, rows, :], self.z_b[0, rows, :])

    def last_row(self, row, value):
        return jnp.where(self.zrow == NZL - 1, jnp.broadcast_to(row, self.plane), value)

    def basis(self, r, s, tx_lo, tx_hi, below, over):
        r_up = self.last_row(over, row_roll(r, -1))
        r_dn = jnp.where(self.zrow == 0, jnp.broadcast_to(below, self.plane), row_roll(r, 1))
        tz_hi, tz_lo = 0.5 / (r + r_up) * self.up_mask, 0.5 / (r + r_dn) * self.down_mask
        ty, ty_lo = y_faces(r)
        d = FINE_DAMPING / (s + tx_lo + tx_hi + tz_hi + tz_lo + ty + ty_lo)
        ey = y_part(d, ty, ty_lo)
        ez = jnp.where(self.at_zb, d * jnp.where(self.odd_z, tz_hi, tz_lo), 0.0)
        return 1.0 - d * s - ey - ez, ey, ez, d, tz_hi, ty

    def top(self, r7, r8, r9, s8, r8_left, r8_right, keep_left, keep_right):
        tx_lo, tx_hi = 2.0 / (r8 + r8_left) * keep_left, 2.0 / (r8 + r8_right) * keep_right
        t78, t89 = 0.5 / (r7 + r8) * self.has_up, 0.5 / (r8 + r9)
        ty, ty_lo = y_faces(r8)
        d = FINE_DAMPING / (s8 + tx_lo + tx_hi + t78 + t89 + ty + ty_lo)
        ey, ez = y_part(d, ty, ty_lo), jnp.where(self.odd_z, d * t78, 0.0)
        return 1.0 - d * s8 - ey - ez, ey, ez, d * tx_lo, d * tx_hi

    def above(self, o, ey, ez, other=None, columns=COLUMNS):
        (a, az), (b, bz) = columns
        out = {
            (a, "u"): jnp.where(self.odd_z, ez, o),
            (a, "v"): jnp.where(self.odd_z, 0.0, ey),
            (az, "u"): jnp.where(self.odd_z, o, 0.0),
            (az, "v"): jnp.where(self.odd_z, ey, 0.0),
        }
        if other is not None:
            out[b, "u"] = jnp.where(self.odd_z, 0.0, other)
            out[bz, "u"] = jnp.where(self.odd_z, other, 0.0)
        return out

    def add(self, key, value):
        self.sums[key] = self.sums[key] + value if key in self.sums else value

    def add_pairs(self, weight, values):
        keys = sorted(values, key=order)
        for i, a in enumerate(keys):
            scaled = weight * values[a]
            for b in keys[i:]:
                self.add((a, b), scaled * values[b])

    def add_plane(self, here, top, s, tz, ty, source, counted=None):
        if counted is not None:
            s, tz, ty, source = s * counted, tz * counted, ty * counted, source * counted
        self.add_pairs(s, here)
        for key, value in here.items():
            self.add(("rhs", key), value * source)
        there = {}
        for key in {**here, **top}:
            there[key] = self.last_row(top[key], row_roll(here[key], -1) if key in here else 0.0)
        self.add_pairs(tz, minus(here, there))
        rolled = {key: lane_roll(value, -1) for key, value in here.items()}
        there = {}
        for node in {key[0]: None for key in here}:
            u, v = rolled.get((node, "u"), 0.0), rolled.get((node, "v"), 0.0)
            there[node, "u"] = jnp.where(self.m_r, v, u)
            there[node, "v"] = jnp.where(self.m_r, u, v)
        self.add_pairs(ty, minus(here, there))


def inner_keys():
    held = [("N", "u"), ("N", "v"), ("Z", "u"), ("Z", "v")]
    keys = [(a, b) for i, a in enumerate(held) for b in held[i:]]
    return keys + [("rhs", key) for key in held[:3]]


def assemble_inner(cls, well, src, z_b, z_a, rows, own, beside_y, beside_z):
    block = Block(z_b, z_a)
    tall = (NXL, NY)
    xrow = lax.broadcasted_iota(jnp.int32, tall, 0)
    r8, r9, s8 = resist(block.up(0)), resist(block.up(1)), sink(block.up(0), block.up(2))
    r7 = resist(cls[:, NZL - 1, :].astype(F32))
    left_mask = jnp.where(xrow == 0, 0.0, 1.0)
    o8, ey8, ez8, _, _ = block.top(r7, r8, r9, s8, row_roll(r8, 1), row_roll(r8, -1), left_mask, 1.0)
    tops = block.above(o8, ey8, ez8)
    last = NXL - 1
    rs = [resist(cls[x].astype(F32)) for x in range(NXL)]
    txs = [jnp.zeros(block.plane, F32)] + [2.0 / (rs[x] + rs[x + 1]) for x in range(last)]
    first = 1.0 - block.has_left
    before = None
    for x in range(last):
        s = sink(cls[x].astype(F32), well[x].astype(F32))
        below = resist(block.down(slice(x, x + 1)))
        o, ey, ez, _, tz, ty = block.basis(rs[x], s, txs[x], txs[x + 1], below, r8[x : x + 1])
        own[x] = o
        beside_y[x] = ey
        beside_z[x] = ez
        here = {("N", "u"): o, ("N", "v"): ey, ("Z", "u"): ez}
        top = {key: value[x : x + 1] for key, value in tops.items()}
        block.add_plane(here, top, s, tz, ty, src[x], first if x == 0 else None)
        if x:
            block.add_pairs(txs[x] * first if x == 1 else txs[x], minus(before, here))
        before = here
    for i, key in enumerate(inner_keys()):
        rows[i : i + 1, :] = jnp.sum(block.sums[key], axis=0, keepdims=True)


def assemble(cls, well, src, z_b, z_a, x_b, x_a, rows, own, beside_y, beside_z, part, edge, lanes_ref, g_ref, out_ref):
    block = Block(z_b, z_a)
    layer, odd_z, has_right, last_row = block.layer, block.odd_z, block.has_right, slice(NZL - 1, NZL)
    right = [jnp.where(block.odd_x, x_b[i], x_a[i]) for i in range(7)]
    left = jnp.where(block.odd_x, x_a[0], x_b[0])
    lines, lines_r = right[6], resist(right[6])

    tail = slice(8, NXL)
    up_c, up_c9, up_w = (block.up(i, tail) for i in range(3))
    up_r, up_r9 = resist(up_c), resist(up_c9)
    r8_14, r8_15, r8_16, r8_17, r9_16 = up_r[6:7], up_r[7:8], lines_r[2:3], lines_r[3:4], lines_r[4:5]
    c_last = cls[NXL - 1].astype(F32)
    r_last, s_last = resist(c_last), sink(c_last, well[NXL - 1].astype(F32))
    o, ey, ez, _, ex = block.top(
        r_last[last_row], r8_15, up_r9[7:8], sink(up_c[7:8], up_w[7:8]), r8_14, r8_16, 1.0, has_right
    )
    top_15 = block.above(o - ex, ey, ez, ex)
    rs = [r_last] + [resist(right[i]) for i in range(3)]
    o, ey, ez, ex, _ = block.top(
        rs[1][last_row], r8_16, r9_16, sink(lines[2:3], lines[5:6]), r8_15, r8_17, has_right, 1.0
    )
    top_16 = block.above(o - ex, ey, ez, ex, COLUMNS[::-1])

    r0 = resist(cls[0].astype(F32))
    t_left, t_right = 2.0 / (resist(left) + r0) * block.has_left, 2.0 / (r0 + resist(cls[1].astype(F32)))
    below = resist(block.down(slice(0, 8)))[0:1]
    over = resist(block.up(0, slice(0, 8)))[0:1]
    o, ey, ez, d, _, _ = block.basis(r0, sink(cls[0].astype(F32), well[0].astype(F32)), t_left, t_right, below, over)
    for i, value in enumerate((o - d * t_left, ey, ez, d * t_left)):
        edge[i] = value

    t_14 = 2.0 / (resist(cls[NXL - 2].astype(F32)) + r_last)
    txs = [t_14, 2.0 / (rs[0] + rs[1]) * has_right, 2.0 / (rs[1] + rs[2]), 2.0 / (rs[2] + rs[3])]
    ss = [s_last] + [sink(right[i], right[3 + i]) for i in range(2)]
    belows = [resist(block.down(tail))[7:8], lines_r[0:1], lines_r[1:2]]
    overs = [r8_15, r8_16, r8_17]
    planes, faces = [], []
    for i in range(3):
        o, ey, ez, d, tz, ty = block.basis(rs[i], ss[i], txs[i], txs[i + 1], belows[i], overs[i])
        (a, az), (b, _) = COLUMNS if i == 0 else COLUMNS[::-1]
        here = {(a, "v"): ey, (az, "u"): ez}
        if i < 2:
            here[b, "u"] = d * txs[1]
            o = o - here[b, "u"]
        if i == 0:
            for k, value in enumerate((o, ey, ez, here[b, "u"])):
                edge[4 + k] = value
        here[a, "u"] = o
        planes.append(here)
        faces.append((tz, ty))
    before = {("N", "u"): own[NXL - 2], ("N", "v"): beside_y[NXL - 2], ("Z", "u"): beside_z[NXL - 2]}
    block.add_pairs(t_14, minus(before, planes[0]))
    block.add_plane(planes[0], top_15, ss[0], *faces[0], src[NXL - 1])
    block.add_pairs(txs[1], minus(planes[0], planes[1]))
    block.add_plane(planes[1], top_16, ss[1], *faces[1], right[5], has_right)
    block.add_pairs(txs[2] * has_right, minus(planes[1], planes[2]))
    sums = block.sums

    index = {key: i for i, key in enumerate(sums)}
    for key, i in index.items():
        row = jnp.sum(sums[key], axis=0, keepdims=True)
        if key in inner_keys():
            inner = inner_keys().index(key)
            row = row + rows[inner : inner + 1, :]
        lanes_ref[i : i + 1, :] = row
    count = -(-len(index) // 8) * 8
    if count > len(index):
        lanes_ref[len(index) : count, :] = jnp.zeros((count - len(index), NY), F32)

    j = lax.broadcasted_iota(jnp.int32, (NY, 128), 0)
    n = lax.broadcasted_iota(jnp.int32, (NY, 128), 1)
    group, pos = n // NCY, j % EDGE
    taken = (group == 0) | ((group == 1) & (pos == 0)) | ((group == 2) & (pos >= EDGE - 2))
    select = ((j // EDGE == n % NCY) & taken).astype(F32)
    grouped = jnp.dot(lanes_ref[0:count, :], select, precision=lax.Precision.HIGHEST, preferred_element_type=F32)
    gl = lax.broadcasted_iota(jnp.int32, (count, 128), 1)
    g_l_next = jnp.where(gl < NCY - 1, lane_roll(grouped, -(NCY + 1)), 0.0)
    g_r_next = jnp.where((gl > 0) & (gl < NCY), lane_roll(grouped, -(2 * NCY - 1)), 0.0)
    forms = {
        "all": jnp.where(gl < NCY, grouped, 0.0),
        "L": jnp.where(gl < NCY, lane_roll(grouped, -NCY), 0.0),
        "R": jnp.where(gl < NCY, lane_roll(grouped, -2 * NCY), 0.0),
        "Ls": g_l_next,
        "Rs": g_r_next,
        "vv": g_l_next + g_r_next,
    }
    at = {}
    for i, (name, value) in enumerate(forms.items()):
        at[name] = i
        g_ref[i, 0:count, :] = value

    def taken_rows(terms):
        total = None
        for name, key in terms:
            if key in index:
                q = index[key]
                row = g_ref[at[name], q : q + 1, :]
                total = row if total is None else total + row
        return total

    def terms_of(a, b, dy):
        au, av, bu, bv = (a, "u"), (a, "v"), (b, "u"), (b, "v")
        if a == b:
            if dy == 0:
                return [("all", pair(au, au)), ("vv", pair(av, av))]
            return [("Ls", pair(au, av)), ("R", pair(au, av))]
        if dy == 0:
            return [("all", pair(au, bu)), ("vv", pair(av, bv))]
        if dy < 0:
            return [("L", pair(au, bv)), ("Rs", pair(av, bu))]
        return [("R", pair(au, bv)), ("Ls", pair(av, bu))]

    nothing = jnp.zeros((1, 128), F32)
    out_ref[...] = jnp.zeros(out_ref.shape, F32)
    spots = [(where, k) for where in ("own", "near", "low") for k in range(NCZ)]
    for (where, key), (r, k) in SLOT.items():
        names = {"own": HERE, "near": BESIDE}.get(where)
        if key[0] == "s":
            row = taken_rows(terms_of(names[key[1]], names[key[2]], key[3]))
        elif key[0] == "r":
            row = taken_rows([("all", ("rhs", (names[key[1]], "u"))), ("vv", ("rhs", (names[key[1]], "v")))])
        else:
            when_odd = taken_rows(terms_of(HERE[key[1]], BESIDE[key[2]], key[3]))
            when_even = taken_rows(terms_of(BESIDE[key[1]], HERE[key[2]], key[3]))
            when_odd = nothing if when_odd is None else when_odd
            when_even = nothing if when_even is None else when_even
            row = jnp.where(odd_z, when_odd, when_even)
        if row is not None:
            out_ref[spots.index((where, k)), r : r + 1, :] = row
    cell = layer // 2
    near_cell = jnp.where(odd_z, cell + 1, cell - 1)
    coarse_layer = {"own": cell, "near": near_cell, "low": jnp.minimum(cell, near_cell)}
    group = lax.broadcasted_iota(jnp.int32, (ROWS, 128), 1) // NCY
    total = jnp.zeros((ROWS, 128), F32)
    for i, (where, k) in enumerate(spots):
        if (where, k) not in {(w, kk) for (w, _), (_, kk) in SLOT.items()}:
            continue
        rows = out_ref[i]
        spread = rows
        for n in range(1, NCZ):
            spread = spread + lane_roll(rows, n * NCY)
        total = total + jnp.where(group == (coarse_layer[where] + k + NCZ) % NCZ, spread, 0.0)
    for k in range(TILES * LAYERS):
        part[k] = total


def solve(rows, own, beside_y, beside_z, edge, pressure):
    tile, layer = lax.axis_index("tile"), lax.axis_index("layer")
    odd_z = layer % 2 == 1
    cell = layer // 2
    near_cell = jnp.where(odd_z, cell + 1, cell - 1)
    shape = (TILES, 128)
    strip = lax.broadcasted_iota(jnp.int32, shape, 0)
    group = lax.broadcasted_iota(jnp.int32, shape, 1) // NCY
    lane_cell = group[0:1]

    loaded = {}

    def load(layer_from, row):
        if (layer_from, row) not in loaded:
            loaded[layer_from, row] = rows[pl.ds(layer_from * ROWS + row, TILES, stride=LAYERS * ROWS), :]
        return loaded[layer_from, row]

    by_shift = {}
    for (where, key), (row, k) in SLOT.items():
        total = None
        for l in range(LAYERS):
            z = cells_of(l)[where]
            if 0 <= z and max(cells_of(l)["own"], cells_of(l)["near"] if where != "own" else 0) < NCZ:
                term = jnp.where(group == (z + k) % NCZ, load(l, row), 0.0)
                total = term if total is None else total + term
        by_shift[key, k] = by_shift[key, k] + total if (key, k) in by_shift else total
    terms = {}
    for (key, k), value in by_shift.items():
        value = lane_roll(value, -k * NCY) if k else value
        terms[key] = terms[key] + value if key in terms else value

    def from_last(value):
        return jnp.where(strip > 0, row_roll(value, 1), 0.0)

    half = {}
    for dy in (0, 1):
        half[0, 0, dy] = terms["s", 0, 0, dy] + from_last(terms["s", 1, 1, dy])
    for dy in (-1, 0, 1):
        half[1, 0, dy] = terms["s", 0, 1, dy]
        half[0, 1, dy] = terms["z", 0, 0, dy] + from_last(terms["z", 1, 1, dy])
        half[1, 1, dy] = terms["z", 0, 1, dy]
        half[-1, 1, dy] = from_last(terms["z", 1, 0, dy])
    rhs = terms["r", 0] + from_last(terms["r", 1])
    centre = half.pop((0, 0, 0))
    scale = COARSE_DAMPING / centre

    def shifted(value, dx, dz, dy):
        by = -(dz * NCY + dy)
        if by:
            value = lane_roll(value, by)
        return row_roll(value, -dx) if dx else value

    full = dict(half)
    for (dx, dz, dy), value in half.items():
        full[-dx, -dz, -dy] = shifted(value, -dx, -dz, -dy)
    coarse = scale * rhs
    for _ in range(SWEEPS - 1):
        applied = centre * coarse
        for dz in (-1, 0, 1):
            for dy in (-1, 0, 1):
                moved = shifted(coarse, 0, dz, dy)
                for dx in (-1, 0, 1):
                    if (dx, dz, dy) in full:
                        applied = applied + full[dx, dz, dy] * shifted(moved, dx, 0, 0)
        coarse = coarse + scale * (rhs - applied)

    def strip_row(at):
        return jnp.sum(jnp.where(strip == at, coarse, 0.0), axis=0, keepdims=True)

    here = strip_row(tile)
    own_row = jnp.where(lane_cell == cell, here, 0.0)
    picked = [
        own_row,
        jnp.where(lane_cell == cell, strip_row(tile - 1), 0.0),
        jnp.where(lane_cell == cell, strip_row(tile + 1), 0.0),
        jnp.where(lane_cell == near_cell, here, 0.0),
        lane_roll(own_row, 1),
        lane_roll(own_row, -1),
        jnp.zeros((2, 128), F32),
    ]
    picked = jnp.concatenate(picked, axis=0)
    i = lax.broadcasted_iota(jnp.int32, (128, NY), 0)
    j = lax.broadcasted_iota(jnp.int32, (128, NY), 1)
    spread = (i % NCY == j // EDGE).astype(F32)
    fine = jnp.dot(picked, spread, precision=lax.Precision.HIGHEST, preferred_element_type=F32)
    lane = lax.broadcasted_iota(jnp.int32, (1, NY), 1) % EDGE
    near_y = jnp.where(lane == 0, fine[4:5], jnp.where(lane == EDGE - 1, fine[5:6], 0.0))
    for x in range(NXL):
        if x in (0, NXL - 1):
            first, row = (0, fine[1:2]) if x == 0 else (4, fine[2:3])
            value = edge[first] * fine[0:1] + edge[first + 1] * near_y + edge[first + 2] * fine[3:4] + edge[first + 3] * row
        else:
            value = own[x] * fine[0:1] + beside_y[x] * near_y + beside_z[x] * fine[3:4]
        pressure[x] = value


def struct(*shape):
    return jax.ShapeDtypeStruct(shape, F32)


def call(kernel, outs, scratch=(), **kw):
    many = isinstance(outs, (list, tuple))
    return pl.pallas_call(
        kernel,
        out_shape=outs,
        out_specs=[VMEM] * len(outs) if many else VMEM,
        scratch_shapes=list(scratch),
        compiler_params=pltpu.CompilerParams(vmem_limit_bytes=48 * 1024 * 1024),
        **kw,
    )


def body(classes, well_mask, source):
    def swap(values, axis):
        far = lax.ppermute(values[0], ("tile", "layer"), swap_pairs(axis, False))
        return far, lax.ppermute(values[1], ("tile", "layer"), swap_pairs(axis, True))

    block = struct(NXL, NZL, NY)
    ints = pltpu.VMEM((NXL, NZL, NY), jnp.int32)
    z_message, x_message = struct(3, NXL, NY), struct(7, NZL, NY)
    z_b, z_a, x_b, x_a = call(
        pack,
        [z_message, z_message, x_message, x_message],
        [ints, ints, pltpu.VMEM((NZL, NY), F32), pltpu.SemaphoreType.DMA((3,))],
        in_specs=[pl.BlockSpec(memory_space=pltpu.HBM)] * 3,
    )(*(pltpu.with_memory_space_constraint(v, pltpu.HBM) for v in (classes, well_mask, source)))
    z_b, z_a = swap((z_b, z_a), "layer")
    x_out = call(pack_lines, [x_message] * 2, in_specs=[VMEM] * 4)(x_b, x_a, z_b, z_a)
    x_b, x_a = swap(x_out, "tile")
    inner, own, beside_y, beside_z = call(
        assemble_inner,
        [struct(16, NY), block, block, block],
        in_specs=[VMEM] * 5,
        cost_estimate=pl.CostEstimate(flops=10**7, bytes_accessed=2 * 10**6, transcendentals=10**5),
    )(classes, well_mask, source, z_b, z_a)
    part, edge = call(
        assemble,
        [struct(TILES * LAYERS, ROWS, 128), struct(8, NZL, NY)],
        [pltpu.VMEM((64, NY), F32), pltpu.VMEM((6, 64, 128), F32), pltpu.VMEM((3 * NCZ, ROWS, 128), F32)],
        in_specs=[VMEM] * 11,
    )(classes, well_mask, source, z_b, z_a, x_b, x_a, inner, own, beside_y, beside_z)
    received = lax.all_to_all(part, ("tile", "layer"), 0, 0, tiled=True)
    rows = received.reshape(TILES * LAYERS * ROWS, 128)
    return call(solve, block, in_specs=[VMEM] * 5)(rows, own, beside_y, beside_z, edge)


def solution(mesh):
    spec = P("tile", "layer", None)
    return jax.shard_map(body, mesh=mesh, in_specs=(spec, spec, spec), out_specs=spec, check_vma=False)
```

```python
import functools

import jax
import jax.numpy as jnp
import numpy as np
from jax import lax
from jax.experimental import pallas as pl
from jax.experimental.pallas import tpu as pltpu
from jax.sharding import PartitionSpec as P

EDGE = 16
SWEEPS = 4
FINE_DAMPING = 0.67
COARSE_DAMPING = 0.5
NXL, NZL, NY = 16, 8, 512
TILES, LAYERS = 16, 8
NCY = NY // EDGE
NCZ = LAYERS * NZL // EDGE
ROWS = 8
F32 = jnp.float32
VMEM = pl.BlockSpec(memory_space=pltpu.VMEM)

NODES = ("N", "Q", "Z", "QZ")


def order(key):
    return NODES.index(key[0]) * 2 + (key[1] == "v")


def pair(a, b):
    return (a, b) if order(a) <= order(b) else (b, a)


SLOT = {}
for where, row in (("own", 0), ("near", 2)):
    for i, key in enumerate(
        [("s", 0, 0, 0), ("s", 0, 0, 1), ("s", 1, 1, 0), ("s", 1, 1, 1)]
        + [("s", 0, 1, -1), ("s", 0, 1, 0), ("s", 0, 1, 1), ("r", 0)]
    ):
        SLOT[where, key] = (row + i // 4, i % 4)
SLOT["own", ("r", 1)] = (7, 0)
SLOT["own", ("r", -1)] = (7, 1)
for i, (lo, hi, dy) in enumerate((lo, hi, dy) for lo in (0, 1) for hi in (0, 1) for dy in (-1, 0, 1)):
    SLOT["low", ("z", lo, hi, dy)] = (4 + i // 4, i % 4)
HERE = ("N", "Q")
BESIDE = ("Z", "QZ")


def cells_of(layer):
    own = layer // 2
    near = own + 1 if layer % 2 else own - 1
    return {"own": own, "near": near, "low": min(own, near)}


def swap_pairs(axis, first):
    pairs = []
    for tile in range(TILES):
        for layer in range(LAYERS):
            at, count = (tile, TILES) if axis == "tile" else (layer, LAYERS)
            if first:
                to = at ^ 1
            else:
                to = at if at in (0, count - 1) else ((at + 1) ^ 1) - 1
            partner = (to, layer) if axis == "tile" else (tile, to)
            if to == at:
                partner = (tile, layer ^ 1) if axis == "tile" else (tile ^ 1, layer)
            pairs.append((tile * LAYERS + layer, partner[0] * LAYERS + partner[1]))
    return pairs


def pack(cls_hbm, well_hbm, z_b, z_a, x_b, x_a, cls, well, sems):
    copies = [pltpu.make_async_copy(cls_hbm, cls, sems.at[0]), pltpu.make_async_copy(well_hbm, well, sems.at[1])]
    for copy in copies:
        copy.start()
    for copy in copies:
        copy.wait()

    def both(first, last, odd, b, a):
        a[0] = jnp.where(odd, first, last)
        b[0] = jnp.where(odd, last, first)

    odd_z = lax.axis_index("layer") % 2 == 1
    odd_x = lax.axis_index("tile") % 2 == 1
    both(cls[:, 0, :].astype(F32), cls[:, NZL - 1, :].astype(F32), odd_z, z_b, z_a)
    both(cls[0].astype(F32), cls[NXL - 1].astype(F32), odd_x, x_b, x_a)
    second = cls[:, 1, :].astype(F32)
    wells = well[:, 0, :].astype(F32)
    for out in (z_b, z_a):
        out[1] = second
        out[2] = wells
    for out in (x_b, x_a):
        out[1] = cls[1].astype(F32)
        out[2] = cls[2].astype(F32)
        out[3] = well[0].astype(F32)
        out[4] = well[1].astype(F32)


def pack_lines(old_b, old_a, z_b, z_a, x_b, x_a):
    odd_z = lax.axis_index("layer") % 2 == 1

    def head(ref, plane):
        return ref[plane, 0:8, :]

    up = [jnp.where(odd_z, head(z_b, i), head(z_a, i)) for i in range(3)]
    down = jnp.where(odd_z, head(z_a, 0), head(z_b, 0))
    lines = [down[0:1], down[1:2], up[0][0:1], up[0][1:2], up[1][0:1], up[2][0:1], jnp.zeros((2, NY), F32)]
    lines = jnp.concatenate(lines, axis=0)
    for old, out in ((old_b, x_b), (old_a, x_a)):
        for i in range(5):
            out[i] = old[i]
        out[5] = lines


def lane_roll(value, by):
    return pltpu.roll(value, by % value.shape[-1], value.ndim - 1)


def row_roll(value, by):
    return pltpu.roll(value, by % value.shape[0], 0)


def resist(c):
    return jnp.exp(2.5 - c * F32(1.0 / 3.0))


def sink(c, w):
    return 0.5 * w * jnp.exp(c * F32(1.0 / 3.0) - 2.5)


def y_faces(r):
    ty = 2.0 / (r + lane_roll(r, -1))
    ty = jnp.where(lax.broadcasted_iota(jnp.int32, r.shape, 1) < NY - 1, ty, 0.0)
    return ty, lane_roll(ty, 1)


def y_part(ty, ty_lo):
    at = lax.broadcasted_iota(jnp.int32, ty.shape, 1) % EDGE
    return jnp.where(at == 0, ty_lo, jnp.where(at == EDGE - 1, ty, 0.0))


def basis(s, others, leave_y, leave_z, tx_lo, tx_hi):
    d = FINE_DAMPING / (s + others + tx_lo + tx_hi)
    ey, ez = d * leave_y, d * leave_z
    return 1.0 - d * s - ey - ez, ey, ez, d


def three(value):
    pieces = []
    for _ in range(3):
        piece = value.astype(jnp.bfloat16)
        pieces.append(piece)
        value = value - piece.astype(F32)
    return jnp.concatenate(pieces, axis=0)


def times_01(value, matrix):
    n = value.shape[0]
    out = jnp.dot(three(value), matrix, preferred_element_type=F32)
    return out[0:n] + (out[n : 2 * n] + out[2 * n : 3 * n])


def row_sums(arrays):
    row = lax.broadcasted_iota(jnp.int32, arrays[0].shape, 0)
    arrays = list(arrays) + [jnp.zeros(arrays[0].shape, F32)] * (8 - len(arrays))
    arrays = [arrays[i] for i in (0, 4, 2, 6, 1, 5, 3, 7)]
    for bit in (4, 2, 1):
        low = row // bit % 2 == 0
        merged = []
        for a, b in zip(arrays[::2], arrays[1::2]):
            keep, move = jnp.where(low, a, b), jnp.where(low, b, a)
            moved = row_roll(move, 4) if bit == 4 else jnp.where(low, row_roll(move, -bit), row_roll(move, bit))
            merged.append(keep + moved)
        arrays = merged
    return arrays[0]


def total_of(values):
    values = list(values)
    while len(values) > 1:
        values = [a + b for a, b in zip(values[::2], values[1::2])] + ([values[-1]] if len(values) % 2 else [])
    return values[0]


def minus(a, b):
    out = {}
    for key in {**a, **b}:
        if key in a and key in b:
            out[key] = a[key] - b[key]
        else:
            out[key] = a[key] if key in a else -b[key]
    return out


COLUMNS = (("N", "Z"), ("Q", "QZ"))


class Block:
    def __init__(self, z_b, z_a):
        self.tile, self.layer = lax.axis_index("tile"), lax.axis_index("layer")
        self.odd_z, self.odd_x = self.layer % 2 == 1, self.tile % 2 == 1
        self.has_up, self.has_down = (self.layer < LAYERS - 1).astype(F32), (self.layer > 0).astype(F32)
        self.has_right, self.has_left = (self.tile < TILES - 1).astype(F32), (self.tile > 0).astype(F32)
        self.plane = (NZL, NY)
        self.zrow = lax.broadcasted_iota(jnp.int32, self.plane, 0)
        self.m_r = lax.broadcasted_iota(jnp.int32, self.plane, 1) % EDGE == EDGE - 1
        self.at_zb = self.zrow == jnp.where(self.odd_z, NZL - 1, 0)
        self.up_mask = jnp.where(self.zrow == NZL - 1, self.has_up, 1.0)
        self.down_mask = jnp.where(self.zrow == 0, self.has_down, 1.0)
        self.sums = {}
        self.z_b, self.z_a = z_b, z_a

    def up(self, i, rows=slice(None)):
        return jnp.where(self.odd_z, self.z_b[i, rows, :], self.z_a[i, rows, :])

    def down(self, rows=slice(None)):
        return jnp.where(self.odd_z, self.z_a[0, rows, :], self.z_b[0, rows, :])

    def last_row(self, row, value):
        return jnp.where(self.zrow == NZL - 1, jnp.broadcast_to(row, self.plane), value)

    def known(self, r, below, over):
        r_up = self.last_row(over, row_roll(r, -1))
        r_dn = jnp.where(self.zrow == 0, jnp.broadcast_to(below, self.plane), row_roll(r, 1))
        tz_hi, tz_lo = 0.5 / (r + r_up) * self.up_mask, 0.5 / (r + r_dn) * self.down_mask
        ty, ty_lo = y_faces(r)
        leave_z = jnp.where(self.at_zb, jnp.where(self.odd_z, tz_hi, tz_lo), 0.0)
        return tz_hi, ty, tz_hi + tz_lo + ty + ty_lo, y_part(ty, ty_lo), leave_z

    def top(self, r7, r8, r9):
        t78, t89 = 0.5 / (r7 + r8) * self.has_up, 0.5 / (r8 + r9)
        ty, ty_lo = y_faces(r8)
        return t78 + t89 + ty + ty_lo, y_part(ty, ty_lo), jnp.where(self.odd_z, t78, 0.0)

    def above(self, o, ey, ez, other=None, columns=COLUMNS):
        (a, az), (b, bz) = columns
        out = {
            (a, "u"): jnp.where(self.odd_z, ez, o),
            (a, "v"): jnp.where(self.odd_z, 0.0, ey),
            (az, "u"): jnp.where(self.odd_z, o, 0.0),
            (az, "v"): jnp.where(self.odd_z, ey, 0.0),
        }
        if other is not None:
            out[b, "u"] = jnp.where(self.odd_z, 0.0, other)
            out[bz, "u"] = jnp.where(self.odd_z, other, 0.0)
        return out

    def add(self, key, value):
        self.sums[key] = self.sums[key] + value if key in self.sums else value

    def add_pairs(self, weight, values):
        keys = sorted(values, key=order)
        for i, a in enumerate(keys):
            scaled = weight * values[a]
            for b in keys[i:]:
                self.add((a, b), scaled * values[b])

    def add_source(self, here, source):
        for key, value in here.items():
            self.add(("rhs", key), value * source)

    def add_plane(self, here, top, s, tz, ty, counted=None):
        if counted is not None:
            s, tz, ty = s * counted, tz * counted, ty * counted
        self.add_pairs(s, here)
        there = {}
        for key in {**here, **top}:
            there[key] = self.last_row(top[key], row_roll(here[key], -1) if key in here else 0.0)
        self.add_pairs(tz, minus(here, there))
        rolled = {key: lane_roll(value, -1) for key, value in here.items()}
        there = {}
        for node in {key[0]: None for key in here}:
            u, v = rolled.get((node, "u"), 0.0), rolled.get((node, "v"), 0.0)
            there[node, "u"] = jnp.where(self.m_r, v, u)
            there[node, "v"] = jnp.where(self.m_r, u, v)
        self.add_pairs(ty, minus(here, there))


def inner_keys():
    held = [("N", "u"), ("N", "v"), ("Z", "u"), ("Z", "v")]
    keys = [(a, b) for i, a in enumerate(held) for b in held[i:]]
    return keys + [("rhs", key) for key in held[:3]]


def assemble_inner(cls, well, src, z_b, z_a, rows, own, beside_y, beside_z, aux, aux_rows, select, spread):
    block = Block(z_b, z_a)
    tall = (NXL, NY)
    xrow = lax.broadcasted_iota(jnp.int32, tall, 0)
    last = NXL - 1
    r8, r9, s8 = resist(block.up(0)), resist(block.up(1)), sink(block.up(0), block.up(2))
    r7 = resist(cls[:, NZL - 1, :].astype(F32))
    others8, leave_y8, leave_z8 = block.top(r7, r8, r9)
    tx8_lo = 2.0 / (r8 + row_roll(r8, 1)) * jnp.where(xrow == 0, 0.0, 1.0)
    o8, ey8, ez8, _ = basis(s8, others8, leave_y8, leave_z8, tx8_lo, 2.0 / (r8 + row_roll(r8, -1)))
    tops = block.above(o8, ey8, ez8)
    for i, value in enumerate((s8, others8 + tx8_lo, leave_y8, leave_z8, r8)):
        aux_rows[i : i + 1, :] = value[last:NXL]
    aux_rows[5:8, :] = jnp.zeros((3, NY), F32)
    rs = [resist(cls[x].astype(F32)) for x in range(NXL)]
    txs = [jnp.zeros(block.plane, F32)] + [2.0 / (rs[x] + rs[x + 1]) for x in range(last)]
    first = 1.0 - block.has_left
    before = None
    for x in range(NXL):
        s = sink(cls[x].astype(F32), well[x].astype(F32))
        below = resist(block.down(slice(x, x + 1)))
        tz, ty, others, leave_y, leave_z = block.known(rs[x], below, r8[x : x + 1])
        if x == 0:
            for i, value in enumerate((s, others + txs[1], leave_y, leave_z, rs[x])):
                aux[i] = value
        if x == last:
            for i, value in enumerate((s, others + txs[last], leave_y, leave_z, rs[x], tz, ty, txs[last])):
                aux[5 + i] = value
            break
        o, ey, ez, _ = basis(s, others, leave_y, leave_z, txs[x], txs[x + 1])
        own[x] = o
        beside_y[x] = ey
        beside_z[x] = ez
        here = {("N", "u"): o, ("N", "v"): ey, ("Z", "u"): ez}
        top = {key: value[x : x + 1] for key, value in tops.items()}
        block.add_plane(here, top, s, tz, ty, first if x == 0 else None)
        if x:
            block.add_source(here, src[x])
            block.add_pairs(txs[x] * first if x == 1 else txs[x], minus(before, here))
        before = here
    keys = inner_keys()
    for i in range(0, len(keys), 8):
        rows[i : i + 8, :] = row_sums([block.sums[key] for key in keys[i : i + 8]])

    j = lax.broadcasted_iota(jnp.int32, (NY, 128), 0)
    n = lax.broadcasted_iota(jnp.int32, (NY, 128), 1)
    group, pos = n // NCY, j % EDGE
    taken = (group == 0) | ((group == 1) & (pos == 0)) | ((group == 2) & (pos >= EDGE - 2))
    select[...] = jnp.where((j // EDGE == n % NCY) & taken, 1.0, 0.0).astype(jnp.bfloat16)
    i = lax.broadcasted_iota(jnp.int32, (128, NY), 0)
    j = lax.broadcasted_iota(jnp.int32, (128, NY), 1)
    spread[...] = jnp.where(i % NCY == j // EDGE, 1.0, 0.0).astype(jnp.bfloat16)


def assemble(
    src, z_b, z_a, x_b, x_a, rows, own, beside_y, beside_z, aux, aux_rows, select, part, edge, lanes_ref, g_ref, out_ref
):
    block = Block(z_b, z_a)
    layer, odd_z, has_right, last_row = block.layer, block.odd_z, block.has_right, slice(NZL - 1, NZL)
    right = [jnp.where(block.odd_x, x_b[i], x_a[i]) for i in range(6)]
    left = jnp.where(block.odd_x, x_a[0], x_b[0])
    lines, lines_r = right[5], resist(right[5])

    r8_15, r8_16, r8_17, r9_16 = aux_rows[4:5], lines_r[2:3], lines_r[3:4], lines_r[4:5]
    tx = 2.0 / (r8_15 + r8_16) * has_right
    o, ey, ez, d = basis(*(aux_rows[i : i + 1] for i in range(4)), 0.0, tx)
    top_15 = block.above(o - d * tx, ey, ez, d * tx)
    rs = [aux[9]] + [resist(right[i]) for i in range(3)]
    o, ey, ez, d = basis(
        sink(lines[2:3], lines[5:6]), *block.top(rs[1][last_row], r8_16, r9_16), tx, 2.0 / (r8_16 + r8_17)
    )
    top_16 = block.above(o - d * tx, ey, ez, d * tx, COLUMNS[::-1])

    t_left = 2.0 / (resist(left) + aux[4]) * block.has_left
    o, ey, ez, d = basis(*(aux[i] for i in range(4)), t_left, 0.0)
    o, ex = o - d * t_left, d * t_left
    for i, value in enumerate((o, ey, ez, ex)):
        edge[i] = value
    block.add_source({("N", "u"): o, ("N", "v"): ey, ("Z", "u"): ez, ("M", "u"): ex}, src[0])

    t_14 = aux[12]
    txs = [0.0, 2.0 / (rs[0] + rs[1]) * has_right, 2.0 / (rs[1] + rs[2]), 2.0 / (rs[2] + rs[3])]
    known = [(aux[10], aux[11], aux[6], aux[7], aux[8])]
    known += [block.known(rs[i], lines_r[i - 1 : i], (r8_16, r8_17)[i - 1]) for i in (1, 2)]
    ss = [aux[5]] + [sink(right[i], right[3 + i]) for i in range(2)]
    planes = []
    for i in range(3):
        o, ey, ez, d = basis(ss[i], *known[i][2:], txs[i], txs[i + 1])
        (a, az), (b, _) = COLUMNS if i == 0 else COLUMNS[::-1]
        here = {(a, "v"): ey, (az, "u"): ez}
        if i < 2:
            here[b, "u"] = d * txs[1]
            o = o - here[b, "u"]
        if i == 0:
            for k, value in enumerate((o, ey, ez, here[b, "u"])):
                edge[4 + k] = value
        here[a, "u"] = o
        planes.append(here)
    before = {("N", "u"): own[NXL - 2], ("N", "v"): beside_y[NXL - 2], ("Z", "u"): beside_z[NXL - 2]}
    block.add_pairs(t_14, minus(before, planes[0]))
    block.add_plane(planes[0], top_15, ss[0], *known[0][:2])
    block.add_source(planes[0], src[NXL - 1])
    block.add_pairs(txs[1], minus(planes[0], planes[1]))
    block.add_plane(planes[1], top_16, ss[1], *known[1][:2], has_right)
    block.add_pairs(txs[2] * has_right, minus(planes[1], planes[2]))
    sums = block.sums

    keys = inner_keys() + [key for key in sums if key not in inner_keys()]
    index = {key: i for i, key in enumerate(keys)}
    count = -(-len(keys) // 16) * 16
    for i in range(0, count, 8):
        here = [sums[key] for key in keys[i : i + 8]]
        value = row_sums(here) if here else jnp.zeros((8, NY), F32)
        lanes_ref[i : i + 8, :] = value + rows[i : i + 8, :] if i < 16 else value
    grouped = times_01(lanes_ref[0:count, :], select[...])
    gl = lax.broadcasted_iota(jnp.int32, (count, 128), 1)
    g_l_next = jnp.where(gl < NCY - 1, lane_roll(grouped, -(NCY + 1)), 0.0)
    g_r_next = jnp.where((gl > 0) & (gl < NCY), lane_roll(grouped, -(2 * NCY - 1)), 0.0)
    forms = {
        "all": jnp.where(gl < NCY, grouped, 0.0),
        "L": jnp.where(gl < NCY, lane_roll(grouped, -NCY), 0.0),
        "R": jnp.where(gl < NCY, lane_roll(grouped, -2 * NCY), 0.0),
        "Ls": g_l_next,
        "Rs": g_r_next,
        "vv": g_l_next + g_r_next,
    }
    at = {}
    for i, (name, value) in enumerate(forms.items()):
        at[name] = i
        g_ref[i, 0:count, :] = value

    def taken_rows(terms):
        total = None
        for name, key in terms:
            if key in index:
                q = index[key]
                row = g_ref[at[name], q : q + 1, :]
                total = row if total is None else total + row
        return total

    def terms_of(a, b, dy):
        au, av, bu, bv = (a, "u"), (a, "v"), (b, "u"), (b, "v")
        if a == b:
            if dy == 0:
                return [("all", pair(au, au)), ("vv", pair(av, av))]
            return [("Ls", pair(au, av)), ("R", pair(au, av))]
        if dy == 0:
            return [("all", pair(au, bu)), ("vv", pair(av, bv))]
        if dy < 0:
            return [("L", pair(au, bv)), ("Rs", pair(av, bu))]
        return [("R", pair(au, bv)), ("Ls", pair(av, bu))]

    nothing = jnp.zeros((1, 128), F32)
    out_ref[...] = jnp.zeros(out_ref.shape, F32)
    spots = [(where, k) for where in ("own", "near", "low") for k in range(NCZ)]
    for (where, key), (r, k) in SLOT.items():
        names = {"own": HERE, "near": BESIDE}.get(where)
        if key[0] == "s":
            row = taken_rows(terms_of(names[key[1]], names[key[2]], key[3]))
        elif key[0] == "r":
            node = "M" if key[1] < 0 else names[key[1]]
            row = taken_rows([("all", ("rhs", (node, "u"))), ("vv", ("rhs", (node, "v")))])
        else:
            when_odd = taken_rows(terms_of(HERE[key[1]], BESIDE[key[2]], key[3]))
            when_even = taken_rows(terms_of(BESIDE[key[1]], HERE[key[2]], key[3]))
            when_odd = nothing if when_odd is None else when_odd
            when_even = nothing if when_even is None else when_even
            row = jnp.where(odd_z, when_odd, when_even)
        if row is not None:
            out_ref[spots.index((where, k)), r : r + 1, :] = row
    cell = layer // 2
    near_cell = jnp.where(odd_z, cell + 1, cell - 1)
    coarse_layer = {"own": cell, "near": near_cell, "low": jnp.minimum(cell, near_cell)}
    group = lax.broadcasted_iota(jnp.int32, (ROWS, 128), 1) // NCY
    total = jnp.zeros((ROWS, 128), F32)
    for i, (where, k) in enumerate(spots):
        if (where, k) not in {(w, kk) for (w, _), (_, kk) in SLOT.items()}:
            continue
        rows = out_ref[i]
        spread = rows
        for n in range(1, NCZ):
            spread = spread + lane_roll(rows, n * NCY)
        total = total + jnp.where(group == (coarse_layer[where] + k + NCZ) % NCZ, spread, 0.0)
    for k in range(TILES * LAYERS):
        part[k] = total


def solve(rows, own, beside_y, beside_z, edge, spread, pressure):
    tile, layer = lax.axis_index("tile"), lax.axis_index("layer")
    odd_z = layer % 2 == 1
    cell = layer // 2
    near_cell = jnp.where(odd_z, cell + 1, cell - 1)
    shape = (TILES, 128)
    strip = lax.broadcasted_iota(jnp.int32, shape, 0)
    group = lax.broadcasted_iota(jnp.int32, shape, 1) // NCY
    lane_cell = group[0:1]

    loaded = {}

    def load(layer_from, row):
        if (layer_from, row) not in loaded:
            loaded[layer_from, row] = rows[pl.ds(layer_from * ROWS + row, TILES, stride=LAYERS * ROWS), :]
        return loaded[layer_from, row]

    by_shift = {}
    for (where, key), (row, k) in SLOT.items():
        found = []
        for l in range(LAYERS):
            z = cells_of(l)[where]
            if 0 <= z and max(cells_of(l)["own"], cells_of(l)["near"] if where != "own" else 0) < NCZ:
                found.append(jnp.where(group == (z + k) % NCZ, load(l, row), 0.0))
        total = total_of(found)
        by_shift[key, k] = by_shift[key, k] + total if (key, k) in by_shift else total
    terms = {}
    for (key, k), value in by_shift.items():
        value = lane_roll(value, -k * NCY) if k else value
        terms[key] = terms[key] + value if key in terms else value

    def from_last(value):
        return jnp.where(strip > 0, row_roll(value, 1), 0.0)

    half = {}
    for dy in (0, 1):
        half[0, 0, dy] = terms["s", 0, 0, dy] + from_last(terms["s", 1, 1, dy])
    for dy in (-1, 0, 1):
        half[1, 0, dy] = terms["s", 0, 1, dy]
        half[0, 1, dy] = terms["z", 0, 0, dy] + from_last(terms["z", 1, 1, dy])
        half[1, 1, dy] = terms["z", 0, 1, dy]
        half[-1, 1, dy] = from_last(terms["z", 1, 0, dy])
    back = jnp.where(strip < TILES - 1, row_roll(terms["r", -1], -1), 0.0)
    rhs = terms["r", 0] + from_last(terms["r", 1]) + back
    centre = half.pop((0, 0, 0))
    scale = COARSE_DAMPING / centre

    def shifted(value, dx, dz, dy):
        by = -(dz * NCY + dy)
        if by:
            value = lane_roll(value, by)
        return row_roll(value, -dx) if dx else value

    full = dict(half)
    for (dx, dz, dy), value in half.items():
        full[-dx, -dz, -dy] = shifted(value, -dx, -dz, -dy)
    coarse = scale * rhs
    for _ in range(SWEEPS - 1):
        applied = [centre * coarse]
        for dz in (-1, 0, 1):
            for dy in (-1, 0, 1):
                moved = shifted(coarse, 0, dz, dy)
                for dx in (-1, 0, 1):
                    if (dx, dz, dy) in full:
                        applied.append(full[dx, dz, dy] * shifted(moved, dx, 0, 0))
        coarse = coarse + scale * (rhs - total_of(applied))

    def strip_row(at):
        return jnp.sum(jnp.where(strip == at, coarse, 0.0), axis=0, keepdims=True)

    here = strip_row(tile)
    own_row = jnp.where(lane_cell == cell, here, 0.0)
    picked = [
        own_row,
        jnp.where(lane_cell == cell, strip_row(tile - 1), 0.0),
        jnp.where(lane_cell == cell, strip_row(tile + 1), 0.0),
        jnp.where(lane_cell == near_cell, here, 0.0),
        lane_roll(own_row, 1),
        lane_roll(own_row, -1),
        jnp.zeros((2, 128), F32),
    ]
    picked = jnp.concatenate(picked, axis=0)
    fine = times_01(picked, spread[...])
    lane = lax.broadcasted_iota(jnp.int32, (1, NY), 1) % EDGE
    near_y = jnp.where(lane == 0, fine[4:5], jnp.where(lane == EDGE - 1, fine[5:6], 0.0))
    for x in range(NXL):
        if x in (0, NXL - 1):
            first, row = (0, fine[1:2]) if x == 0 else (4, fine[2:3])
            value = edge[first] * fine[0:1] + edge[first + 1] * near_y + edge[first + 2] * fine[3:4] + edge[first + 3] * row
        else:
            value = own[x] * fine[0:1] + beside_y[x] * near_y + beside_z[x] * fine[3:4]
        pressure[x] = value


def struct(*shape):
    return jax.ShapeDtypeStruct(shape, F32)


def call(kernel, outs, scratch=(), **kw):
    many = isinstance(outs, (list, tuple))
    return pl.pallas_call(
        kernel,
        out_shape=outs,
        out_specs=[VMEM] * len(outs) if many else VMEM,
        scratch_shapes=list(scratch),
        compiler_params=pltpu.CompilerParams(vmem_limit_bytes=48 * 1024 * 1024),
        **kw,
    )


def body(classes, well_mask, source):
    def swap(values, axis):
        far = lax.ppermute(values[0], ("tile", "layer"), swap_pairs(axis, False))
        return far, lax.ppermute(values[1], ("tile", "layer"), swap_pairs(axis, True))

    block = struct(NXL, NZL, NY)
    ints = pltpu.VMEM((NXL, NZL, NY), jnp.int32)
    z_message, x_message = struct(3, NXL, NY), struct(6, NZL, NY)
    z_b, z_a, x_b, x_a = call(
        pack,
        [z_message, z_message, x_message, x_message],
        [ints, ints, pltpu.SemaphoreType.DMA((2,))],
        in_specs=[pl.BlockSpec(memory_space=pltpu.HBM)] * 2,
    )(*(pltpu.with_memory_space_constraint(v, pltpu.HBM) for v in (classes, well_mask)))
    z_b, z_a = swap((z_b, z_a), "layer")
    x_out = call(pack_lines, [x_message] * 2, in_specs=[VMEM] * 4)(x_b, x_a, z_b, z_a)
    x_b, x_a = swap(x_out, "tile")
    select, spread = jax.ShapeDtypeStruct((NY, 128), jnp.bfloat16), jax.ShapeDtypeStruct((128, NY), jnp.bfloat16)
    inner, own, beside_y, beside_z, aux, aux_rows, select, spread = call(
        assemble_inner,
        [struct(16, NY), block, block, block, struct(13, NZL, NY), struct(8, NY), select, spread],
        in_specs=[VMEM] * 5,
        cost_estimate=pl.CostEstimate(flops=10**7, bytes_accessed=2 * 10**6, transcendentals=10**5),
    )(classes, well_mask, source, z_b, z_a)
    part, edge = call(
        assemble,
        [struct(TILES * LAYERS, ROWS, 128), struct(8, NZL, NY)],
        [pltpu.VMEM((64, NY), F32), pltpu.VMEM((6, 64, 128), F32), pltpu.VMEM((3 * NCZ, ROWS, 128), F32)],
        in_specs=[VMEM] * 12,
    )(source, z_b, z_a, x_b, x_a, inner, own, beside_y, beside_z, aux, aux_rows, select)
    received = lax.all_to_all(part, ("tile", "layer"), 0, 0, tiled=True)
    rows = received.reshape(TILES * LAYERS * ROWS, 128)
    return call(solve, block, in_specs=[VMEM] * 6)(rows, own, beside_y, beside_z, edge, spread)


def solution(mesh):
    spec = P("tile", "layer", None)
    return jax.shard_map(body, mesh=mesh, in_specs=(spec, spec, spec), out_specs=spec, check_vma=False)
```

```python
import functools

import jax
import jax.numpy as jnp
import numpy as np
from jax import lax
from jax.experimental import pallas as pl
from jax.experimental.pallas import tpu as pltpu
from jax.sharding import PartitionSpec as P

EDGE = 16
SWEEPS = 4
FINE_DAMPING = 0.67
COARSE_DAMPING = 0.5
NXL, NZL, NY = 16, 8, 512
TILES, LAYERS = 16, 8
NCY = NY // EDGE
NCZ = LAYERS * NZL // EDGE
ROWS = 8
F32 = jnp.float32
VMEM = pl.BlockSpec(memory_space=pltpu.VMEM)

NODES = ("N", "Q", "Z", "QZ")


def order(key):
    return NODES.index(key[0]) * 2 + (key[1] == "v")


def pair(a, b):
    return (a, b) if order(a) <= order(b) else (b, a)


SLOT = {}
for where, row in (("own", 0), ("near", 2)):
    for i, key in enumerate(
        [("s", 0, 0, 0), ("s", 0, 0, 1), ("s", 1, 1, 0), ("s", 1, 1, 1)]
        + [("s", 0, 1, -1), ("s", 0, 1, 0), ("s", 0, 1, 1), ("r", 0)]
    ):
        SLOT[where, key] = (row + i // 4, i % 4)
SLOT["own", ("r", 1)] = (7, 0)
SLOT["own", ("r", -1)] = (7, 1)
for i, (lo, hi, dy) in enumerate((lo, hi, dy) for lo in (0, 1) for hi in (0, 1) for dy in (-1, 0, 1)):
    SLOT["low", ("z", lo, hi, dy)] = (4 + i // 4, i % 4)
HERE = ("N", "Q")
BESIDE = ("Z", "QZ")


def cells_of(layer):
    own = layer // 2
    near = own + 1 if layer % 2 else own - 1
    return {"own": own, "near": near, "low": min(own, near)}


def swap_pairs(axis, first):
    pairs = []
    for tile in range(TILES):
        for layer in range(LAYERS):
            at, count = (tile, TILES) if axis == "tile" else (layer, LAYERS)
            if first:
                to = at ^ 1
            else:
                to = at if at in (0, count - 1) else ((at + 1) ^ 1) - 1
            partner = (to, layer) if axis == "tile" else (tile, to)
            if to == at:
                partner = (tile, layer ^ 1) if axis == "tile" else (tile ^ 1, layer)
            pairs.append((tile * LAYERS + layer, partner[0] * LAYERS + partner[1]))
    return pairs


def pack(cls_hbm, well_hbm, z_b, z_a, x_b, x_a, cls, well, sems):
    copies = [pltpu.make_async_copy(cls_hbm, cls, sems.at[0]), pltpu.make_async_copy(well_hbm, well, sems.at[1])]
    for copy in copies:
        copy.start()
    for copy in copies:
        copy.wait()

    def both(first, last, odd, b, a):
        a[0] = jnp.where(odd, first, last)
        b[0] = jnp.where(odd, last, first)

    odd_z = lax.axis_index("layer") % 2 == 1
    odd_x = lax.axis_index("tile") % 2 == 1
    low, high = slice(0, 8), slice(8, NXL)
    down = [cls[:, 0, :], jnp.concatenate([cls[low, 1, :], well[low, 0, :]], axis=0)]
    up = [cls[:, NZL - 1, :], jnp.concatenate([cls[high, NZL - 2, :], well[high, NZL - 1, :]], axis=0)]
    for i in range(2):
        both(down[i].astype(F32), up[i].astype(F32), odd_z, z_b.at[i : i + 1], z_a.at[i : i + 1])
    both(cls[0].astype(F32), cls[NXL - 1].astype(F32), odd_x, x_b, x_a)
    for out in (x_b, x_a):
        out[1] = cls[1].astype(F32)
        out[2] = cls[2].astype(F32)
        out[3] = well[0].astype(F32)
        out[4] = well[1].astype(F32)


def pack_lines(old_b, old_a, z_b, z_a, x_b, x_a):
    odd_z = lax.axis_index("layer") % 2 == 1

    def head(ref, plane, first=0):
        return ref[plane, first : first + 8, :]

    up = [jnp.where(odd_z, head(z_b, *at), head(z_a, *at)) for at in ((0, 0), (1, 0), (1, 8))]
    down = jnp.where(odd_z, head(z_a, 0), head(z_b, 0))
    lines = [down[0:1], down[1:2], up[0][0:1], up[0][1:2], up[1][0:1], up[2][0:1], jnp.zeros((2, NY), F32)]
    lines = jnp.concatenate(lines, axis=0)
    for old, out in ((old_b, x_b), (old_a, x_a)):
        for i in range(5):
            out[i] = old[i]
        out[5] = lines


def lane_roll(value, by):
    return pltpu.roll(value, by % value.shape[-1], value.ndim - 1)


def row_roll(value, by):
    return pltpu.roll(value, by % value.shape[0], 0)


def resist(c):
    return jnp.exp(2.5 - c * F32(1.0 / 3.0))


def sink(c, w):
    return 0.5 * w * jnp.exp(c * F32(1.0 / 3.0) - 2.5)


def y_faces(r):
    ty = 2.0 / (r + lane_roll(r, -1))
    ty = jnp.where(lax.broadcasted_iota(jnp.int32, r.shape, 1) < NY - 1, ty, 0.0)
    return ty, lane_roll(ty, 1)


def y_part(ty, ty_lo):
    at = lax.broadcasted_iota(jnp.int32, ty.shape, 1) % EDGE
    return jnp.where(at == 0, ty_lo, jnp.where(at == EDGE - 1, ty, 0.0))


def basis(s, others, leave_y, leave_z, tx_lo, tx_hi):
    d = FINE_DAMPING / (s + others + tx_lo + tx_hi)
    ey, ez = d * leave_y, d * leave_z
    return 1.0 - d * s - ey - ez, ey, ez, d


def three(value):
    pieces = []
    for _ in range(3):
        piece = value.astype(jnp.bfloat16)
        pieces.append(piece)
        value = value - piece.astype(F32)
    return jnp.concatenate(pieces, axis=0)


def times_01(value, matrix):
    n = value.shape[0]
    out = jnp.dot(three(value), matrix, preferred_element_type=F32)
    return out[0:n] + (out[n : 2 * n] + out[2 * n : 3 * n])


def row_sums(arrays):
    row = lax.broadcasted_iota(jnp.int32, arrays[0].shape, 0)
    arrays = list(arrays) + [jnp.zeros(arrays[0].shape, F32)] * (8 - len(arrays))
    arrays = [arrays[i] for i in (0, 4, 2, 6, 1, 5, 3, 7)]
    for bit in (4, 2, 1):
        low = row // bit % 2 == 0
        merged = []
        for a, b in zip(arrays[::2], arrays[1::2]):
            keep, move = jnp.where(low, a, b), jnp.where(low, b, a)
            moved = row_roll(move, 4) if bit == 4 else jnp.where(low, row_roll(move, -bit), row_roll(move, bit))
            merged.append(keep + moved)
        arrays = merged
    return arrays[0]


def total_of(values):
    values = list(values)
    while len(values) > 1:
        values = [a + b for a, b in zip(values[::2], values[1::2])] + ([values[-1]] if len(values) % 2 else [])
    return values[0]


def minus(a, b):
    out = {}
    for key in {**a, **b}:
        if key in a and key in b:
            out[key] = a[key] - b[key]
        else:
            out[key] = a[key] if key in a else -b[key]
    return out


COLUMNS = (("N", "Z"), ("Q", "QZ"))


class Block:
    def __init__(self, z_b, z_a):
        self.tile, self.layer = lax.axis_index("tile"), lax.axis_index("layer")
        self.odd_z, self.odd_x = self.layer % 2 == 1, self.tile % 2 == 1
        self.has_up, self.has_down = (self.layer < LAYERS - 1).astype(F32), (self.layer > 0).astype(F32)
        self.has_right, self.has_left = (self.tile < TILES - 1).astype(F32), (self.tile > 0).astype(F32)
        self.plane = (NZL, NY)
        self.zrow = lax.broadcasted_iota(jnp.int32, self.plane, 0)
        self.m_r = lax.broadcasted_iota(jnp.int32, self.plane, 1) % EDGE == EDGE - 1
        self.at_zb = self.zrow == jnp.where(self.odd_z, NZL - 1, 0)
        self.up_mask = jnp.where(self.zrow == NZL - 1, self.has_up, 1.0)
        self.down_mask = jnp.where(self.zrow == 0, self.has_down, 1.0)
        self.sums = {}
        self.z_b, self.z_a = z_b, z_a

    def beyond(self, up):
        first, second = (self.z_b, self.z_a) if up else (self.z_a, self.z_b)
        planes = [jnp.where(self.odd_z, first[i], second[i]) for i in range(2)]
        return planes[0], planes[1][0:8], planes[1][8:16]

    def last_row(self, row, value):
        return jnp.where(self.zrow == NZL - 1, jnp.broadcast_to(row, self.plane), value)

    def known(self, r, below, over, upper=True):
        r_up = self.last_row(over, row_roll(r, -1))
        r_dn = jnp.where(self.zrow == 0, jnp.broadcast_to(below, self.plane), row_roll(r, 1))
        tz_hi, tz_lo = 0.5 / (r + r_up) * self.up_mask, 0.5 / (r + r_dn) * self.down_mask
        ty, ty_lo = y_faces(r)
        leave_z = jnp.where(self.at_zb, jnp.where(self.odd_z, tz_hi, tz_lo), 0.0)
        others = tz_hi + tz_lo + ty + ty_lo
        return tz_hi if upper else row_roll(tz_lo, -1), ty, others, y_part(ty, ty_lo), leave_z

    def crosses(self, upper):
        return self.odd_z if upper else ~self.odd_z

    def outer(self, r_edge, r, r_next, upper=True):
        t_edge, t_next = 0.5 / (r_edge + r) * (self.has_up if upper else self.has_down), 0.5 / (r + r_next)
        ty, ty_lo = y_faces(r)
        return t_edge + t_next + ty + ty_lo, y_part(ty, ty_lo), jnp.where(self.crosses(upper), t_edge, 0.0)

    def held(self, o, ey, ez, other=None, columns=COLUMNS, upper=True):
        (a, az), (b, bz) = columns
        crosses = self.crosses(upper)
        out = {
            (a, "u"): jnp.where(crosses, ez, o),
            (a, "v"): jnp.where(crosses, 0.0, ey),
            (az, "u"): jnp.where(crosses, o, 0.0),
            (az, "v"): jnp.where(crosses, ey, 0.0),
        }
        if other is not None:
            out[b, "u"] = jnp.where(crosses, 0.0, other)
            out[bz, "u"] = jnp.where(crosses, other, 0.0)
        return out

    def add(self, key, value):
        self.sums[key] = self.sums[key] + value if key in self.sums else value

    def add_pairs(self, weight, values):
        keys = sorted(values, key=order)
        for i, a in enumerate(keys):
            scaled = weight * values[a]
            for b in keys[i:]:
                self.add((a, b), scaled * values[b])

    def add_source(self, here, source):
        for key, value in here.items():
            self.add(("rhs", key), value * source)

    def add_plane(self, here, outer, s, tz, ty, counted=None, upper=True):
        if counted is not None:
            s, tz, ty = s * counted, tz * counted, ty * counted
        self.add_pairs(s, here)
        near, there = dict(here), {key: row_roll(value, -1) for key, value in here.items()}
        changed = there if upper else near
        for key, row in outer.items():
            changed[key] = self.last_row(row, changed.get(key, 0.0))
        self.add_pairs(tz, minus(near, there))
        rolled = {key: lane_roll(value, -1) for key, value in here.items()}
        there = {}
        for node in {key[0]: None for key in here}:
            u, v = rolled.get((node, "u"), 0.0), rolled.get((node, "v"), 0.0)
            there[node, "u"] = jnp.where(self.m_r, v, u)
            there[node, "v"] = jnp.where(self.m_r, u, v)
        self.add_pairs(ty, minus(here, there))


def inner_keys():
    held = [("N", "u"), ("N", "v"), ("Z", "u"), ("Z", "v")]
    keys = [(a, b) for i, a in enumerate(held) for b in held[i:]]
    return keys + [("rhs", key) for key in held[:3]]


def assemble_inner(cls, well, src, z_b, z_a, rows, own, beside_y, beside_z, aux, aux_rows, select, spread):
    block = Block(z_b, z_a)
    last, half = NXL - 1, NXL // 2
    r8, rm = None, None
    outers = []
    for upper in (True, False):
        adjacent, after, wells = block.beyond(upper)
        rows_here = slice(0, half) if upper else slice(half, NXL)
        r_all = resist(adjacent)
        r, s = r_all[rows_here], sink(adjacent[rows_here], wells)
        r_edge = resist(cls[rows_here, NZL - 1 if upper else 0, :].astype(F32))
        others, leave_y, leave_z = block.outer(r_edge, r, resist(after), upper)
        tx_lo = 2.0 / (r + row_roll(r_all, 1)[rows_here])
        if upper:
            tx_lo = jnp.where(lax.broadcasted_iota(jnp.int32, r.shape, 0) == 0, 0.0, tx_lo)
        o, ey, ez, _ = basis(s, others, leave_y, leave_z, tx_lo, 2.0 / (r + row_roll(r_all, -1)[rows_here]))
        held = block.held(o, ey, ez, upper=upper)
        outers += [{key: value[x : x + 1] for key, value in held.items()} for x in range(half)]
        if upper:
            r8 = r_all
        else:
            rm = r_all
            for i, value in enumerate((s, others + tx_lo, leave_y, leave_z, r)):
                aux_rows[i : i + 1, :] = value[half - 1 : half]
    aux_rows[5:6, :] = r8[last:NXL]
    aux_rows[6:8, :] = jnp.zeros((2, NY), F32)
    rs = [resist(cls[x].astype(F32)) for x in range(NXL)]
    txs = [jnp.zeros(block.plane, F32)] + [2.0 / (rs[x] + rs[x + 1]) for x in range(last)]
    first = 1.0 - block.has_left
    before = None
    for x in range(NXL):
        s = sink(cls[x].astype(F32), well[x].astype(F32))
        upper = x < half
        tz, ty, others, leave_y, leave_z = block.known(rs[x], rm[x : x + 1], r8[x : x + 1], upper)
        if x == 0:
            for i, value in enumerate((s, others + txs[1], leave_y, leave_z, rs[x])):
                aux[i] = value
        if x == last:
            for i, value in enumerate((s, others + txs[last], leave_y, leave_z, rs[x], tz, ty, txs[last])):
                aux[5 + i] = value
            break
        o, ey, ez, _ = basis(s, others, leave_y, leave_z, txs[x], txs[x + 1])
        own[x] = o
        beside_y[x] = ey
        beside_z[x] = ez
        here = {("N", "u"): o, ("N", "v"): ey, ("Z", "u"): ez}
        block.add_plane(here, outers[x], s, tz, ty, first if x == 0 else None, upper)
        if x:
            block.add_source(here, src[x])
            block.add_pairs(txs[x] * first if x == 1 else txs[x], minus(before, here))
        before = here
    keys = inner_keys()
    for i in range(0, len(keys), 8):
        rows[i : i + 8, :] = row_sums([block.sums[key] for key in keys[i : i + 8]])

    j = lax.broadcasted_iota(jnp.int32, (NY, 128), 0)
    n = lax.broadcasted_iota(jnp.int32, (NY, 128), 1)
    group, pos = n // NCY, j % EDGE
    taken = (group == 0) | ((group == 1) & (pos == 0)) | ((group == 2) & (pos >= EDGE - 2))
    select[...] = jnp.where((j // EDGE == n % NCY) & taken, 1.0, 0.0).astype(jnp.bfloat16)
    i = lax.broadcasted_iota(jnp.int32, (128, NY), 0)
    j = lax.broadcasted_iota(jnp.int32, (128, NY), 1)
    spread[...] = jnp.where(i % NCY == j // EDGE, 1.0, 0.0).astype(jnp.bfloat16)


def assemble(
    src, z_b, z_a, x_b, x_a, rows, own, beside_y, beside_z, aux, aux_rows, select, part, edge, lanes_ref, g_ref, out_ref
):
    block = Block(z_b, z_a)
    layer, odd_z, has_right, last_row = block.layer, block.odd_z, block.has_right, slice(NZL - 1, NZL)
    right = [jnp.where(block.odd_x, x_b[i], x_a[i]) for i in range(6)]
    left = jnp.where(block.odd_x, x_a[0], x_b[0])
    lines, lines_r = right[5], resist(right[5])

    tx = 2.0 / (aux_rows[4:5] + lines_r[0:1]) * has_right
    o, ey, ez, d = basis(*(aux_rows[i : i + 1] for i in range(4)), 0.0, tx)
    below_15 = block.held(o - d * tx, ey, ez, d * tx, upper=False)
    r8_15, r8_16, r8_17, r9_16 = aux_rows[5:6], lines_r[2:3], lines_r[3:4], lines_r[4:5]
    tx = 2.0 / (r8_15 + r8_16) * has_right
    rs = [aux[9]] + [resist(right[i]) for i in range(3)]
    o, ey, ez, d = basis(
        sink(lines[2:3], lines[5:6]), *block.outer(rs[1][last_row], r8_16, r9_16), tx, 2.0 / (r8_16 + r8_17)
    )
    above_16 = block.held(o - d * tx, ey, ez, d * tx, COLUMNS[::-1])

    t_left = 2.0 / (resist(left) + aux[4]) * block.has_left
    o, ey, ez, d = basis(*(aux[i] for i in range(4)), t_left, 0.0)
    o, ex = o - d * t_left, d * t_left
    for i, value in enumerate((o, ey, ez, ex)):
        edge[i] = value
    block.add_source({("N", "u"): o, ("N", "v"): ey, ("Z", "u"): ez, ("M", "u"): ex}, src[0])

    t_14 = aux[12]
    txs = [0.0, 2.0 / (rs[0] + rs[1]) * has_right, 2.0 / (rs[1] + rs[2]), 2.0 / (rs[2] + rs[3])]
    known = [(aux[10], aux[11], aux[6], aux[7], aux[8])]
    known += [block.known(rs[i], lines_r[i - 1 : i], (r8_16, r8_17)[i - 1]) for i in (1, 2)]
    ss = [aux[5]] + [sink(right[i], right[3 + i]) for i in range(2)]
    planes = []
    for i in range(3):
        o, ey, ez, d = basis(ss[i], *known[i][2:], txs[i], txs[i + 1])
        (a, az), (b, _) = COLUMNS if i == 0 else COLUMNS[::-1]
        here = {(a, "v"): ey, (az, "u"): ez}
        if i < 2:
            here[b, "u"] = d * txs[1]
            o = o - here[b, "u"]
        if i == 0:
            for k, value in enumerate((o, ey, ez, here[b, "u"])):
                edge[4 + k] = value
        here[a, "u"] = o
        planes.append(here)
    before = {("N", "u"): own[NXL - 2], ("N", "v"): beside_y[NXL - 2], ("Z", "u"): beside_z[NXL - 2]}
    block.add_pairs(t_14, minus(before, planes[0]))
    block.add_plane(planes[0], below_15, ss[0], *known[0][:2], upper=False)
    block.add_source(planes[0], src[NXL - 1])
    block.add_pairs(txs[1], minus(planes[0], planes[1]))
    block.add_plane(planes[1], above_16, ss[1], *known[1][:2], has_right)
    block.add_pairs(txs[2] * has_right, minus(planes[1], planes[2]))
    sums = block.sums

    keys = inner_keys() + [key for key in sums if key not in inner_keys()]
    index = {key: i for i, key in enumerate(keys)}
    count = -(-len(keys) // 16) * 16
    for i in range(0, count, 8):
        here = [sums[key] for key in keys[i : i + 8]]
        value = row_sums(here) if here else jnp.zeros((8, NY), F32)
        lanes_ref[i : i + 8, :] = value + rows[i : i + 8, :] if i < 16 else value
    grouped = times_01(lanes_ref[0:count, :], select[...])
    gl = lax.broadcasted_iota(jnp.int32, (count, 128), 1)
    g_l_next = jnp.where(gl < NCY - 1, lane_roll(grouped, -(NCY + 1)), 0.0)
    g_r_next = jnp.where((gl > 0) & (gl < NCY), lane_roll(grouped, -(2 * NCY - 1)), 0.0)
    forms = {
        "all": jnp.where(gl < NCY, grouped, 0.0),
        "L": jnp.where(gl < NCY, lane_roll(grouped, -NCY), 0.0),
        "R": jnp.where(gl < NCY, lane_roll(grouped, -2 * NCY), 0.0),
        "Ls": g_l_next,
        "Rs": g_r_next,
        "vv": g_l_next + g_r_next,
    }
    at = {}
    for i, (name, value) in enumerate(forms.items()):
        at[name] = i
        g_ref[i, 0:count, :] = value

    def taken_rows(terms):
        total = None
        for name, key in terms:
            if key in index:
                q = index[key]
                row = g_ref[at[name], q : q + 1, :]
                total = row if total is None else total + row
        return total

    def terms_of(a, b, dy):
        au, av, bu, bv = (a, "u"), (a, "v"), (b, "u"), (b, "v")
        if a == b:
            if dy == 0:
                return [("all", pair(au, au)), ("vv", pair(av, av))]
            return [("Ls", pair(au, av)), ("R", pair(au, av))]
        if dy == 0:
            return [("all", pair(au, bu)), ("vv", pair(av, bv))]
        if dy < 0:
            return [("L", pair(au, bv)), ("Rs", pair(av, bu))]
        return [("R", pair(au, bv)), ("Ls", pair(av, bu))]

    nothing = jnp.zeros((1, 128), F32)
    out_ref[...] = jnp.zeros(out_ref.shape, F32)
    spots = [(where, k) for where in ("own", "near", "low") for k in range(NCZ)]
    for (where, key), (r, k) in SLOT.items():
        names = {"own": HERE, "near": BESIDE}.get(where)
        if key[0] == "s":
            row = taken_rows(terms_of(names[key[1]], names[key[2]], key[3]))
        elif key[0] == "r":
            node = "M" if key[1] < 0 else names[key[1]]
            row = taken_rows([("all", ("rhs", (node, "u"))), ("vv", ("rhs", (node, "v")))])
        else:
            when_odd = taken_rows(terms_of(HERE[key[1]], BESIDE[key[2]], key[3]))
            when_even = taken_rows(terms_of(BESIDE[key[1]], HERE[key[2]], key[3]))
            when_odd = nothing if when_odd is None else when_odd
            when_even = nothing if when_even is None else when_even
            row = jnp.where(odd_z, when_odd, when_even)
        if row is not None:
            out_ref[spots.index((where, k)), r : r + 1, :] = row
    cell = layer // 2
    near_cell = jnp.where(odd_z, cell + 1, cell - 1)
    coarse_layer = {"own": cell, "near": near_cell, "low": jnp.minimum(cell, near_cell)}
    group = lax.broadcasted_iota(jnp.int32, (ROWS, 128), 1) // NCY
    total = jnp.zeros((ROWS, 128), F32)
    for i, (where, k) in enumerate(spots):
        if (where, k) not in {(w, kk) for (w, _), (_, kk) in SLOT.items()}:
            continue
        rows = out_ref[i]
        spread = rows
        for n in range(1, NCZ):
            spread = spread + lane_roll(rows, n * NCY)
        total = total + jnp.where(group == (coarse_layer[where] + k + NCZ) % NCZ, spread, 0.0)
    for k in range(TILES * LAYERS):
        part[k] = total


def solve(rows, own, beside_y, beside_z, edge, spread, pressure):
    tile, layer = lax.axis_index("tile"), lax.axis_index("layer")
    odd_z = layer % 2 == 1
    cell = layer // 2
    near_cell = jnp.where(odd_z, cell + 1, cell - 1)
    shape = (TILES, 128)
    strip = lax.broadcasted_iota(jnp.int32, shape, 0)
    group = lax.broadcasted_iota(jnp.int32, shape, 1) // NCY
    lane_cell = group[0:1]

    loaded = {}

    def load(layer_from, row):
        if (layer_from, row) not in loaded:
            loaded[layer_from, row] = rows[pl.ds(layer_from * ROWS + row, TILES, stride=LAYERS * ROWS), :]
        return loaded[layer_from, row]

    by_shift = {}
    for (where, key), (row, k) in SLOT.items():
        found = []
        for l in range(LAYERS):
            z = cells_of(l)[where]
            if 0 <= z and max(cells_of(l)["own"], cells_of(l)["near"] if where != "own" else 0) < NCZ:
                found.append(jnp.where(group == (z + k) % NCZ, load(l, row), 0.0))
        total = total_of(found)
        by_shift[key, k] = by_shift[key, k] + total if (key, k) in by_shift else total
    terms = {}
    for (key, k), value in by_shift.items():
        value = lane_roll(value, -k * NCY) if k else value
        terms[key] = terms[key] + value if key in terms else value

    def from_last(value):
        return jnp.where(strip > 0, row_roll(value, 1), 0.0)

    half = {}
    for dy in (0, 1):
        half[0, 0, dy] = terms["s", 0, 0, dy] + from_last(terms["s", 1, 1, dy])
    for dy in (-1, 0, 1):
        half[1, 0, dy] = terms["s", 0, 1, dy]
        half[0, 1, dy] = terms["z", 0, 0, dy] + from_last(terms["z", 1, 1, dy])
        half[1, 1, dy] = terms["z", 0, 1, dy]
        half[-1, 1, dy] = from_last(terms["z", 1, 0, dy])
    back = jnp.where(strip < TILES - 1, row_roll(terms["r", -1], -1), 0.0)
    rhs = terms["r", 0] + from_last(terms["r", 1]) + back
    centre = half.pop((0, 0, 0))
    scale = COARSE_DAMPING / centre

    def shifted(value, dx, dz, dy):
        by = -(dz * NCY + dy)
        if by:
            value = lane_roll(value, by)
        return row_roll(value, -dx) if dx else value

    full = dict(half)
    for (dx, dz, dy), value in half.items():
        full[-dx, -dz, -dy] = shifted(value, -dx, -dz, -dy)
    coarse = scale * rhs
    for _ in range(SWEEPS - 1):
        applied = [centre * coarse]
        for dz in (-1, 0, 1):
            for dy in (-1, 0, 1):
                moved = shifted(coarse, 0, dz, dy)
                for dx in (-1, 0, 1):
                    if (dx, dz, dy) in full:
                        applied.append(full[dx, dz, dy] * shifted(moved, dx, 0, 0))
        coarse = coarse + scale * (rhs - total_of(applied))

    def strip_row(at):
        return jnp.sum(jnp.where(strip == at, coarse, 0.0), axis=0, keepdims=True)

    here = strip_row(tile)
    own_row = jnp.where(lane_cell == cell, here, 0.0)
    picked = [
        own_row,
        jnp.where(lane_cell == cell, strip_row(tile - 1), 0.0),
        jnp.where(lane_cell == cell, strip_row(tile + 1), 0.0),
        jnp.where(lane_cell == near_cell, here, 0.0),
        lane_roll(own_row, 1),
        lane_roll(own_row, -1),
        jnp.zeros((2, 128), F32),
    ]
    picked = jnp.concatenate(picked, axis=0)
    fine = times_01(picked, spread[...])
    lane = lax.broadcasted_iota(jnp.int32, (1, NY), 1) % EDGE
    near_y = jnp.where(lane == 0, fine[4:5], jnp.where(lane == EDGE - 1, fine[5:6], 0.0))
    for x in range(NXL):
        if x in (0, NXL - 1):
            first, row = (0, fine[1:2]) if x == 0 else (4, fine[2:3])
            value = edge[first] * fine[0:1] + edge[first + 1] * near_y + edge[first + 2] * fine[3:4] + edge[first + 3] * row
        else:
            value = own[x] * fine[0:1] + beside_y[x] * near_y + beside_z[x] * fine[3:4]
        pressure[x] = value


def struct(*shape):
    return jax.ShapeDtypeStruct(shape, F32)


def call(kernel, outs, scratch=(), **kw):
    many = isinstance(outs, (list, tuple))
    return pl.pallas_call(
        kernel,
        out_shape=outs,
        out_specs=[VMEM] * len(outs) if many else VMEM,
        scratch_shapes=list(scratch),
        compiler_params=pltpu.CompilerParams(vmem_limit_bytes=48 * 1024 * 1024),
        **kw,
    )


def body(classes, well_mask, source):
    def swap(values, axis):
        far = lax.ppermute(values[0], ("tile", "layer"), swap_pairs(axis, False))
        return far, lax.ppermute(values[1], ("tile", "layer"), swap_pairs(axis, True))

    block = struct(NXL, NZL, NY)
    ints = pltpu.VMEM((NXL, NZL, NY), jnp.int32)
    z_message, x_message = struct(2, NXL, NY), struct(6, NZL, NY)
    z_b, z_a, x_b, x_a = call(
        pack,
        [z_message, z_message, x_message, x_message],
        [ints, ints, pltpu.SemaphoreType.DMA((2,))],
        in_specs=[pl.BlockSpec(memory_space=pltpu.HBM)] * 2,
    )(*(pltpu.with_memory_space_constraint(v, pltpu.HBM) for v in (classes, well_mask)))
    z_b, z_a = swap((z_b, z_a), "layer")
    x_out = call(pack_lines, [x_message] * 2, in_specs=[VMEM] * 4)(x_b, x_a, z_b, z_a)
    x_b, x_a = swap(x_out, "tile")
    select, spread = jax.ShapeDtypeStruct((NY, 128), jnp.bfloat16), jax.ShapeDtypeStruct((128, NY), jnp.bfloat16)
    inner, own, beside_y, beside_z, aux, aux_rows, select, spread = call(
        assemble_inner,
        [struct(16, NY), block, block, block, struct(13, NZL, NY), struct(8, NY), select, spread],
        in_specs=[VMEM] * 5,
        cost_estimate=pl.CostEstimate(flops=10**7, bytes_accessed=2 * 10**6, transcendentals=10**5),
    )(classes, well_mask, source, z_b, z_a)
    part, edge = call(
        assemble,
        [struct(TILES * LAYERS, ROWS, 128), struct(8, NZL, NY)],
        [pltpu.VMEM((64, NY), F32), pltpu.VMEM((6, 64, 128), F32), pltpu.VMEM((3 * NCZ, ROWS, 128), F32)],
        in_specs=[VMEM] * 12,
    )(source, z_b, z_a, x_b, x_a, inner, own, beside_y, beside_z, aux, aux_rows, select)
    received = lax.all_to_all(part, ("tile", "layer"), 0, 0, tiled=True)
    rows = received.reshape(TILES * LAYERS * ROWS, 128)
    return call(solve, block, in_specs=[VMEM] * 6)(rows, own, beside_y, beside_z, edge, spread)


def solution(mesh):
    spec = P("tile", "layer", None)
    return jax.shard_map(body, mesh=mesh, in_specs=(spec, spec, spec), out_specs=spec, check_vma=False)
```

```python
import jax
import jax.numpy as jnp
from jax import lax
from jax.experimental import pallas as pl
from jax.experimental.pallas import tpu as pltpu
from jax.sharding import PartitionSpec as P

EDGE = 16
SWEEPS = 4
FINE_DAMPING = 0.67
COARSE_DAMPING = 0.5
NXL, NZL, NY = 16, 8, 512
TILES, LAYERS = 16, 8
NCY = NY // EDGE
NCZ = LAYERS * NZL // EDGE
ROWS = 8
F32 = jnp.float32
VMEM = pl.BlockSpec(memory_space=pltpu.VMEM)

NODES = ("N", "Q", "Z", "QZ")


def order(key):
    return NODES.index(key[0]) * 2 + (key[1] == "v")


def pair(a, b):
    return (a, b) if order(a) <= order(b) else (b, a)


SLOT = {}
for where, row in (("own", 0), ("near", 2)):
    for i, key in enumerate(
        [("s", 0, 0, 0), ("s", 0, 0, 1), ("s", 1, 1, 0), ("s", 1, 1, 1)]
        + [("s", 0, 1, -1), ("s", 0, 1, 0), ("s", 0, 1, 1), ("r", 0)]
    ):
        SLOT[where, key] = (row + i // 4, i % 4)
SLOT["own", ("r", 1)] = (7, 0)
SLOT["own", ("r", -1)] = (7, 1)
for i, (lo, hi, dy) in enumerate((lo, hi, dy) for lo in (0, 1) for hi in (0, 1) for dy in (-1, 0, 1)):
    SLOT["low", ("z", lo, hi, dy)] = (4 + i // 4, i % 4)
HERE = ("N", "Q")
BESIDE = ("Z", "QZ")


def cells_of(layer):
    own = layer // 2
    near = own + 1 if layer % 2 else own - 1
    return {"own": own, "near": near, "low": min(own, near)}


def swap_pairs(axis, first):
    pairs = []
    for tile in range(TILES):
        for layer in range(LAYERS):
            at, count = (tile, TILES) if axis == "tile" else (layer, LAYERS)
            if first:
                to = at ^ 1
            else:
                to = at if at in (0, count - 1) else ((at + 1) ^ 1) - 1
            partner = (to, layer) if axis == "tile" else (tile, to)
            if to == at:
                partner = (tile, layer ^ 1) if axis == "tile" else (tile ^ 1, layer)
            pairs.append((tile * LAYERS + layer, partner[0] * LAYERS + partner[1]))
    return pairs


def pack(cls_hbm, well_hbm, z_b, z_a, x_b, x_a, cls, well, sems):
    copies = [pltpu.make_async_copy(cls_hbm, cls, sems.at[0]), pltpu.make_async_copy(well_hbm, well, sems.at[1])]
    for copy in copies:
        copy.start()
    for copy in copies:
        copy.wait()

    def both(first, last, odd, b, a):
        a[0] = jnp.where(odd, first, last)
        b[0] = jnp.where(odd, last, first)

    odd_z = lax.axis_index("layer") % 2 == 1
    odd_x = lax.axis_index("tile") % 2 == 1
    low, high = slice(0, 8), slice(8, NXL)
    down = [cls[:, 0, :], jnp.concatenate([cls[low, 1, :], well[low, 0, :]], axis=0)]
    up = [cls[:, NZL - 1, :], jnp.concatenate([cls[high, NZL - 2, :], well[high, NZL - 1, :]], axis=0)]
    for i in range(2):
        both(down[i].astype(F32), up[i].astype(F32), odd_z, z_b.at[i : i + 1], z_a.at[i : i + 1])
    both(cls[0].astype(F32), cls[NXL - 1].astype(F32), odd_x, x_b, x_a)
    for out in (x_b, x_a):
        out[1] = cls[1].astype(F32)
        out[2] = cls[2].astype(F32)
        out[3] = well[0].astype(F32)
        out[4] = well[1].astype(F32)


def pack_lines(old_a, z_b, z_a, lines, x_a):
    odd_z = lax.axis_index("layer") % 2 == 1

    def head(ref, plane, first=0):
        return ref[plane, first : first + 8, :]

    up = [jnp.where(odd_z, head(z_b, *at), head(z_a, *at)) for at in ((0, 0), (1, 0), (1, 8))]
    down = jnp.where(odd_z, head(z_a, 0), head(z_b, 0))
    rows = [down[0:1], down[1:2], up[0][0:1], up[0][1:2], up[1][0:1], up[2][0:1], jnp.zeros((2, NY), F32)]
    rows = jnp.concatenate(rows, axis=0)
    lines[...] = rows
    for i in range(5):
        x_a[i] = old_a[i]
    x_a[5] = rows


def lane_roll(value, by):
    return pltpu.roll(value, by % value.shape[-1], value.ndim - 1)


def row_roll(value, by):
    return pltpu.roll(value, by % value.shape[0], 0)


def resist(c):
    return jnp.exp(2.5 - c * F32(1.0 / 3.0))


def sink(c, w):
    return 0.5 * w * jnp.exp(c * F32(1.0 / 3.0) - 2.5)


def y_faces(r):
    ty = 2.0 / (r + lane_roll(r, -1))
    ty = jnp.where(lax.broadcasted_iota(jnp.int32, r.shape, 1) < NY - 1, ty, 0.0)
    return ty, lane_roll(ty, 1)


def y_part(ty, ty_lo):
    at = lax.broadcasted_iota(jnp.int32, ty.shape, 1) % EDGE
    return jnp.where(at == 0, ty_lo, jnp.where(at == EDGE - 1, ty, 0.0))


def basis(s, others, leave_y, leave_z, tx_lo, tx_hi):
    d = FINE_DAMPING / (s + others + tx_lo + tx_hi)
    ey, ez = d * leave_y, d * leave_z
    return 1.0 - d * s - ey - ez, ey, ez, d


def three(value):
    pieces = []
    for _ in range(3):
        piece = value.astype(jnp.bfloat16)
        pieces.append(piece)
        value = value - piece.astype(F32)
    return jnp.concatenate(pieces, axis=0)


def times_01(value, matrix):
    n = value.shape[0]
    out = jnp.dot(three(value), matrix, preferred_element_type=F32)
    return out[0:n] + (out[n : 2 * n] + out[2 * n : 3 * n])


def row_sums(arrays):
    row = lax.broadcasted_iota(jnp.int32, arrays[0].shape, 0)
    arrays = list(arrays) + [jnp.zeros(arrays[0].shape, F32)] * (8 - len(arrays))
    arrays = [arrays[i] for i in (0, 4, 2, 6, 1, 5, 3, 7)]
    for bit in (4, 2, 1):
        low = row // bit % 2 == 0
        merged = []
        for a, b in zip(arrays[::2], arrays[1::2]):
            keep, move = jnp.where(low, a, b), jnp.where(low, b, a)
            moved = row_roll(move, 4) if bit == 4 else jnp.where(low, row_roll(move, -bit), row_roll(move, bit))
            merged.append(keep + moved)
        arrays = merged
    return arrays[0]


def total_of(values):
    values = list(values)
    while len(values) > 1:
        values = [a + b for a, b in zip(values[::2], values[1::2])] + ([values[-1]] if len(values) % 2 else [])
    return values[0]


def minus(a, b):
    out = {}
    for key in {**a, **b}:
        if key in a and key in b:
            out[key] = a[key] - b[key]
        else:
            out[key] = a[key] if key in a else -b[key]
    return out


COLUMNS = (("N", "Z"), ("Q", "QZ"))


class Block:
    def __init__(self, z_b, z_a):
        self.tile, self.layer = lax.axis_index("tile"), lax.axis_index("layer")
        self.odd_z, self.odd_x = self.layer % 2 == 1, self.tile % 2 == 1
        self.has_up, self.has_down = (self.layer < LAYERS - 1).astype(F32), (self.layer > 0).astype(F32)
        self.has_right, self.has_left = (self.tile < TILES - 1).astype(F32), (self.tile > 0).astype(F32)
        self.plane = (NZL, NY)
        self.zrow = lax.broadcasted_iota(jnp.int32, self.plane, 0)
        self.m_r = lax.broadcasted_iota(jnp.int32, self.plane, 1) % EDGE == EDGE - 1
        self.at_zb = self.zrow == jnp.where(self.odd_z, NZL - 1, 0)
        self.up_mask = jnp.where(self.zrow == NZL - 1, self.has_up, 1.0)
        self.down_mask = jnp.where(self.zrow == 0, self.has_down, 1.0)
        self.sums = {}
        self.z_b, self.z_a = z_b, z_a

    def beyond(self, up):
        first, second = (self.z_b, self.z_a) if up else (self.z_a, self.z_b)
        planes = [jnp.where(self.odd_z, first[i], second[i]) for i in range(2)]
        return planes[0], planes[1][0:8], planes[1][8:16]

    def last_row(self, row, value):
        return jnp.where(self.zrow == NZL - 1, jnp.broadcast_to(row, self.plane), value)

    def known(self, r, below, over, upper=True):
        r_up = self.last_row(over, row_roll(r, -1))
        r_dn = jnp.where(self.zrow == 0, jnp.broadcast_to(below, self.plane), row_roll(r, 1))
        tz_hi, tz_lo = 0.5 / (r + r_up) * self.up_mask, 0.5 / (r + r_dn) * self.down_mask
        ty, ty_lo = y_faces(r)
        leave_z = jnp.where(self.at_zb, jnp.where(self.odd_z, tz_hi, tz_lo), 0.0)
        others = tz_hi + tz_lo + ty + ty_lo
        return tz_hi if upper else row_roll(tz_lo, -1), ty, others, y_part(ty, ty_lo), leave_z

    def crosses(self, upper):
        return self.odd_z if upper else ~self.odd_z

    def outer(self, r_edge, r, r_next, upper=True):
        t_edge, t_next = 0.5 / (r_edge + r) * (self.has_up if upper else self.has_down), 0.5 / (r + r_next)
        ty, ty_lo = y_faces(r)
        return t_edge + t_next + ty + ty_lo, y_part(ty, ty_lo), jnp.where(self.crosses(upper), t_edge, 0.0)

    def held(self, o, ey, ez, other=None, columns=COLUMNS, upper=True):
        (a, az), (b, bz) = columns
        crosses = self.crosses(upper)
        out = {
            (a, "u"): jnp.where(crosses, ez, o),
            (a, "v"): jnp.where(crosses, 0.0, ey),
            (az, "u"): jnp.where(crosses, o, 0.0),
            (az, "v"): jnp.where(crosses, ey, 0.0),
        }
        if other is not None:
            out[b, "u"] = jnp.where(crosses, 0.0, other)
            out[bz, "u"] = jnp.where(crosses, other, 0.0)
        return out

    def add(self, key, value):
        self.sums[key] = self.sums[key] + value if key in self.sums else value

    def add_pairs(self, weight, values):
        keys = sorted(values, key=order)
        for i, a in enumerate(keys):
            scaled = weight * values[a]
            for b in keys[i:]:
                self.add((a, b), scaled * values[b])

    def add_source(self, here, source):
        for key, value in here.items():
            self.add(("rhs", key), value * source)

    def add_plane(self, here, outer, s, tz, ty, counted=None, upper=True):
        if counted is not None:
            s, tz, ty = s * counted, tz * counted, ty * counted
        self.add_pairs(s, here)
        near, there = dict(here), {key: row_roll(value, -1) for key, value in here.items()}
        changed = there if upper else near
        for key, row in outer.items():
            changed[key] = self.last_row(row, changed.get(key, 0.0))
        self.add_pairs(tz, minus(near, there))
        rolled = {key: lane_roll(value, -1) for key, value in here.items()}
        there = {}
        for node in {key[0]: None for key in here}:
            u, v = rolled.get((node, "u"), 0.0), rolled.get((node, "v"), 0.0)
            there[node, "u"] = jnp.where(self.m_r, v, u)
            there[node, "v"] = jnp.where(self.m_r, u, v)
        self.add_pairs(ty, minus(here, there))


def inner_keys():
    held = [("N", "u"), ("N", "v"), ("Z", "u"), ("Z", "v")]
    keys = [(a, b) for i, a in enumerate(held) for b in held[i:]]
    return keys + [("rhs", key) for key in held[:3]]


def assemble_inner(cls, well, src, z_b, z_a, rows, own, beside_y, beside_z, aux, aux_rows, select, spread):
    block = Block(z_b, z_a)
    last, half = NXL - 1, NXL // 2
    r8, rm = None, None
    outers = []
    for upper in (True, False):
        adjacent, after, wells = block.beyond(upper)
        rows_here = slice(0, half) if upper else slice(half, NXL)
        r_all = resist(adjacent)
        r, s = r_all[rows_here], sink(adjacent[rows_here], wells)
        r_edge = resist(cls[rows_here, NZL - 1 if upper else 0, :].astype(F32))
        others, leave_y, leave_z = block.outer(r_edge, r, resist(after), upper)
        tx_lo = 2.0 / (r + row_roll(r_all, 1)[rows_here])
        if upper:
            tx_lo = jnp.where(lax.broadcasted_iota(jnp.int32, r.shape, 0) == 0, 0.0, tx_lo)
        o, ey, ez, _ = basis(s, others, leave_y, leave_z, tx_lo, 2.0 / (r + row_roll(r_all, -1)[rows_here]))
        held = block.held(o, ey, ez, upper=upper)
        outers += [{key: value[x : x + 1] for key, value in held.items()} for x in range(half)]
        if upper:
            r8 = r_all
        else:
            rm = r_all
            for i, value in enumerate((s, others + tx_lo, leave_y, leave_z, r)):
                aux_rows[i : i + 1, :] = value[half - 1 : half]
    aux_rows[5:6, :] = r8[last:NXL]
    aux_rows[6:8, :] = jnp.zeros((2, NY), F32)
    rs = [resist(cls[x].astype(F32)) for x in range(NXL)]
    txs = [jnp.zeros(block.plane, F32)] + [2.0 / (rs[x] + rs[x + 1]) for x in range(last)]
    first = 1.0 - block.has_left
    before = None
    for x in range(NXL):
        s = sink(cls[x].astype(F32), well[x].astype(F32))
        upper = x < half
        tz, ty, others, leave_y, leave_z = block.known(rs[x], rm[x : x + 1], r8[x : x + 1], upper)
        if x == 0:
            for i, value in enumerate((s, others + txs[1], leave_y, leave_z, rs[x])):
                aux[i] = value
        if x == last:
            for i, value in enumerate((s, others + txs[last], leave_y, leave_z, rs[x], tz, ty, txs[last])):
                aux[5 + i] = value
            break
        o, ey, ez, _ = basis(s, others, leave_y, leave_z, txs[x], txs[x + 1])
        own[x] = o
        beside_y[x] = ey
        beside_z[x] = ez
        here = {("N", "u"): o, ("N", "v"): ey, ("Z", "u"): ez}
        block.add_plane(here, outers[x], s, tz, ty, first if x == 0 else None, upper)
        if x:
            block.add_source(here, src[x])
            block.add_pairs(txs[x] * first if x == 1 else txs[x], minus(before, here))
        before = here
    keys = inner_keys()
    for i in range(0, len(keys), 8):
        rows[i : i + 8, :] = row_sums([block.sums[key] for key in keys[i : i + 8]])

    j = lax.broadcasted_iota(jnp.int32, (NY, 128), 0)
    n = lax.broadcasted_iota(jnp.int32, (NY, 128), 1)
    group, pos = n // NCY, j % EDGE
    taken = (group == 0) | ((group == 1) & (pos == 0)) | ((group == 2) & (pos >= EDGE - 2))
    select[...] = jnp.where((j // EDGE == n % NCY) & taken, 1.0, 0.0).astype(jnp.bfloat16)
    i = lax.broadcasted_iota(jnp.int32, (128, NY), 0)
    j = lax.broadcasted_iota(jnp.int32, (128, NY), 1)
    spread[...] = jnp.where(i % NCY == j // EDGE, 1.0, 0.0).astype(jnp.bfloat16)


def assemble(
    src, z_b, z_a, line_b, x_b, x_a, rows, own, beside_y, beside_z, aux, aux_rows, select, part, edge, lanes_ref, g_ref, out_ref
):
    block = Block(z_b, z_a)
    layer, odd_z, has_right, last_row = block.layer, block.odd_z, block.has_right, slice(NZL - 1, NZL)
    right = [jnp.where(block.odd_x, x_b[i], x_a[i]) for i in range(5)]
    right.append(jnp.where(block.odd_x, line_b[...], x_a[5]))
    left = jnp.where(block.odd_x, x_a[0], x_b[0])
    lines, lines_r = right[5], resist(right[5])

    tx = 2.0 / (aux_rows[4:5] + lines_r[0:1]) * has_right
    o, ey, ez, d = basis(*(aux_rows[i : i + 1] for i in range(4)), 0.0, tx)
    below_15 = block.held(o - d * tx, ey, ez, d * tx, upper=False)
    r8_15, r8_16, r8_17, r9_16 = aux_rows[5:6], lines_r[2:3], lines_r[3:4], lines_r[4:5]
    tx = 2.0 / (r8_15 + r8_16) * has_right
    rs = [aux[9]] + [resist(right[i]) for i in range(3)]
    o, ey, ez, d = basis(
        sink(lines[2:3], lines[5:6]), *block.outer(rs[1][last_row], r8_16, r9_16), tx, 2.0 / (r8_16 + r8_17)
    )
    above_16 = block.held(o - d * tx, ey, ez, d * tx, COLUMNS[::-1])

    t_left = 2.0 / (resist(left) + aux[4]) * block.has_left
    o, ey, ez, d = basis(*(aux[i] for i in range(4)), t_left, 0.0)
    o, ex = o - d * t_left, d * t_left
    for i, value in enumerate((o, ey, ez, ex)):
        edge[i] = value
    block.add_source({("N", "u"): o, ("N", "v"): ey, ("Z", "u"): ez, ("M", "u"): ex}, src[0])

    t_14 = aux[12]
    txs = [0.0, 2.0 / (rs[0] + rs[1]) * has_right, 2.0 / (rs[1] + rs[2]), 2.0 / (rs[2] + rs[3])]
    known = [(aux[10], aux[11], aux[6], aux[7], aux[8])]
    known += [block.known(rs[i], lines_r[i - 1 : i], (r8_16, r8_17)[i - 1]) for i in (1, 2)]
    ss = [aux[5]] + [sink(right[i], right[3 + i]) for i in range(2)]
    planes = []
    for i in range(3):
        o, ey, ez, d = basis(ss[i], *known[i][2:], txs[i], txs[i + 1])
        (a, az), (b, _) = COLUMNS if i == 0 else COLUMNS[::-1]
        here = {(a, "v"): ey, (az, "u"): ez}
        if i < 2:
            here[b, "u"] = d * txs[1]
            o = o - here[b, "u"]
        if i == 0:
            for k, value in enumerate((o, ey, ez, here[b, "u"])):
                edge[4 + k] = value
        here[a, "u"] = o
        planes.append(here)
    before = {("N", "u"): own[NXL - 2], ("N", "v"): beside_y[NXL - 2], ("Z", "u"): beside_z[NXL - 2]}
    block.add_pairs(t_14, minus(before, planes[0]))
    block.add_plane(planes[0], below_15, ss[0], *known[0][:2], upper=False)
    block.add_source(planes[0], src[NXL - 1])
    block.add_pairs(txs[1], minus(planes[0], planes[1]))
    block.add_plane(planes[1], above_16, ss[1], *known[1][:2], has_right)
    block.add_pairs(txs[2] * has_right, minus(planes[1], planes[2]))
    sums = block.sums

    keys = inner_keys() + [key for key in sums if key not in inner_keys()]
    index = {key: i for i, key in enumerate(keys)}
    count = -(-len(keys) // 16) * 16
    for i in range(0, count, 8):
        here = [sums[key] for key in keys[i : i + 8]]
        value = row_sums(here) if here else jnp.zeros((8, NY), F32)
        lanes_ref[i : i + 8, :] = value + rows[i : i + 8, :] if i < 16 else value
    grouped = times_01(lanes_ref[0:count, :], select[...])
    gl = lax.broadcasted_iota(jnp.int32, (count, 128), 1)
    g_l_next = jnp.where(gl < NCY - 1, lane_roll(grouped, -(NCY + 1)), 0.0)
    g_r_next = jnp.where((gl > 0) & (gl < NCY), lane_roll(grouped, -(2 * NCY - 1)), 0.0)
    forms = {
        "all": jnp.where(gl < NCY, grouped, 0.0),
        "L": jnp.where(gl < NCY, lane_roll(grouped, -NCY), 0.0),
        "R": jnp.where(gl < NCY, lane_roll(grouped, -2 * NCY), 0.0),
        "Ls": g_l_next,
        "Rs": g_r_next,
        "vv": g_l_next + g_r_next,
    }
    at = {}
    for i, (name, value) in enumerate(forms.items()):
        at[name] = i
        g_ref[i, 0:count, :] = value

    def taken_rows(terms):
        total = None
        for name, key in terms:
            if key in index:
                q = index[key]
                row = g_ref[at[name], q : q + 1, :]
                total = row if total is None else total + row
        return total

    def terms_of(a, b, dy):
        au, av, bu, bv = (a, "u"), (a, "v"), (b, "u"), (b, "v")
        if a == b:
            if dy == 0:
                return [("all", pair(au, au)), ("vv", pair(av, av))]
            return [("Ls", pair(au, av)), ("R", pair(au, av))]
        if dy == 0:
            return [("all", pair(au, bu)), ("vv", pair(av, bv))]
        if dy < 0:
            return [("L", pair(au, bv)), ("Rs", pair(av, bu))]
        return [("R", pair(au, bv)), ("Ls", pair(av, bu))]

    nothing = jnp.zeros((1, 128), F32)
    out_ref[...] = jnp.zeros(out_ref.shape, F32)
    spots = [(where, k) for where in ("own", "near", "low") for k in range(NCZ)]
    for (where, key), (r, k) in SLOT.items():
        names = {"own": HERE, "near": BESIDE}.get(where)
        if key[0] == "s":
            row = taken_rows(terms_of(names[key[1]], names[key[2]], key[3]))
        elif key[0] == "r":
            node = "M" if key[1] < 0 else names[key[1]]
            row = taken_rows([("all", ("rhs", (node, "u"))), ("vv", ("rhs", (node, "v")))])
        else:
            when_odd = taken_rows(terms_of(HERE[key[1]], BESIDE[key[2]], key[3]))
            when_even = taken_rows(terms_of(BESIDE[key[1]], HERE[key[2]], key[3]))
            when_odd = nothing if when_odd is None else when_odd
            when_even = nothing if when_even is None else when_even
            row = jnp.where(odd_z, when_odd, when_even)
        if row is not None:
            out_ref[spots.index((where, k)), r : r + 1, :] = row
    cell = layer // 2
    near_cell = jnp.where(odd_z, cell + 1, cell - 1)
    coarse_layer = {"own": cell, "near": near_cell, "low": jnp.minimum(cell, near_cell)}
    group = lax.broadcasted_iota(jnp.int32, (ROWS, 128), 1) // NCY
    total = jnp.zeros((ROWS, 128), F32)
    for i, (where, k) in enumerate(spots):
        if (where, k) not in {(w, kk) for (w, _), (_, kk) in SLOT.items()}:
            continue
        rows = out_ref[i]
        spread = rows
        for n in range(1, NCZ):
            spread = spread + lane_roll(rows, n * NCY)
        total = total + jnp.where(group == (coarse_layer[where] + k + NCZ) % NCZ, spread, 0.0)
    for k in range(TILES * LAYERS):
        part[k] = total


def solve(rows, own, beside_y, beside_z, edge, spread, pressure):
    tile, layer = lax.axis_index("tile"), lax.axis_index("layer")
    odd_z = layer % 2 == 1
    cell = layer // 2
    near_cell = jnp.where(odd_z, cell + 1, cell - 1)
    shape = (TILES, 128)
    strip = lax.broadcasted_iota(jnp.int32, shape, 0)
    group = lax.broadcasted_iota(jnp.int32, shape, 1) // NCY
    lane_cell = group[0:1]

    loaded = {}

    def load(layer_from, row):
        if (layer_from, row) not in loaded:
            loaded[layer_from, row] = rows[pl.ds(layer_from * ROWS + row, TILES, stride=LAYERS * ROWS), :]
        return loaded[layer_from, row]

    by_shift = {}
    for (where, key), (row, k) in SLOT.items():
        found = []
        for l in range(LAYERS):
            z = cells_of(l)[where]
            if 0 <= z and max(cells_of(l)["own"], cells_of(l)["near"] if where != "own" else 0) < NCZ:
                found.append(jnp.where(group == (z + k) % NCZ, load(l, row), 0.0))
        total = total_of(found)
        by_shift[key, k] = by_shift[key, k] + total if (key, k) in by_shift else total
    terms = {}
    for (key, k), value in by_shift.items():
        value = lane_roll(value, -k * NCY) if k else value
        terms[key] = terms[key] + value if key in terms else value

    def from_last(value):
        return jnp.where(strip > 0, row_roll(value, 1), 0.0)

    half = {}
    for dy in (0, 1):
        half[0, 0, dy] = terms["s", 0, 0, dy] + from_last(terms["s", 1, 1, dy])
    for dy in (-1, 0, 1):
        half[1, 0, dy] = terms["s", 0, 1, dy]
        half[0, 1, dy] = terms["z", 0, 0, dy] + from_last(terms["z", 1, 1, dy])
        half[1, 1, dy] = terms["z", 0, 1, dy]
        half[-1, 1, dy] = from_last(terms["z", 1, 0, dy])
    back = jnp.where(strip < TILES - 1, row_roll(terms["r", -1], -1), 0.0)
    rhs = terms["r", 0] + from_last(terms["r", 1]) + back
    centre = half.pop((0, 0, 0))
    scale = COARSE_DAMPING / centre

    def shifted(value, dx, dz, dy):
        by = -(dz * NCY + dy)
        if by:
            value = lane_roll(value, by)
        return row_roll(value, -dx) if dx else value

    full = dict(half)
    for (dx, dz, dy), value in half.items():
        full[-dx, -dz, -dy] = shifted(value, -dx, -dz, -dy)
    coarse = scale * rhs
    for _ in range(SWEEPS - 1):
        applied = [centre * coarse]
        for dz in (-1, 0, 1):
            for dy in (-1, 0, 1):
                moved = shifted(coarse, 0, dz, dy)
                for dx in (-1, 0, 1):
                    if (dx, dz, dy) in full:
                        applied.append(full[dx, dz, dy] * shifted(moved, dx, 0, 0))
        coarse = coarse + scale * (rhs - total_of(applied))

    def strip_row(at):
        return jnp.sum(jnp.where(strip == at, coarse, 0.0), axis=0, keepdims=True)

    here = strip_row(tile)
    own_row = jnp.where(lane_cell == cell, here, 0.0)
    picked = [
        own_row,
        jnp.where(lane_cell == cell, strip_row(tile - 1), 0.0),
        jnp.where(lane_cell == cell, strip_row(tile + 1), 0.0),
        jnp.where(lane_cell == near_cell, here, 0.0),
        lane_roll(own_row, 1),
        lane_roll(own_row, -1),
        jnp.zeros((2, 128), F32),
    ]
    picked = jnp.concatenate(picked, axis=0)
    fine = times_01(picked, spread[...])
    lane = lax.broadcasted_iota(jnp.int32, (1, NY), 1) % EDGE
    near_y = jnp.where(lane == 0, fine[4:5], jnp.where(lane == EDGE - 1, fine[5:6], 0.0))
    for x in range(NXL):
        if x in (0, NXL - 1):
            first, row = (0, fine[1:2]) if x == 0 else (4, fine[2:3])
            value = edge[first] * fine[0:1] + edge[first + 1] * near_y + edge[first + 2] * fine[3:4] + edge[first + 3] * row
        else:
            value = own[x] * fine[0:1] + beside_y[x] * near_y + beside_z[x] * fine[3:4]
        pressure[x] = value


def struct(*shape):
    return jax.ShapeDtypeStruct(shape, F32)


def call(kernel, outs, scratch=(), **kw):
    many = isinstance(outs, (list, tuple))
    return pl.pallas_call(
        kernel,
        out_shape=outs,
        out_specs=[VMEM] * len(outs) if many else VMEM,
        scratch_shapes=list(scratch),
        compiler_params=pltpu.CompilerParams(vmem_limit_bytes=48 * 1024 * 1024),
        **kw,
    )


def body(classes, well_mask, source):
    def swap(values, axis):
        out = []
        for i, v in enumerate(values):
            out.append(lax.ppermute(v, ("tile", "layer"), swap_pairs(axis, i == 1)))
        return out

    block = struct(NXL, NZL, NY)
    ints = jax.ShapeDtypeStruct((NXL, NZL, NY), jnp.int32)
    z_message, x_message = struct(2, NXL, NY), struct(5, NZL, NY)
    z_b, z_a, x_b, x_a, cls, well = call(
        pack,
        [z_message, z_message, x_message, x_message, ints, ints],
        [pltpu.SemaphoreType.DMA((2,))],
        in_specs=[pl.BlockSpec(memory_space=pltpu.HBM)] * 2,
    )(*(pltpu.with_memory_space_constraint(v, pltpu.HBM) for v in (classes, well_mask)))
    z_b, z_a = swap((z_b, z_a), "layer")
    (x_b,) = swap((x_b,), "tile")
    x_out = call(pack_lines, [struct(NZL, NY), struct(6, NZL, NY)], in_specs=[VMEM] * 3)(x_a, z_b, z_a)
    line_b, x_a = swap(x_out, "tile")
    select, spread = jax.ShapeDtypeStruct((NY, 128), jnp.bfloat16), jax.ShapeDtypeStruct((128, NY), jnp.bfloat16)
    inner, own, beside_y, beside_z, aux, aux_rows, select, spread = call(
        assemble_inner,
        [struct(16, NY), block, block, block, struct(13, NZL, NY), struct(8, NY), select, spread],
        in_specs=[VMEM] * 5,
        cost_estimate=pl.CostEstimate(flops=10**7, bytes_accessed=2 * 10**6, transcendentals=10**5),
    )(cls, well, source, z_b, z_a)
    part, edge = call(
        assemble,
        [struct(TILES * LAYERS, ROWS, 128), struct(8, NZL, NY)],
        [pltpu.VMEM((64, NY), F32), pltpu.VMEM((6, 64, 128), F32), pltpu.VMEM((3 * NCZ, ROWS, 128), F32)],
        in_specs=[VMEM] * 13,
    )(source, z_b, z_a, line_b, x_b, x_a, inner, own, beside_y, beside_z, aux, aux_rows, select)
    received = lax.all_to_all(part, ("tile", "layer"), 0, 0, tiled=True)
    rows = received.reshape(TILES * LAYERS * ROWS, 128)
    return call(solve, block, in_specs=[VMEM] * 6)(rows, own, beside_y, beside_z, edge, spread)


def solution(mesh):
    spec = P("tile", "layer", None)
    return jax.shard_map(body, mesh=mesh, in_specs=(spec, spec, spec), out_specs=spec, check_vma=False)
```

```python
import jax
import jax.numpy as jnp
from jax import lax
from jax.experimental import pallas as pl
from jax.experimental.pallas import tpu as pltpu
from jax.sharding import PartitionSpec as P

EDGE = 16
SWEEPS = 4
FINE_DAMPING = 0.67
COARSE_DAMPING = 0.5
NXL, NZL, NY = 16, 8, 512
TILES, LAYERS = 16, 8
NCY = NY // EDGE
NCZ = LAYERS * NZL // EDGE
ROWS = 8
HALF = TILES * LAYERS // 2
F32 = jnp.float32
VMEM = pl.BlockSpec(memory_space=pltpu.VMEM)

NODES = ("N", "Q", "Z", "QZ")


def order(key):
    return NODES.index(key[0]) * 2 + (key[1] == "v")


def pair(a, b):
    return (a, b) if order(a) <= order(b) else (b, a)


SLOT = {}
for where, row in (("own", 0), ("near", 2)):
    for i, key in enumerate(
        [("s", 0, 0, 0), ("s", 0, 0, 1), ("s", 1, 1, 0), ("s", 1, 1, 1)]
        + [("s", 0, 1, -1), ("s", 0, 1, 0), ("s", 0, 1, 1), ("r", 0)]
    ):
        SLOT[where, key] = (row + i // 4, i % 4)
SLOT["own", ("r", 1)] = (7, 0)
SLOT["own", ("r", -1)] = (7, 1)
for i, (lo, hi, dy) in enumerate((lo, hi, dy) for lo in (0, 1) for hi in (0, 1) for dy in (-1, 0, 1)):
    SLOT["low", ("z", lo, hi, dy)] = (4 + i // 4, i % 4)
HERE = ("N", "Q")
BESIDE = ("Z", "QZ")


def cells_of(layer):
    own = layer // 2
    near = own + 1 if layer % 2 else own - 1
    return {"own": own, "near": near, "low": min(own, near)}


def swap_pairs(axis, first):
    pairs = []
    for tile in range(TILES):
        for layer in range(LAYERS):
            at, count = (tile, TILES) if axis == "tile" else (layer, LAYERS)
            if first:
                to = at ^ 1
            else:
                to = at if at in (0, count - 1) else ((at + 1) ^ 1) - 1
            partner = (to, layer) if axis == "tile" else (tile, to)
            if to == at:
                partner = (tile, layer ^ 1) if axis == "tile" else (tile ^ 1, layer)
            pairs.append((tile * LAYERS + layer, partner[0] * LAYERS + partner[1]))
    return pairs


def pack(cls_hbm, well_hbm, z_b, z_a, x_b, x_a, cls, well, sems):
    copies = [pltpu.make_async_copy(cls_hbm, cls, sems.at[0]), pltpu.make_async_copy(well_hbm, well, sems.at[1])]
    for copy in copies:
        copy.start()
    for copy in copies:
        copy.wait()

    def both(first, last, odd, b, a):
        a[0] = jnp.where(odd, first, last)
        b[0] = jnp.where(odd, last, first)

    odd_z = lax.axis_index("layer") % 2 == 1
    odd_x = lax.axis_index("tile") % 2 == 1
    low, high = slice(0, 8), slice(8, NXL)
    down = [cls[:, 0, :], jnp.concatenate([cls[low, 1, :], well[low, 0, :]], axis=0)]
    up = [cls[:, NZL - 1, :], jnp.concatenate([cls[high, NZL - 2, :], well[high, NZL - 1, :]], axis=0)]
    for i in range(2):
        both(down[i].astype(F32), up[i].astype(F32), odd_z, z_b.at[i : i + 1], z_a.at[i : i + 1])
    both(cls[0].astype(F32), cls[NXL - 1].astype(F32), odd_x, x_b, x_a)
    for out in (x_b, x_a):
        out[1] = cls[1].astype(F32)
        out[2] = cls[2].astype(F32)
        out[3] = well[0].astype(F32)
        out[4] = well[1].astype(F32)


def pack_lines(old_a, z_b, z_a, lines, x_a):
    odd_z = lax.axis_index("layer") % 2 == 1

    def head(ref, plane, first=0):
        return ref[plane, first : first + 8, :]

    up = [jnp.where(odd_z, head(z_b, *at), head(z_a, *at)) for at in ((0, 0), (1, 0), (1, 8))]
    down = jnp.where(odd_z, head(z_a, 0), head(z_b, 0))
    rows = [down[0:1], down[1:2], up[0][0:1], up[0][1:2], up[1][0:1], up[2][0:1], jnp.zeros((2, NY), F32)]
    rows = jnp.concatenate(rows, axis=0)
    lines[...] = rows
    for i in range(5):
        x_a[i] = old_a[i]
    x_a[5] = rows


def lane_roll(value, by):
    return pltpu.roll(value, by % value.shape[-1], value.ndim - 1)


def row_roll(value, by):
    return pltpu.roll(value, by % value.shape[0], 0)


def resist(c):
    return jnp.exp(2.5 - c * F32(1.0 / 3.0))


def sink(c, w):
    return 0.5 * w * jnp.exp(c * F32(1.0 / 3.0) - 2.5)


def y_faces(r):
    ty = 2.0 / (r + lane_roll(r, -1))
    ty = jnp.where(lax.broadcasted_iota(jnp.int32, r.shape, 1) < NY - 1, ty, 0.0)
    return ty, lane_roll(ty, 1)


def y_part(ty, ty_lo):
    at = lax.broadcasted_iota(jnp.int32, ty.shape, 1) % EDGE
    return jnp.where(at == 0, ty_lo, jnp.where(at == EDGE - 1, ty, 0.0))


def basis(s, others, leave_y, leave_z, tx_lo, tx_hi):
    d = FINE_DAMPING / (s + others + tx_lo + tx_hi)
    ey, ez = d * leave_y, d * leave_z
    return 1.0 - d * s - ey - ez, ey, ez, d


def three(value):
    pieces = []
    for _ in range(3):
        piece = value.astype(jnp.bfloat16)
        pieces.append(piece)
        value = value - piece.astype(F32)
    return jnp.concatenate(pieces, axis=0)


def times_01(value, matrix):
    n = value.shape[0]
    out = jnp.dot(three(value), matrix, preferred_element_type=F32)
    return out[0:n] + (out[n : 2 * n] + out[2 * n : 3 * n])


def row_sums(arrays):
    row = lax.broadcasted_iota(jnp.int32, arrays[0].shape, 0)
    arrays = list(arrays) + [jnp.zeros(arrays[0].shape, F32)] * (8 - len(arrays))
    arrays = [arrays[i] for i in (0, 4, 2, 6, 1, 5, 3, 7)]
    for bit in (4, 2, 1):
        low = row // bit % 2 == 0
        merged = []
        for a, b in zip(arrays[::2], arrays[1::2]):
            keep, move = jnp.where(low, a, b), jnp.where(low, b, a)
            moved = row_roll(move, 4) if bit == 4 else jnp.where(low, row_roll(move, -bit), row_roll(move, bit))
            merged.append(keep + moved)
        arrays = merged
    return arrays[0]


def total_of(values):
    values = list(values)
    while len(values) > 1:
        values = [a + b for a, b in zip(values[::2], values[1::2])] + ([values[-1]] if len(values) % 2 else [])
    return values[0]


def minus(a, b):
    out = {}
    for key in {**a, **b}:
        if key in a and key in b:
            out[key] = a[key] - b[key]
        else:
            out[key] = a[key] if key in a else -b[key]
    return out


COLUMNS = (("N", "Z"), ("Q", "QZ"))


class Block:
    def __init__(self, z_b, z_a):
        self.tile, self.layer = lax.axis_index("tile"), lax.axis_index("layer")
        self.odd_z, self.odd_x = self.layer % 2 == 1, self.tile % 2 == 1
        self.has_up, self.has_down = (self.layer < LAYERS - 1).astype(F32), (self.layer > 0).astype(F32)
        self.has_right, self.has_left = (self.tile < TILES - 1).astype(F32), (self.tile > 0).astype(F32)
        self.plane = (NZL, NY)
        self.zrow = lax.broadcasted_iota(jnp.int32, self.plane, 0)
        self.m_r = lax.broadcasted_iota(jnp.int32, self.plane, 1) % EDGE == EDGE - 1
        self.at_zb = self.zrow == jnp.where(self.odd_z, NZL - 1, 0)
        self.up_mask = jnp.where(self.zrow == NZL - 1, self.has_up, 1.0)
        self.down_mask = jnp.where(self.zrow == 0, self.has_down, 1.0)
        self.sums = {}
        self.z_b, self.z_a = z_b, z_a

    def beyond(self, up):
        first, second = (self.z_b, self.z_a) if up else (self.z_a, self.z_b)
        planes = [jnp.where(self.odd_z, first[i], second[i]) for i in range(2)]
        return planes[0], planes[1][0:8], planes[1][8:16]

    def last_row(self, row, value):
        return jnp.where(self.zrow == NZL - 1, jnp.broadcast_to(row, self.plane), value)

    def known(self, r, below, over, upper=True):
        r_up = self.last_row(over, row_roll(r, -1))
        r_dn = jnp.where(self.zrow == 0, jnp.broadcast_to(below, self.plane), row_roll(r, 1))
        tz_hi, tz_lo = 0.5 / (r + r_up) * self.up_mask, 0.5 / (r + r_dn) * self.down_mask
        ty, ty_lo = y_faces(r)
        leave_z = jnp.where(self.at_zb, jnp.where(self.odd_z, tz_hi, tz_lo), 0.0)
        others = tz_hi + tz_lo + ty + ty_lo
        return tz_hi if upper else row_roll(tz_lo, -1), ty, others, y_part(ty, ty_lo), leave_z

    def crosses(self, upper):
        return self.odd_z if upper else ~self.odd_z

    def outer(self, r_edge, r, r_next, upper=True):
        t_edge, t_next = 0.5 / (r_edge + r) * (self.has_up if upper else self.has_down), 0.5 / (r + r_next)
        ty, ty_lo = y_faces(r)
        return t_edge + t_next + ty + ty_lo, y_part(ty, ty_lo), jnp.where(self.crosses(upper), t_edge, 0.0)

    def held(self, o, ey, ez, other=None, columns=COLUMNS, upper=True):
        (a, az), (b, bz) = columns
        crosses = self.crosses(upper)
        out = {
            (a, "u"): jnp.where(crosses, ez, o),
            (a, "v"): jnp.where(crosses, 0.0, ey),
            (az, "u"): jnp.where(crosses, o, 0.0),
            (az, "v"): jnp.where(crosses, ey, 0.0),
        }
        if other is not None:
            out[b, "u"] = jnp.where(crosses, 0.0, other)
            out[bz, "u"] = jnp.where(crosses, other, 0.0)
        return out

    def add(self, key, value):
        self.sums[key] = self.sums[key] + value if key in self.sums else value

    def add_pairs(self, weight, values):
        keys = sorted(values, key=order)
        for i, a in enumerate(keys):
            scaled = weight * values[a]
            for b in keys[i:]:
                self.add((a, b), scaled * values[b])

    def add_source(self, here, source):
        for key, value in here.items():
            self.add(("rhs", key), value * source)

    def add_plane(self, here, outer, s, tz, ty, counted=None, upper=True):
        if counted is not None:
            s, tz, ty = s * counted, tz * counted, ty * counted
        self.add_pairs(s, here)
        near, there = dict(here), {key: row_roll(value, -1) for key, value in here.items()}
        changed = there if upper else near
        for key, row in outer.items():
            changed[key] = self.last_row(row, changed.get(key, 0.0))
        self.add_pairs(tz, minus(near, there))
        rolled = {key: lane_roll(value, -1) for key, value in here.items()}
        there = {}
        for node in {key[0]: None for key in here}:
            u, v = rolled.get((node, "u"), 0.0), rolled.get((node, "v"), 0.0)
            there[node, "u"] = jnp.where(self.m_r, v, u)
            there[node, "v"] = jnp.where(self.m_r, u, v)
        self.add_pairs(ty, minus(here, there))


def inner_keys():
    held = [("N", "u"), ("N", "v"), ("Z", "u"), ("Z", "v")]
    keys = [(a, b) for i, a in enumerate(held) for b in held[i:]]
    return keys + [("rhs", key) for key in held[:3]]


def assemble_inner(cls, well, src, z_b, z_a, rows, own, beside_y, beside_z, aux, aux_rows, select, spread):
    block = Block(z_b, z_a)
    last, half = NXL - 1, NXL // 2
    r8, rm = None, None
    outers = []
    for upper in (True, False):
        adjacent, after, wells = block.beyond(upper)
        rows_here = slice(0, half) if upper else slice(half, NXL)
        r_all = resist(adjacent)
        r, s = r_all[rows_here], sink(adjacent[rows_here], wells)
        r_edge = resist(cls[rows_here, NZL - 1 if upper else 0, :].astype(F32))
        others, leave_y, leave_z = block.outer(r_edge, r, resist(after), upper)
        tx_lo = 2.0 / (r + row_roll(r_all, 1)[rows_here])
        if upper:
            tx_lo = jnp.where(lax.broadcasted_iota(jnp.int32, r.shape, 0) == 0, 0.0, tx_lo)
        o, ey, ez, _ = basis(s, others, leave_y, leave_z, tx_lo, 2.0 / (r + row_roll(r_all, -1)[rows_here]))
        held = block.held(o, ey, ez, upper=upper)
        outers += [{key: value[x : x + 1] for key, value in held.items()} for x in range(half)]
        if upper:
            r8 = r_all
        else:
            rm = r_all
            for i, value in enumerate((s, others + tx_lo, leave_y, leave_z, r)):
                aux_rows[i : i + 1, :] = value[half - 1 : half]
    aux_rows[5:6, :] = r8[last:NXL]
    aux_rows[6:8, :] = jnp.zeros((2, NY), F32)
    rs = [resist(cls[x].astype(F32)) for x in range(NXL)]
    txs = [jnp.zeros(block.plane, F32)] + [2.0 / (rs[x] + rs[x + 1]) for x in range(last)]
    first = 1.0 - block.has_left
    before = None
    for x in range(NXL):
        s = sink(cls[x].astype(F32), well[x].astype(F32))
        upper = x < half
        tz, ty, others, leave_y, leave_z = block.known(rs[x], rm[x : x + 1], r8[x : x + 1], upper)
        if x == 0:
            for i, value in enumerate((s, others + txs[1], leave_y, leave_z, rs[x])):
                aux[i] = value
        if x == last:
            for i, value in enumerate((s, others + txs[last], leave_y, leave_z, rs[x], tz, ty, txs[last])):
                aux[5 + i] = value
            break
        o, ey, ez, _ = basis(s, others, leave_y, leave_z, txs[x], txs[x + 1])
        own[x] = o
        beside_y[x] = ey
        beside_z[x] = ez
        here = {("N", "u"): o, ("N", "v"): ey, ("Z", "u"): ez}
        block.add_plane(here, outers[x], s, tz, ty, first if x == 0 else None, upper)
        if x:
            block.add_source(here, src[x])
            block.add_pairs(txs[x] * first if x == 1 else txs[x], minus(before, here))
        before = here
    keys = inner_keys()
    for i in range(0, len(keys), 8):
        rows[i : i + 8, :] = row_sums([block.sums[key] for key in keys[i : i + 8]])

    j = lax.broadcasted_iota(jnp.int32, (NY, 128), 0)
    n = lax.broadcasted_iota(jnp.int32, (NY, 128), 1)
    group, pos = n // NCY, j % EDGE
    taken = (group == 0) | ((group == 1) & (pos == 0)) | ((group == 2) & (pos >= EDGE - 2))
    select[...] = jnp.where((j // EDGE == n % NCY) & taken, 1.0, 0.0).astype(jnp.bfloat16)
    i = lax.broadcasted_iota(jnp.int32, (128, NY), 0)
    j = lax.broadcasted_iota(jnp.int32, (128, NY), 1)
    spread[...] = jnp.where(i % NCY == j // EDGE, 1.0, 0.0).astype(jnp.bfloat16)


def assemble(
    src, z_b, z_a, line_b, x_b, x_a, rows, own, beside_y, beside_z, aux, aux_rows, select, part, edge, lanes_ref, g_ref, out_ref
):
    block = Block(z_b, z_a)
    layer, odd_z, has_right, last_row = block.layer, block.odd_z, block.has_right, slice(NZL - 1, NZL)
    right = [jnp.where(block.odd_x, x_b[i], x_a[i]) for i in range(5)]
    right.append(jnp.where(block.odd_x, line_b[...], x_a[5]))
    left = jnp.where(block.odd_x, x_a[0], x_b[0])
    lines, lines_r = right[5], resist(right[5])

    tx = 2.0 / (aux_rows[4:5] + lines_r[0:1]) * has_right
    o, ey, ez, d = basis(*(aux_rows[i : i + 1] for i in range(4)), 0.0, tx)
    below_15 = block.held(o - d * tx, ey, ez, d * tx, upper=False)
    r8_15, r8_16, r8_17, r9_16 = aux_rows[5:6], lines_r[2:3], lines_r[3:4], lines_r[4:5]
    tx = 2.0 / (r8_15 + r8_16) * has_right
    rs = [aux[9]] + [resist(right[i]) for i in range(3)]
    o, ey, ez, d = basis(
        sink(lines[2:3], lines[5:6]), *block.outer(rs[1][last_row], r8_16, r9_16), tx, 2.0 / (r8_16 + r8_17)
    )
    above_16 = block.held(o - d * tx, ey, ez, d * tx, COLUMNS[::-1])

    t_left = 2.0 / (resist(left) + aux[4]) * block.has_left
    o, ey, ez, d = basis(*(aux[i] for i in range(4)), t_left, 0.0)
    o, ex = o - d * t_left, d * t_left
    for i, value in enumerate((o, ey, ez, ex)):
        edge[i] = value
    block.add_source({("N", "u"): o, ("N", "v"): ey, ("Z", "u"): ez, ("M", "u"): ex}, src[0])

    t_14 = aux[12]
    txs = [0.0, 2.0 / (rs[0] + rs[1]) * has_right, 2.0 / (rs[1] + rs[2]), 2.0 / (rs[2] + rs[3])]
    known = [(aux[10], aux[11], aux[6], aux[7], aux[8])]
    known += [block.known(rs[i], lines_r[i - 1 : i], (r8_16, r8_17)[i - 1]) for i in (1, 2)]
    ss = [aux[5]] + [sink(right[i], right[3 + i]) for i in range(2)]
    planes = []
    for i in range(3):
        o, ey, ez, d = basis(ss[i], *known[i][2:], txs[i], txs[i + 1])
        (a, az), (b, _) = COLUMNS if i == 0 else COLUMNS[::-1]
        here = {(a, "v"): ey, (az, "u"): ez}
        if i < 2:
            here[b, "u"] = d * txs[1]
            o = o - here[b, "u"]
        if i == 0:
            for k, value in enumerate((o, ey, ez, here[b, "u"])):
                edge[4 + k] = value
        here[a, "u"] = o
        planes.append(here)
    before = {("N", "u"): own[NXL - 2], ("N", "v"): beside_y[NXL - 2], ("Z", "u"): beside_z[NXL - 2]}
    block.add_pairs(t_14, minus(before, planes[0]))
    block.add_plane(planes[0], below_15, ss[0], *known[0][:2], upper=False)
    block.add_source(planes[0], src[NXL - 1])
    block.add_pairs(txs[1], minus(planes[0], planes[1]))
    block.add_plane(planes[1], above_16, ss[1], *known[1][:2], has_right)
    block.add_pairs(txs[2] * has_right, minus(planes[1], planes[2]))
    sums = block.sums

    keys = inner_keys() + [key for key in sums if key not in inner_keys()]
    index = {key: i for i, key in enumerate(keys)}
    count = -(-len(keys) // 16) * 16
    for i in range(0, count, 8):
        here = [sums[key] for key in keys[i : i + 8]]
        value = row_sums(here) if here else jnp.zeros((8, NY), F32)
        lanes_ref[i : i + 8, :] = value + rows[i : i + 8, :] if i < 16 else value
    grouped = times_01(lanes_ref[0:count, :], select[...])
    gl = lax.broadcasted_iota(jnp.int32, (count, 128), 1)
    g_l_next = jnp.where(gl < NCY - 1, lane_roll(grouped, -(NCY + 1)), 0.0)
    g_r_next = jnp.where((gl > 0) & (gl < NCY), lane_roll(grouped, -(2 * NCY - 1)), 0.0)
    forms = {
        "all": jnp.where(gl < NCY, grouped, 0.0),
        "L": jnp.where(gl < NCY, lane_roll(grouped, -NCY), 0.0),
        "R": jnp.where(gl < NCY, lane_roll(grouped, -2 * NCY), 0.0),
        "Ls": g_l_next,
        "Rs": g_r_next,
        "vv": g_l_next + g_r_next,
    }
    at = {}
    for i, (name, value) in enumerate(forms.items()):
        at[name] = i
        g_ref[i, 0:count, :] = value

    def taken_rows(terms):
        total = None
        for name, key in terms:
            if key in index:
                q = index[key]
                row = g_ref[at[name], q : q + 1, :]
                total = row if total is None else total + row
        return total

    def terms_of(a, b, dy):
        au, av, bu, bv = (a, "u"), (a, "v"), (b, "u"), (b, "v")
        if a == b:
            if dy == 0:
                return [("all", pair(au, au)), ("vv", pair(av, av))]
            return [("Ls", pair(au, av)), ("R", pair(au, av))]
        if dy == 0:
            return [("all", pair(au, bu)), ("vv", pair(av, bv))]
        if dy < 0:
            return [("L", pair(au, bv)), ("Rs", pair(av, bu))]
        return [("R", pair(au, bv)), ("Ls", pair(av, bu))]

    nothing = jnp.zeros((1, 128), F32)
    out_ref[...] = jnp.zeros(out_ref.shape, F32)
    spots = [(where, k) for where in ("own", "near", "low") for k in range(NCZ)]
    for (where, key), (r, k) in SLOT.items():
        names = {"own": HERE, "near": BESIDE}.get(where)
        if key[0] == "s":
            row = taken_rows(terms_of(names[key[1]], names[key[2]], key[3]))
        elif key[0] == "r":
            node = "M" if key[1] < 0 else names[key[1]]
            row = taken_rows([("all", ("rhs", (node, "u"))), ("vv", ("rhs", (node, "v")))])
        else:
            when_odd = taken_rows(terms_of(HERE[key[1]], BESIDE[key[2]], key[3]))
            when_even = taken_rows(terms_of(BESIDE[key[1]], HERE[key[2]], key[3]))
            when_odd = nothing if when_odd is None else when_odd
            when_even = nothing if when_even is None else when_even
            row = jnp.where(odd_z, when_odd, when_even)
        if row is not None:
            out_ref[spots.index((where, k)), r : r + 1, :] = row
    cell = layer // 2
    near_cell = jnp.where(odd_z, cell + 1, cell - 1)
    coarse_layer = {"own": cell, "near": near_cell, "low": jnp.minimum(cell, near_cell)}
    group = lax.broadcasted_iota(jnp.int32, (ROWS, 128), 1) // NCY
    total = jnp.zeros((ROWS, 128), F32)
    for i, (where, k) in enumerate(spots):
        if (where, k) not in {(w, kk) for (w, _), (_, kk) in SLOT.items()}:
            continue
        rows = out_ref[i]
        spread = rows
        for n in range(1, NCZ):
            spread = spread + lane_roll(rows, n * NCY)
        total = total + jnp.where(group == (coarse_layer[where] + k + NCZ) % NCZ, spread, 0.0)
    for k in range(HALF):
        part[k] = total


TERMS = list(dict.fromkeys(key for _, key in SLOT))


def unpacked(rows):
    group = lax.broadcasted_iota(jnp.int32, (TILES // 2, 128), 1) // NCY
    loaded = {}

    def load(layer_from, row):
        if (layer_from, row) not in loaded:
            loaded[layer_from, row] = rows[pl.ds(layer_from * ROWS + row, TILES // 2, stride=LAYERS * ROWS), :]
        return loaded[layer_from, row]

    by_shift = {}
    for (where, key), (row, k) in SLOT.items():
        found = []
        for l in range(LAYERS):
            z = cells_of(l)[where]
            if 0 <= z and max(cells_of(l)["own"], cells_of(l)["near"] if where != "own" else 0) < NCZ:
                found.append(jnp.where(group == (z + k) % NCZ, load(l, row), 0.0))
        by_shift.setdefault((key, k), []).append(total_of(found))
    terms = {}
    for (key, k), values in by_shift.items():
        value = total_of(values)
        value = lane_roll(value, -k * NCY) if k else value
        terms[key] = terms[key] + value if key in terms else value
    return terms


def unpack(rows, out):
    for key, value in unpacked(rows).items():
        out[TERMS.index(key)] = value


def solve(mine, rows, own, beside_y, beside_z, edge, spread, pressure):
    tile, layer = lax.axis_index("tile"), lax.axis_index("layer")
    odd_z, odd_x = layer % 2 == 1, tile % 2 == 1
    cell = layer // 2
    near_cell = jnp.where(odd_z, cell + 1, cell - 1)
    row = lax.broadcasted_iota(jnp.int32, (TILES, 128), 0)
    strip = row % 8 * 2 + row // 8
    lane_cell = lax.broadcasted_iota(jnp.int32, (1, 128), 1) // NCY
    terms = {}
    for key, other in unpacked(rows).items():
        here = mine[TERMS.index(key)]
        terms[key] = jnp.concatenate([jnp.where(odd_x, other, here), jnp.where(odd_x, here, other)], axis=0)

    def strips_on(value, by):
        even, odd = value[0:8], value[8:16]
        if by > 0:
            return jnp.concatenate([odd, row_roll(even, -1)], axis=0)
        return jnp.concatenate([row_roll(odd, 1), even], axis=0)

    def from_last(value):
        return jnp.where(strip > 0, strips_on(value, -1), 0.0)

    half = {}
    for dy in (0, 1):
        half[0, 0, dy] = terms["s", 0, 0, dy] + from_last(terms["s", 1, 1, dy])
    for dy in (-1, 0, 1):
        half[1, 0, dy] = terms["s", 0, 1, dy]
        half[0, 1, dy] = terms["z", 0, 0, dy] + from_last(terms["z", 1, 1, dy])
        half[1, 1, dy] = terms["z", 0, 1, dy]
        half[-1, 1, dy] = from_last(terms["z", 1, 0, dy])
    back = jnp.where(strip < TILES - 1, strips_on(terms["r", -1], 1), 0.0)
    rhs = terms["r", 0] + from_last(terms["r", 1]) + back
    centre = half.pop((0, 0, 0))
    scale = COARSE_DAMPING / centre

    def shifted(value, dx, dz, dy):
        by = -(dz * NCY + dy)
        if by:
            value = lane_roll(value, by)
        return strips_on(value, dx) if dx else value

    full = dict(half)
    for (dx, dz, dy), value in half.items():
        full[-dx, -dz, -dy] = shifted(value, -dx, -dz, -dy)
    coarse = scale * rhs
    for _ in range(SWEEPS - 1):
        applied = [centre * coarse]
        for dz in (-1, 0, 1):
            for dy in (-1, 0, 1):
                moved = shifted(coarse, 0, dz, dy)
                for dx in (-1, 0, 1):
                    if (dx, dz, dy) in full:
                        applied.append(full[dx, dz, dy] * shifted(moved, dx, 0, 0))
        coarse = coarse + scale * (rhs - total_of(applied))

    def strip_row(at):
        return jnp.sum(jnp.where(strip == at, coarse, 0.0), axis=0, keepdims=True)

    here = strip_row(tile)
    own_row = jnp.where(lane_cell == cell, here, 0.0)
    picked = [
        own_row,
        jnp.where(lane_cell == cell, strip_row(tile - 1), 0.0),
        jnp.where(lane_cell == cell, strip_row(tile + 1), 0.0),
        jnp.where(lane_cell == near_cell, here, 0.0),
        lane_roll(own_row, 1),
        lane_roll(own_row, -1),
        jnp.zeros((2, 128), F32),
    ]
    picked = jnp.concatenate(picked, axis=0)
    fine = times_01(picked, spread[...])
    lane = lax.broadcasted_iota(jnp.int32, (1, NY), 1) % EDGE
    near_y = jnp.where(lane == 0, fine[4:5], jnp.where(lane == EDGE - 1, fine[5:6], 0.0))
    for x in range(NXL):
        if x in (0, NXL - 1):
            first, row = (0, fine[1:2]) if x == 0 else (4, fine[2:3])
            value = edge[first] * fine[0:1] + edge[first + 1] * near_y + edge[first + 2] * fine[3:4] + edge[first + 3] * row
        else:
            value = own[x] * fine[0:1] + beside_y[x] * near_y + beside_z[x] * fine[3:4]
        pressure[x] = value


def struct(*shape):
    return jax.ShapeDtypeStruct(shape, F32)


def call(kernel, outs, scratch=(), **kw):
    many = isinstance(outs, (list, tuple))
    return pl.pallas_call(
        kernel,
        out_shape=outs,
        out_specs=[VMEM] * len(outs) if many else VMEM,
        scratch_shapes=list(scratch),
        compiler_params=pltpu.CompilerParams(vmem_limit_bytes=48 * 1024 * 1024),
        **kw,
    )


def body(classes, well_mask, source):
    def swap(values, axis, near=False):
        out = []
        for i, v in enumerate(values):
            out.append(lax.ppermute(v, ("tile", "layer"), swap_pairs(axis, near or i == 1)))
        return out

    block = struct(NXL, NZL, NY)
    ints = jax.ShapeDtypeStruct((NXL, NZL, NY), jnp.int32)
    z_message, x_message = struct(2, NXL, NY), struct(5, NZL, NY)
    z_b, z_a, x_b, x_a, cls, well = call(
        pack,
        [z_message, z_message, x_message, x_message, ints, ints],
        [pltpu.SemaphoreType.DMA((2,))],
        in_specs=[pl.BlockSpec(memory_space=pltpu.HBM)] * 2,
    )(*(pltpu.with_memory_space_constraint(v, pltpu.HBM) for v in (classes, well_mask)))
    z_b, z_a = swap((z_b, z_a), "layer")
    (x_b,) = swap((x_b,), "tile")
    x_out = call(pack_lines, [struct(NZL, NY), struct(6, NZL, NY)], in_specs=[VMEM] * 3)(x_a, z_b, z_a)
    line_b, x_a = swap(x_out, "tile")
    select, spread = jax.ShapeDtypeStruct((NY, 128), jnp.bfloat16), jax.ShapeDtypeStruct((128, NY), jnp.bfloat16)
    inner, own, beside_y, beside_z, aux, aux_rows, select, spread = call(
        assemble_inner,
        [struct(16, NY), block, block, block, struct(13, NZL, NY), struct(8, NY), select, spread],
        in_specs=[VMEM] * 5,
        cost_estimate=pl.CostEstimate(flops=10**7, bytes_accessed=2 * 10**6, transcendentals=10**5),
    )(cls, well, source, z_b, z_a)
    part, edge = call(
        assemble,
        [struct(HALF, ROWS, 128), struct(8, NZL, NY)],
        [pltpu.VMEM((64, NY), F32), pltpu.VMEM((6, 64, 128), F32), pltpu.VMEM((3 * NCZ, ROWS, 128), F32)],
        in_specs=[VMEM] * 13,
    )(source, z_b, z_a, line_b, x_b, x_a, inner, own, beside_y, beside_z, aux, aux_rows, select)
    halves = [[(2 * k + core) * LAYERS + l for k in range(TILES // 2) for l in range(LAYERS)] for core in (0, 1)]
    mine = lax.all_to_all(part, ("tile", "layer"), 0, 0, axis_index_groups=halves, tiled=True)
    (other,) = swap((mine,), "tile", True)
    mine = call(
        unpack,
        struct(len(TERMS), TILES // 2, 128),
        in_specs=[VMEM],
        cost_estimate=pl.CostEstimate(flops=10**6, bytes_accessed=10**6, transcendentals=0),
    )(mine.reshape(HALF * ROWS, 128))
    rows = other.reshape(HALF * ROWS, 128)
    return call(solve, block, in_specs=[VMEM] * 7)(mine, rows, own, beside_y, beside_z, edge, spread)


def solution(mesh):
    spec = P("tile", "layer", None)
    return jax.shard_map(body, mesh=mesh, in_specs=(spec, spec, spec), out_specs=spec, check_vma=False)
```

```python
import jax
import jax.numpy as jnp
from jax import lax
from jax.experimental import pallas as pl
from jax.experimental.pallas import tpu as pltpu
from jax.sharding import PartitionSpec as P

EDGE = 16
SWEEPS = 4
FINE_DAMPING = 0.67
COARSE_DAMPING = 0.5
NXL, NZL, NY = 16, 8, 512
TILES, LAYERS = 16, 8
NCY = NY // EDGE
NCZ = LAYERS * NZL // EDGE
ROWS = 8
HALF = TILES * LAYERS // 2
F32 = jnp.float32
VMEM = pl.BlockSpec(memory_space=pltpu.VMEM)

NODES = ("N", "Q", "Z", "QZ")


def order(key):
    return NODES.index(key[0]) * 2 + (key[1] == "v")


def pair(a, b):
    return (a, b) if order(a) <= order(b) else (b, a)


SLOT = {}
for where, row in (("own", 0), ("near", 2)):
    for i, key in enumerate(
        [("s", 0, 0, 0), ("s", 0, 0, 1), ("s", 1, 1, 0), ("s", 1, 1, 1)]
        + [("s", 0, 1, -1), ("s", 0, 1, 0), ("s", 0, 1, 1), ("r", 0)]
    ):
        SLOT[where, key] = (row + i // 4, i % 4)
SLOT["own", ("r", 1)] = (7, 0)
SLOT["own", ("r", -1)] = (7, 1)
for i, (lo, hi, dy) in enumerate((lo, hi, dy) for lo in (0, 1) for hi in (0, 1) for dy in (-1, 0, 1)):
    SLOT["low", ("z", lo, hi, dy)] = (4 + i // 4, i % 4)
HERE = ("N", "Q")
BESIDE = ("Z", "QZ")


def cells_of(layer):
    own = layer // 2
    near = own + 1 if layer % 2 else own - 1
    return {"own": own, "near": near, "low": min(own, near)}


def swap_pairs(axis, first):
    pairs = []
    for tile in range(TILES):
        for layer in range(LAYERS):
            at, count = (tile, TILES) if axis == "tile" else (layer, LAYERS)
            if first:
                to = at ^ 1
            else:
                to = at if at in (0, count - 1) else ((at + 1) ^ 1) - 1
            partner = (to, layer) if axis == "tile" else (tile, to)
            if to == at:
                partner = (tile, layer ^ 1) if axis == "tile" else (tile ^ 1, layer)
            pairs.append((tile * LAYERS + layer, partner[0] * LAYERS + partner[1]))
    return pairs


def pack(cls_hbm, well_hbm, z_b, z_a, x_b, x_a, cls, well, sems):
    copies = [pltpu.make_async_copy(cls_hbm, cls, sems.at[0]), pltpu.make_async_copy(well_hbm, well, sems.at[1])]
    for copy in copies:
        copy.start()
    for copy in copies:
        copy.wait()

    def both(first, last, odd, b, a):
        a[0] = jnp.where(odd, first, last)
        b[0] = jnp.where(odd, last, first)

    odd_z = lax.axis_index("layer") % 2 == 1
    odd_x = lax.axis_index("tile") % 2 == 1
    low, high = slice(0, 8), slice(8, NXL)
    down = [cls[:, 0, :], jnp.concatenate([cls[low, 1, :], well[low, 0, :]], axis=0)]
    up = [cls[:, NZL - 1, :], jnp.concatenate([cls[high, NZL - 2, :], well[high, NZL - 1, :]], axis=0)]
    for i in range(2):
        both(down[i].astype(F32), up[i].astype(F32), odd_z, z_b.at[i : i + 1], z_a.at[i : i + 1])
    both(cls[0].astype(F32), cls[NXL - 1].astype(F32), odd_x, x_b, x_a)
    for out in (x_b, x_a):
        out[1] = cls[1].astype(F32)
        out[2] = cls[2].astype(F32)
        out[3] = well[0].astype(F32)
        out[4] = well[1].astype(F32)


def pack_lines(old_a, z_b, z_a, lines, x_a):
    odd_z = lax.axis_index("layer") % 2 == 1

    def head(ref, plane, first=0):
        return ref[plane, first : first + 8, :]

    up = [jnp.where(odd_z, head(z_b, *at), head(z_a, *at)) for at in ((0, 0), (1, 0), (1, 8))]
    down = jnp.where(odd_z, head(z_a, 0), head(z_b, 0))
    rows = [down[0:1], down[1:2], up[0][0:1], up[0][1:2], up[1][0:1], up[2][0:1], jnp.zeros((2, NY), F32)]
    rows = jnp.concatenate(rows, axis=0)
    lines[...] = rows
    for i in range(5):
        x_a[i] = old_a[i]
    x_a[5] = rows


def lane_roll(value, by):
    return pltpu.roll(value, by % value.shape[-1], value.ndim - 1)


def row_roll(value, by):
    return pltpu.roll(value, by % value.shape[0], 0)


def resist(c):
    return jnp.exp(2.5 - c * F32(1.0 / 3.0))


def sink(c, w):
    return 0.5 * w * jnp.exp(c * F32(1.0 / 3.0) - 2.5)


def y_faces(r):
    ty = 2.0 / (r + lane_roll(r, -1))
    ty = jnp.where(lax.broadcasted_iota(jnp.int32, r.shape, 1) < NY - 1, ty, 0.0)
    return ty, lane_roll(ty, 1)


def y_part(ty, ty_lo):
    at = lax.broadcasted_iota(jnp.int32, ty.shape, 1) % EDGE
    return jnp.where(at == 0, ty_lo, jnp.where(at == EDGE - 1, ty, 0.0))


def basis(s, others, leave_y, leave_z, tx_lo, tx_hi):
    d = FINE_DAMPING / (s + others + tx_lo + tx_hi)
    ey, ez = d * leave_y, d * leave_z
    return 1.0 - d * s - ey - ez, ey, ez, d


def three(value):
    pieces = []
    for _ in range(3):
        piece = value.astype(jnp.bfloat16)
        pieces.append(piece)
        value = value - piece.astype(F32)
    return jnp.concatenate(pieces, axis=0)


def times_01(value, matrix):
    n = value.shape[0]
    out = jnp.dot(three(value), matrix, preferred_element_type=F32)
    return out[0:n] + (out[n : 2 * n] + out[2 * n : 3 * n])


def row_sums(arrays):
    row = lax.broadcasted_iota(jnp.int32, arrays[0].shape, 0)
    arrays = list(arrays) + [jnp.zeros(arrays[0].shape, F32)] * (8 - len(arrays))
    arrays = [arrays[i] for i in (0, 4, 2, 6, 1, 5, 3, 7)]
    for bit in (4, 2, 1):
        low = row // bit % 2 == 0
        merged = []
        for a, b in zip(arrays[::2], arrays[1::2]):
            keep, move = jnp.where(low, a, b), jnp.where(low, b, a)
            moved = row_roll(move, 4) if bit == 4 else jnp.where(low, row_roll(move, -bit), row_roll(move, bit))
            merged.append(keep + moved)
        arrays = merged
    return arrays[0]


def total_of(values):
    values = list(values)
    while len(values) > 1:
        values = [a + b for a, b in zip(values[::2], values[1::2])] + ([values[-1]] if len(values) % 2 else [])
    return values[0]


def minus(a, b):
    out = {}
    for key in {**a, **b}:
        if key in a and key in b:
            out[key] = a[key] - b[key]
        else:
            out[key] = a[key] if key in a else -b[key]
    return out


COLUMNS = (("N", "Z"), ("Q", "QZ"))


class Block:
    def __init__(self, z_b, z_a):
        self.tile, self.layer = lax.axis_index("tile"), lax.axis_index("layer")
        self.odd_z, self.odd_x = self.layer % 2 == 1, self.tile % 2 == 1
        self.has_up, self.has_down = (self.layer < LAYERS - 1).astype(F32), (self.layer > 0).astype(F32)
        self.has_right, self.has_left = (self.tile < TILES - 1).astype(F32), (self.tile > 0).astype(F32)
        self.plane = (NZL, NY)
        self.zrow = lax.broadcasted_iota(jnp.int32, self.plane, 0)
        self.m_r = lax.broadcasted_iota(jnp.int32, self.plane, 1) % EDGE == EDGE - 1
        self.at_zb = self.zrow == jnp.where(self.odd_z, NZL - 1, 0)
        self.up_mask = jnp.where(self.zrow == NZL - 1, self.has_up, 1.0)
        self.down_mask = jnp.where(self.zrow == 0, self.has_down, 1.0)
        self.sums = {}
        self.z_b, self.z_a = z_b, z_a

    def beyond(self, up):
        first, second = (self.z_b, self.z_a) if up else (self.z_a, self.z_b)
        planes = [jnp.where(self.odd_z, first[i], second[i]) for i in range(2)]
        return planes[0], planes[1][0:8], planes[1][8:16]

    def last_row(self, row, value):
        return jnp.where(self.zrow == NZL - 1, jnp.broadcast_to(row, self.plane), value)

    def known(self, r, below, over, upper=True):
        r_up = self.last_row(over, row_roll(r, -1))
        r_dn = jnp.where(self.zrow == 0, jnp.broadcast_to(below, self.plane), row_roll(r, 1))
        tz_hi, tz_lo = 0.5 / (r + r_up) * self.up_mask, 0.5 / (r + r_dn) * self.down_mask
        ty, ty_lo = y_faces(r)
        leave_z = jnp.where(self.at_zb, jnp.where(self.odd_z, tz_hi, tz_lo), 0.0)
        others = tz_hi + tz_lo + ty + ty_lo
        return tz_hi if upper else row_roll(tz_lo, -1), ty, others, y_part(ty, ty_lo), leave_z

    def crosses(self, upper):
        return self.odd_z if upper else ~self.odd_z

    def outer(self, r_edge, r, r_next, upper=True):
        t_edge, t_next = 0.5 / (r_edge + r) * (self.has_up if upper else self.has_down), 0.5 / (r + r_next)
        ty, ty_lo = y_faces(r)
        return t_edge + t_next + ty + ty_lo, y_part(ty, ty_lo), jnp.where(self.crosses(upper), t_edge, 0.0)

    def held(self, o, ey, ez, other=None, columns=COLUMNS, upper=True):
        (a, az), (b, bz) = columns
        crosses = self.crosses(upper)
        out = {
            (a, "u"): jnp.where(crosses, ez, o),
            (a, "v"): jnp.where(crosses, 0.0, ey),
            (az, "u"): jnp.where(crosses, o, 0.0),
            (az, "v"): jnp.where(crosses, ey, 0.0),
        }
        if other is not None:
            out[b, "u"] = jnp.where(crosses, 0.0, other)
            out[bz, "u"] = jnp.where(crosses, other, 0.0)
        return out

    def add(self, key, value):
        self.sums[key] = self.sums[key] + value if key in self.sums else value

    def add_pairs(self, weight, values):
        keys = sorted(values, key=order)
        for i, a in enumerate(keys):
            scaled = weight * values[a]
            for b in keys[i:]:
                self.add((a, b), scaled * values[b])

    def add_source(self, here, source):
        for key, value in here.items():
            self.add(("rhs", key), value * source)

    def add_plane(self, here, outer, s, tz, ty, counted=None, upper=True):
        if counted is not None:
            s, tz, ty = s * counted, tz * counted, ty * counted
        self.add_pairs(s, here)
        near, there = dict(here), {key: row_roll(value, -1) for key, value in here.items()}
        changed = there if upper else near
        for key, row in outer.items():
            changed[key] = self.last_row(row, changed.get(key, 0.0))
        self.add_pairs(tz, minus(near, there))
        rolled = {key: lane_roll(value, -1) for key, value in here.items()}
        there = {}
        for node in {key[0]: None for key in here}:
            u, v = rolled.get((node, "u"), 0.0), rolled.get((node, "v"), 0.0)
            there[node, "u"] = jnp.where(self.m_r, v, u)
            there[node, "v"] = jnp.where(self.m_r, u, v)
        self.add_pairs(ty, minus(here, there))


def inner_keys():
    held = [("N", "u"), ("N", "v"), ("Z", "u"), ("Z", "v")]
    keys = [(a, b) for i, a in enumerate(held) for b in held[i:]]
    return keys + [("rhs", key) for key in held[:3]]


def assemble_inner(cls, well, src, z_b, z_a, rows, own, beside_y, beside_z, aux, aux_rows, select, spread):
    block = Block(z_b, z_a)
    last, half = NXL - 1, NXL // 2
    r8, rm = None, None
    outers = []
    for upper in (True, False):
        adjacent, after, wells = block.beyond(upper)
        rows_here = slice(0, half) if upper else slice(half, NXL)
        r_all = resist(adjacent)
        r, s = r_all[rows_here], sink(adjacent[rows_here], wells)
        r_edge = resist(cls[rows_here, NZL - 1 if upper else 0, :].astype(F32))
        others, leave_y, leave_z = block.outer(r_edge, r, resist(after), upper)
        tx_lo = 2.0 / (r + row_roll(r_all, 1)[rows_here])
        if upper:
            tx_lo = jnp.where(lax.broadcasted_iota(jnp.int32, r.shape, 0) == 0, 0.0, tx_lo)
        o, ey, ez, _ = basis(s, others, leave_y, leave_z, tx_lo, 2.0 / (r + row_roll(r_all, -1)[rows_here]))
        held = block.held(o, ey, ez, upper=upper)
        outers += [{key: value[x : x + 1] for key, value in held.items()} for x in range(half)]
        if upper:
            r8 = r_all
        else:
            rm = r_all
            for i, value in enumerate((s, others + tx_lo, leave_y, leave_z, r)):
                aux_rows[i : i + 1, :] = value[half - 1 : half]
    aux_rows[5:6, :] = r8[last:NXL]
    aux_rows[6:8, :] = jnp.zeros((2, NY), F32)
    rs = [resist(cls[x].astype(F32)) for x in range(NXL)]
    txs = [jnp.zeros(block.plane, F32)] + [2.0 / (rs[x] + rs[x + 1]) for x in range(last)]
    first = 1.0 - block.has_left
    before = None
    for x in range(NXL):
        s = sink(cls[x].astype(F32), well[x].astype(F32))
        upper = x < half
        tz, ty, others, leave_y, leave_z = block.known(rs[x], rm[x : x + 1], r8[x : x + 1], upper)
        if x == 0:
            for i, value in enumerate((s, others + txs[1], leave_y, leave_z, rs[x])):
                aux[i] = value
        if x == last:
            for i, value in enumerate((s, others + txs[last], leave_y, leave_z, rs[x], tz, ty, txs[last])):
                aux[5 + i] = value
            break
        o, ey, ez, _ = basis(s, others, leave_y, leave_z, txs[x], txs[x + 1])
        own[x] = o
        beside_y[x] = ey
        beside_z[x] = ez
        here = {("N", "u"): o, ("N", "v"): ey, ("Z", "u"): ez}
        block.add_plane(here, outers[x], s, tz, ty, first if x == 0 else None, upper)
        if x:
            block.add_source(here, src[x])
            block.add_pairs(txs[x] * first if x == 1 else txs[x], minus(before, here))
        before = here
    keys = inner_keys()
    for i in range(0, len(keys), 8):
        rows[i : i + 8, :] = row_sums([block.sums[key] for key in keys[i : i + 8]])

    j = lax.broadcasted_iota(jnp.int32, (NY, 128), 0)
    n = lax.broadcasted_iota(jnp.int32, (NY, 128), 1)
    group, pos = n // NCY, j % EDGE
    taken = (group == 0) | ((group == 1) & (pos == 0)) | ((group == 2) & (pos >= EDGE - 2))
    select[...] = jnp.where((j // EDGE == n % NCY) & taken, 1.0, 0.0).astype(jnp.bfloat16)
    i = lax.broadcasted_iota(jnp.int32, (128, NY), 0)
    j = lax.broadcasted_iota(jnp.int32, (128, NY), 1)
    spread[...] = jnp.where(i % NCY == j // EDGE, 1.0, 0.0).astype(jnp.bfloat16)


def assemble(
    src, z_b, z_a, line_b, x_b, x_a, rows, own, beside_y, beside_z, aux, aux_rows, select, part, edge, lanes_ref, g_ref, out_ref
):
    block = Block(z_b, z_a)
    layer, odd_z, has_right, last_row = block.layer, block.odd_z, block.has_right, slice(NZL - 1, NZL)
    right = [jnp.where(block.odd_x, x_b[i], x_a[i]) for i in range(5)]
    right.append(jnp.where(block.odd_x, line_b[...], x_a[5]))
    left = jnp.where(block.odd_x, x_a[0], x_b[0])
    lines, lines_r = right[5], resist(right[5])

    tx = 2.0 / (aux_rows[4:5] + lines_r[0:1]) * has_right
    o, ey, ez, d = basis(*(aux_rows[i : i + 1] for i in range(4)), 0.0, tx)
    below_15 = block.held(o - d * tx, ey, ez, d * tx, upper=False)
    r8_15, r8_16, r8_17, r9_16 = aux_rows[5:6], lines_r[2:3], lines_r[3:4], lines_r[4:5]
    tx = 2.0 / (r8_15 + r8_16) * has_right
    rs = [aux[9]] + [resist(right[i]) for i in range(3)]
    o, ey, ez, d = basis(
        sink(lines[2:3], lines[5:6]), *block.outer(rs[1][last_row], r8_16, r9_16), tx, 2.0 / (r8_16 + r8_17)
    )
    above_16 = block.held(o - d * tx, ey, ez, d * tx, COLUMNS[::-1])

    t_left = 2.0 / (resist(left) + aux[4]) * block.has_left
    o, ey, ez, d = basis(*(aux[i] for i in range(4)), t_left, 0.0)
    o, ex = o - d * t_left, d * t_left
    for i, value in enumerate((o, ey, ez, ex)):
        edge[i] = value
    block.add_source({("N", "u"): o, ("N", "v"): ey, ("Z", "u"): ez, ("M", "u"): ex}, src[0])

    t_14 = aux[12]
    txs = [0.0, 2.0 / (rs[0] + rs[1]) * has_right, 2.0 / (rs[1] + rs[2]), 2.0 / (rs[2] + rs[3])]
    known = [(aux[10], aux[11], aux[6], aux[7], aux[8])]
    known += [block.known(rs[i], lines_r[i - 1 : i], (r8_16, r8_17)[i - 1]) for i in (1, 2)]
    ss = [aux[5]] + [sink(right[i], right[3 + i]) for i in range(2)]
    planes = []
    for i in range(3):
        o, ey, ez, d = basis(ss[i], *known[i][2:], txs[i], txs[i + 1])
        (a, az), (b, _) = COLUMNS if i == 0 else COLUMNS[::-1]
        here = {(a, "v"): ey, (az, "u"): ez}
        if i < 2:
            here[b, "u"] = d * txs[1]
            o = o - here[b, "u"]
        if i == 0:
            for k, value in enumerate((o, ey, ez, here[b, "u"])):
                edge[4 + k] = value
        here[a, "u"] = o
        planes.append(here)
    before = {("N", "u"): own[NXL - 2], ("N", "v"): beside_y[NXL - 2], ("Z", "u"): beside_z[NXL - 2]}
    block.add_pairs(t_14, minus(before, planes[0]))
    block.add_plane(planes[0], below_15, ss[0], *known[0][:2], upper=False)
    block.add_source(planes[0], src[NXL - 1])
    block.add_pairs(txs[1], minus(planes[0], planes[1]))
    block.add_plane(planes[1], above_16, ss[1], *known[1][:2], has_right)
    block.add_pairs(txs[2] * has_right, minus(planes[1], planes[2]))
    sums = block.sums

    keys = inner_keys() + [key for key in sums if key not in inner_keys()]
    index = {key: i for i, key in enumerate(keys)}
    count = -(-len(keys) // 16) * 16
    for i in range(0, count, 8):
        here = [sums[key] for key in keys[i : i + 8]]
        value = row_sums(here) if here else jnp.zeros((8, NY), F32)
        lanes_ref[i : i + 8, :] = value + rows[i : i + 8, :] if i < 16 else value
    grouped = times_01(lanes_ref[0:count, :], select[...])
    gl = lax.broadcasted_iota(jnp.int32, (count, 128), 1)
    g_l_next = jnp.where(gl < NCY - 1, lane_roll(grouped, -(NCY + 1)), 0.0)
    g_r_next = jnp.where((gl > 0) & (gl < NCY), lane_roll(grouped, -(2 * NCY - 1)), 0.0)
    forms = {
        "all": jnp.where(gl < NCY, grouped, 0.0),
        "L": jnp.where(gl < NCY, lane_roll(grouped, -NCY), 0.0),
        "R": jnp.where(gl < NCY, lane_roll(grouped, -2 * NCY), 0.0),
        "Ls": g_l_next,
        "Rs": g_r_next,
        "vv": g_l_next + g_r_next,
    }
    at = {}
    for i, (name, value) in enumerate(forms.items()):
        at[name] = i
        g_ref[i, 0:count, :] = value

    def taken_rows(terms):
        total = None
        for name, key in terms:
            if key in index:
                q = index[key]
                row = g_ref[at[name], q : q + 1, :]
                total = row if total is None else total + row
        return total

    def terms_of(a, b, dy):
        au, av, bu, bv = (a, "u"), (a, "v"), (b, "u"), (b, "v")
        if a == b:
            if dy == 0:
                return [("all", pair(au, au)), ("vv", pair(av, av))]
            return [("Ls", pair(au, av)), ("R", pair(au, av))]
        if dy == 0:
            return [("all", pair(au, bu)), ("vv", pair(av, bv))]
        if dy < 0:
            return [("L", pair(au, bv)), ("Rs", pair(av, bu))]
        return [("R", pair(au, bv)), ("Ls", pair(av, bu))]

    nothing = jnp.zeros((1, 128), F32)
    out_ref[...] = jnp.zeros(out_ref.shape, F32)
    spots = [(where, k) for where in ("own", "near", "low") for k in range(NCZ)]
    for (where, key), (r, k) in SLOT.items():
        names = {"own": HERE, "near": BESIDE}.get(where)
        if key[0] == "s":
            row = taken_rows(terms_of(names[key[1]], names[key[2]], key[3]))
        elif key[0] == "r":
            node = "M" if key[1] < 0 else names[key[1]]
            row = taken_rows([("all", ("rhs", (node, "u"))), ("vv", ("rhs", (node, "v")))])
        else:
            when_odd = taken_rows(terms_of(HERE[key[1]], BESIDE[key[2]], key[3]))
            when_even = taken_rows(terms_of(BESIDE[key[1]], HERE[key[2]], key[3]))
            when_odd = nothing if when_odd is None else when_odd
            when_even = nothing if when_even is None else when_even
            row = jnp.where(odd_z, when_odd, when_even)
        if row is not None:
            out_ref[spots.index((where, k)), r : r + 1, :] = row
    cell = layer // 2
    near_cell = jnp.where(odd_z, cell + 1, cell - 1)
    coarse_layer = {"own": cell, "near": near_cell, "low": jnp.minimum(cell, near_cell)}
    group = lax.broadcasted_iota(jnp.int32, (ROWS, 128), 1) // NCY
    total = jnp.zeros((ROWS, 128), F32)
    for i, (where, k) in enumerate(spots):
        if (where, k) not in {(w, kk) for (w, _), (_, kk) in SLOT.items()}:
            continue
        rows = out_ref[i]
        spread = rows
        for n in range(1, NCZ):
            spread = spread + lane_roll(rows, n * NCY)
        total = total + jnp.where(group == (coarse_layer[where] + k + NCZ) % NCZ, spread, 0.0)
    for k in range(HALF):
        part[k] = total


def flipped(k):
    return k // 4


TERMS = list(dict.fromkeys(key for _, key in SLOT))


def unpacked(rows):
    group = lax.broadcasted_iota(jnp.int32, (TILES // 2, 128), 1) // NCY
    loaded = {}

    def load(layer_from, row):
        if (layer_from, row) not in loaded:
            loaded[layer_from, row] = rows[pl.ds(layer_from * ROWS + row, TILES // 2, stride=LAYERS * ROWS), :]
        return loaded[layer_from, row]

    by_shift = {}
    for (where, key), (row, k) in SLOT.items():
        found = []
        for l in range(LAYERS):
            z = cells_of(l)[where]
            if 0 <= z and max(cells_of(l)["own"], cells_of(l)["near"] if where != "own" else 0) < NCZ:
                found.append(jnp.where(group == (z + k) % NCZ, load(l, row), 0.0))
        by_shift.setdefault((key, k), []).append(total_of(found))
    terms = {}
    for (key, k), values in by_shift.items():
        value = total_of(values)
        value = lane_roll(value, -k * NCY) if k else value
        terms[key] = terms[key] + value if key in terms else value
    return terms


def unpack(rows, out):
    for key, value in unpacked(rows).items():
        out[TERMS.index(key)] = value


def solve(mine, rows, own, beside_y, beside_z, edge, spread, pressure):
    tile, layer = lax.axis_index("tile"), lax.axis_index("layer")
    odd_z = layer % 2 == 1
    cell = layer // 2
    near_cell = jnp.where(odd_z, cell + 1, cell - 1)
    row = lax.broadcasted_iota(jnp.int32, (TILES, 128), 0)
    strip = row % 8 * 2 + row // 8
    lane_cell = lax.broadcasted_iota(jnp.int32, (1, 128), 1) // NCY
    pairs = lax.broadcasted_iota(jnp.int32, (TILES // 2, 128), 0)
    is_odd = (flipped(pairs) + flipped(tile // 2) + tile) % 2 == 1
    terms = {}
    for key, other in unpacked(rows).items():
        here = mine[TERMS.index(key)]
        terms[key] = jnp.concatenate([jnp.where(is_odd, other, here), jnp.where(is_odd, here, other)], axis=0)

    def strips_on(value, by):
        even, odd = value[0:8], value[8:16]
        if by > 0:
            return jnp.concatenate([odd, row_roll(even, -1)], axis=0)
        return jnp.concatenate([row_roll(odd, 1), even], axis=0)

    def from_last(value):
        return jnp.where(strip > 0, strips_on(value, -1), 0.0)

    half = {}
    for dy in (0, 1):
        half[0, 0, dy] = terms["s", 0, 0, dy] + from_last(terms["s", 1, 1, dy])
    for dy in (-1, 0, 1):
        half[1, 0, dy] = terms["s", 0, 1, dy]
        half[0, 1, dy] = terms["z", 0, 0, dy] + from_last(terms["z", 1, 1, dy])
        half[1, 1, dy] = terms["z", 0, 1, dy]
        half[-1, 1, dy] = from_last(terms["z", 1, 0, dy])
    back = jnp.where(strip < TILES - 1, strips_on(terms["r", -1], 1), 0.0)
    rhs = terms["r", 0] + from_last(terms["r", 1]) + back
    centre = half.pop((0, 0, 0))
    scale = COARSE_DAMPING / centre

    def shifted(value, dx, dz, dy):
        by = -(dz * NCY + dy)
        if by:
            value = lane_roll(value, by)
        return strips_on(value, dx) if dx else value

    full = dict(half)
    for (dx, dz, dy), value in half.items():
        full[-dx, -dz, -dy] = shifted(value, -dx, -dz, -dy)
    coarse = scale * rhs
    for _ in range(SWEEPS - 1):
        applied = [centre * coarse]
        for dz in (-1, 0, 1):
            for dy in (-1, 0, 1):
                moved = shifted(coarse, 0, dz, dy)
                for dx in (-1, 0, 1):
                    if (dx, dz, dy) in full:
                        applied.append(full[dx, dz, dy] * shifted(moved, dx, 0, 0))
        coarse = coarse + scale * (rhs - total_of(applied))

    def strip_row(at):
        return jnp.sum(jnp.where(strip == at, coarse, 0.0), axis=0, keepdims=True)

    here = strip_row(tile)
    own_row = jnp.where(lane_cell == cell, here, 0.0)
    picked = [
        own_row,
        jnp.where(lane_cell == cell, strip_row(tile - 1), 0.0),
        jnp.where(lane_cell == cell, strip_row(tile + 1), 0.0),
        jnp.where(lane_cell == near_cell, here, 0.0),
        lane_roll(own_row, 1),
        lane_roll(own_row, -1),
        jnp.zeros((2, 128), F32),
    ]
    picked = jnp.concatenate(picked, axis=0)
    fine = times_01(picked, spread[...])
    lane = lax.broadcasted_iota(jnp.int32, (1, NY), 1) % EDGE
    near_y = jnp.where(lane == 0, fine[4:5], jnp.where(lane == EDGE - 1, fine[5:6], 0.0))
    for x in range(NXL):
        if x in (0, NXL - 1):
            first, row = (0, fine[1:2]) if x == 0 else (4, fine[2:3])
            value = edge[first] * fine[0:1] + edge[first + 1] * near_y + edge[first + 2] * fine[3:4] + edge[first + 3] * row
        else:
            value = own[x] * fine[0:1] + beside_y[x] * near_y + beside_z[x] * fine[3:4]
        pressure[x] = value


def struct(*shape):
    return jax.ShapeDtypeStruct(shape, F32)


def call(kernel, outs, scratch=(), **kw):
    many = isinstance(outs, (list, tuple))
    return pl.pallas_call(
        kernel,
        out_shape=outs,
        out_specs=[VMEM] * len(outs) if many else VMEM,
        scratch_shapes=list(scratch),
        compiler_params=pltpu.CompilerParams(vmem_limit_bytes=48 * 1024 * 1024),
        **kw,
    )


def body(classes, well_mask, source):
    def swap(values, axis, near=False):
        out = []
        for i, v in enumerate(values):
            out.append(lax.ppermute(v, ("tile", "layer"), swap_pairs(axis, near or i == 1)))
        return out

    block = struct(NXL, NZL, NY)
    ints = jax.ShapeDtypeStruct((NXL, NZL, NY), jnp.int32)
    z_message, x_message = struct(2, NXL, NY), struct(5, NZL, NY)
    z_b, z_a, x_b, x_a, cls, well = call(
        pack,
        [z_message, z_message, x_message, x_message, ints, ints],
        [pltpu.SemaphoreType.DMA((2,))],
        in_specs=[pl.BlockSpec(memory_space=pltpu.HBM)] * 2,
    )(*(pltpu.with_memory_space_constraint(v, pltpu.HBM) for v in (classes, well_mask)))
    z_b, z_a = swap((z_b, z_a), "layer")
    (x_b,) = swap((x_b,), "tile")
    x_out = call(pack_lines, [struct(NZL, NY), struct(6, NZL, NY)], in_specs=[VMEM] * 3)(x_a, z_b, z_a)
    line_b, x_a = swap(x_out, "tile")
    select, spread = jax.ShapeDtypeStruct((NY, 128), jnp.bfloat16), jax.ShapeDtypeStruct((128, NY), jnp.bfloat16)
    inner, own, beside_y, beside_z, aux, aux_rows, select, spread = call(
        assemble_inner,
        [struct(16, NY), block, block, block, struct(13, NZL, NY), struct(8, NY), select, spread],
        in_specs=[VMEM] * 5,
        cost_estimate=pl.CostEstimate(flops=10**7, bytes_accessed=2 * 10**6, transcendentals=10**5),
    )(cls, well, source, z_b, z_a)
    part, edge = call(
        assemble,
        [struct(HALF, ROWS, 128), struct(8, NZL, NY)],
        [pltpu.VMEM((64, NY), F32), pltpu.VMEM((6, 64, 128), F32), pltpu.VMEM((3 * NCZ, ROWS, 128), F32)],
        in_specs=[VMEM] * 13,
    )(source, z_b, z_a, line_b, x_b, x_a, inner, own, beside_y, beside_z, aux, aux_rows, select)
    halves = [
        [(2 * k + (p + flipped(k)) % 2) * LAYERS + l for k in range(TILES // 2) for l in range(LAYERS)] for p in (0, 1)
    ]
    mine = lax.all_to_all(part, ("tile", "layer"), 0, 0, axis_index_groups=halves, tiled=True)
    (other,) = swap((mine,), "tile", True)
    mine = call(
        unpack,
        struct(len(TERMS), TILES // 2, 128),
        in_specs=[VMEM],
        cost_estimate=pl.CostEstimate(flops=10**6, bytes_accessed=10**6, transcendentals=0),
    )(mine.reshape(HALF * ROWS, 128))
    rows = other.reshape(HALF * ROWS, 128)
    return call(solve, block, in_specs=[VMEM] * 7)(mine, rows, own, beside_y, beside_z, edge, spread)


def solution(mesh):
    spec = P("tile", "layer", None)
    return jax.shard_map(body, mesh=mesh, in_specs=(spec, spec, spec), out_specs=spec, check_vma=False)
```
